256 devices in a mesh: dp: 64 (over y, z, core), tensor: 4 (over x).
Axes of the slice: x: 4, y: 4, z: 8, core: 2. Of those that a mesh axis runs over, the one named last changes fastest.
Arguments:
- queries: bfloat16 [32768, 4096], P('dp', 'tensor'), may hold values from -6 to 6
- passages: bfloat16 [16384, 4096], P('dp', 'tensor'), may hold values from -6 to 6
- neg_lists: int32 [512, 16], replicated, may hold values from -1 to 1023, as said below
- positives: int32 [32768], P('dp'), may hold values from 0 to 16383, as said below
Outputs:
- query_grad: bfloat16 [32768, 4096], P('dp', 'tensor')
- passage_grad: bfloat16 [16384, 4096], P('dp', 'tensor')
- query_loss: float32 [32768], P('dp')
The draws below stay inside these ranges and needn't reach their ends.
Inputs may be any that keep to these rules, and one draw needn't show every extreme that they name: `neg_lists`: each row names distinct blocks, its live entries first and then -1, with 8 or more live. The rows of query blocks d * 8 to (d + 1) * 8 - 1 name at most 64 distinct blocks, and at most 1 distinct blocks of one owner, blocks d * 16 to (d + 1) * 16 - 1 belonging to index d of dp. `positives`: the positive of a query is a passage of a live block in its query block's row.
All inputs are finite; a program needn't handle non-finite values.
Results may differ from the reference program's by a relative error of at most 0.0051.
Values may be sent and summed in bfloat16 or wider, within the bound.
No kernel may reach another device: no remote copies, remote signals or barrier semaphores. Data moves between devices by JAX's collectives and lax.ppermute only.
A program may use at most 128 MiB of HBM per device.

```python
import jax
import jax.numpy as jnp
from jax import lax

D = 4096
MINP = 64
NPRE = 7
QBLK = 64
NEG = 16
PBLK = 16
QBD = 8
PBD = 16
POOL = 64
CAP = 1
NQB = 512
NPB = 1024
NQ = 32768
NP = 16384


def draw_structure(key):
    base_key = jax.random.fold_in(key, 17)
    owner_count = POOL // CAP

    def one_index(dp_index):
        index_key = jax.random.fold_in(base_key, dp_index)
        key_owner, key_start, key_first, key_second, key_counts, key_shuffle, key_pick, key_offset = jax.random.split(index_key, 8)
        owners = jax.random.permutation(key_owner, jnp.arange(POOL, dtype=jnp.int32) % owner_count)
        start = jax.random.randint(key_start, (owner_count,), 0, PBD, dtype=jnp.int32)
        pool_order = jnp.arange(POOL, dtype=jnp.int32)
        occurrence = jnp.sum(((owners[None, :] == owners[:, None]) & (pool_order[None, :] < pool_order[:, None])).astype(jnp.int32), axis=1)
        pool_ids = owners * PBD + (start[owners] + occurrence) % PBD
        first_half = pool_ids[jax.random.permutation(key_first, POOL)]
        second_half = pool_ids[jax.random.permutation(key_second, POOL)]
        list_rows = jnp.concatenate([first_half, second_half]).reshape(QBD, NEG)
        counts = jnp.concatenate([jax.random.randint(key_counts, (QBD // 2,), NEG // 2, NEG + 1, dtype=jnp.int32), jnp.full((QBD // 2,), NEG, jnp.int32)])
        keep_mask = jnp.arange(NEG, dtype=jnp.int32)[None, :] < counts[:, None]
        list_rows = jnp.where(keep_mask, list_rows, -1)
        shuffle = jax.random.permutation(key_shuffle, QBD)
        list_rows = list_rows[shuffle]
        counts = counts[shuffle]
        picked = jax.random.randint(key_pick, (QBD, QBLK), 0, counts[:, None], dtype=jnp.int32)
        offset = jax.random.randint(key_offset, (QBD, QBLK), 0, PBLK, dtype=jnp.int32)
        chosen = jnp.take_along_axis(list_rows, picked, axis=1)
        positive = chosen * PBLK + offset
        return (list_rows, positive.reshape(QBD * QBLK))
    list_rows, positive = jax.vmap(one_index)(jnp.arange(owner_count, dtype=jnp.int32))
    return (list_rows.reshape(NQB, NEG), positive.reshape(NQ))


def draw_neg_lists(key, part):
    return draw_structure(key)[0]


def draw_positives(key, part):
    return draw_structure(key)[1]


def block_scale(own_key, extent, cuts, smallest, high):
    level, own = 1.0, jax.random.fold_in(own_key, 6)
    for position, shards_of in cuts:
        steps = jnp.exp(jax.random.uniform(jax.random.fold_in(own, position), (shards_of,), jnp.float32, smallest / len(cuts), high / len(cuts)))
        level = level * jnp.repeat(steps, extent[position] // shards_of).reshape([-1 if axis == position else 1 for axis in range(len(extent))])
    return level


def scatter_about(rng, dims, width, bound, pieces=(), kind=jnp.bfloat16):
    gain = block_scale(rng, dims, pieces, -0.22, 0.18) if pieces else 1.0
    array = jax.random.normal(rng, dims, jnp.float32) * width * gain
    return jnp.minimum(jnp.maximum(array, -bound), bound).astype(kind)


def setup_inputs(seed: int = 0) -> dict:
    seeds = jax.random.split(jax.random.key(seed), 5)
    queries = scatter_about(seeds[0], (NQ, D), 1.0, 6.0, ((0, 64), (1, 4)))
    passages = scatter_about(seeds[1], (NP, D), 1.0, 6.0, ((0, 64), (1, 4)))
    neg_lists = draw_neg_lists(jax.random.fold_in(seeds[4], 71), 0)
    positives = draw_positives(jax.random.fold_in(seeds[4], 71), 0)
    return {"queries": queries, "passages": passages, "neg_lists": neg_lists, "positives": positives}


EPS = 1e-06
INV_TEMP = 20.0

def prefix_terms(dot_sums, query_sq, passage_sq, cand_mask, labels, weight):
    query_scale = lax.rsqrt(query_sq + EPS)
    passage_scale = jnp.where(cand_mask, lax.rsqrt(passage_sq + EPS), 0.0)
    logits = dot_sums * query_scale[..., :, None] * passage_scale[..., None, :] * INV_TEMP
    exponent = jnp.where(cand_mask[..., None, :], jnp.exp(logits), 0.0)
    exp_total = lax.optimization_barrier(jnp.sum(exponent, axis=-1))
    probability = exponent / exp_total[..., None]
    cross_entropy = jnp.log(exp_total) - lax.optimization_barrier(jnp.sum(labels * logits, axis=-1))
    gradient = weight * (probability - labels)
    coefficient = gradient * query_scale[..., :, None] * passage_scale[..., None, :] * INV_TEMP
    inner_term = gradient * logits
    row_term = jnp.square(query_scale) * lax.optimization_barrier(jnp.sum(inner_term, axis=-1))
    col_term = jnp.square(passage_scale) * lax.optimization_barrier(jnp.sum(inner_term, axis=-2))
    return (coefficient, row_term, col_term, weight * cross_entropy)

def reference(queries, passages, neg_lists, positives):
    prefix_sizes = [MINP * 2 ** level_index for level_index in range(NPRE)]
    bounds = [0] + prefix_sizes
    weight_total = sum((prefix_size / MINP for prefix_size in prefix_sizes))
    query_blocks = queries.reshape(NQB, QBLK, D)
    passage_blocks = passages.reshape(NPB, PBLK, D)
    positive_rows = positives.reshape(NQB, QBLK)
    within_block = jnp.arange(PBLK, dtype=jnp.int32)
    cand_count = NEG * PBLK

    def one_block(accumulated, item_data):
        query_block, block_row, positive_row = item_data
        is_valid = block_row >= 0
        safe_row = jnp.where(is_valid, block_row, 0).astype(jnp.int32)
        candidates = jnp.where(is_valid[:, None, None], passage_blocks[safe_row], jnp.zeros((), jnp.bfloat16))
        candidates = candidates.reshape(cand_count, D)
        cand_mask = jnp.repeat(is_valid, PBLK)
        cand_ids = (safe_row[:, None] * PBLK + within_block[None, :]).reshape(cand_count)
        labels = ((cand_ids[None, :] == positive_row[:, None]) & cand_mask[None, :]).astype(jnp.float32)
        dot_sums = jnp.zeros((QBLK, cand_count), jnp.float32)
        query_sq = jnp.zeros((QBLK,), jnp.float32)
        passage_sq = jnp.zeros((cand_count,), jnp.float32)
        coef_list, row_list, col_list = ([], [], [])
        loss_sum = jnp.zeros((QBLK,), jnp.float32)
        for level_index in range(NPRE):
            low_col, high_col = (bounds[level_index], bounds[level_index + 1])
            query_seg = query_block[:, low_col:high_col]
            passage_seg = candidates[:, low_col:high_col]
            dot_sums = dot_sums + jnp.dot(query_seg, passage_seg.T, preferred_element_type=jnp.float32)
            query_sq = query_sq + lax.optimization_barrier(jnp.sum(jnp.square(query_seg.astype(jnp.float32)), axis=1))
            passage_sq = passage_sq + lax.optimization_barrier(jnp.sum(jnp.square(passage_seg.astype(jnp.float32)), axis=1))
            coefficient, row_term, col_term, weighted = prefix_terms(dot_sums, query_sq, passage_sq, cand_mask, labels, prefix_sizes[level_index] / MINP)
            coef_list.append(coefficient)
            row_list.append(row_term)
            col_list.append(col_term)
            loss_sum = loss_sum + weighted
        sum_coef = jnp.zeros((QBLK, cand_count), jnp.float32)
        sum_row = jnp.zeros((QBLK,), jnp.float32)
        sum_col = jnp.zeros((cand_count,), jnp.float32)
        query_parts, passage_parts = ([], [])
        for level_index in reversed(range(NPRE)):
            sum_coef = sum_coef + coef_list[level_index]
            sum_row = sum_row + row_list[level_index]
            sum_col = sum_col + col_list[level_index]
            low_col, high_col = (bounds[level_index], bounds[level_index + 1])
            query_seg = query_block[:, low_col:high_col]
            passage_seg = candidates[:, low_col:high_col]
            coef_half = sum_coef.astype(jnp.bfloat16)
            query_parts.append(jnp.dot(coef_half, passage_seg, preferred_element_type=jnp.float32) - sum_row[:, None] * query_seg.astype(jnp.float32))
            passage_parts.append(jnp.dot(coef_half.T, query_seg, preferred_element_type=jnp.float32) - sum_col[:, None] * passage_seg.astype(jnp.float32))
        query_grad = jnp.concatenate(query_parts[::-1], axis=1).astype(jnp.bfloat16)
        cand_grad = jnp.concatenate(passage_parts[::-1], axis=1).reshape(NEG, PBLK, D)
        cand_grad = jnp.where(is_valid[:, None, None], cand_grad, 0.0)
        accumulated = accumulated.at[safe_row].add(cand_grad)
        return (accumulated, (query_grad, loss_sum / weight_total))
    start_grad = jnp.zeros((NPB, PBLK, D), jnp.float32)
    passage_total, outputs = lax.scan(one_block, start_grad, (query_blocks, neg_lists, positive_rows))
    query_grad, query_loss = outputs
    return (query_grad.reshape(NQ, D), passage_total.reshape(NP, D).astype(jnp.bfloat16), query_loss.reshape(NQ))
```

```python
from functools import partial

import jax
import jax.numpy as jnp
from jax import lax
from jax.experimental import pallas as pl
from jax.experimental.pallas import tpu as pltpu
from jax.sharding import PartitionSpec as P

MINP = 64
NPRE = 7
PBLK = 16

EPS = 1e-06
INV_TEMP = 20.0

F32 = jnp.float32
BF16 = jnp.bfloat16

AUX = 8
COEF_AUX = 32


def vmem():
    return pl.BlockSpec(memory_space=pltpu.VMEM)


def smem():
    return pl.BlockSpec(memory_space=pltpu.SMEM)


def params():
    return pltpu.CompilerParams(vmem_limit_bytes=40 * 2**20)


def contract(a, b, da, db):
    return lax.dot_general(a, b, (((da,), (db,)), ((), ())), preferred_element_type=F32)


def eye(n):
    return lax.broadcasted_iota(jnp.int32, (n, n), 0) == lax.broadcasted_iota(jnp.int32, (n, n), 1)


def to_col(row):
    return jnp.sum(jnp.where(eye(row.shape[1]), row, 0.0), axis=1, keepdims=True)


def to_row(col):
    return jnp.sum(jnp.where(eye(col.shape[0]), col, 0.0), axis=0, keepdims=True)


def square_sums_as_row(half):
    wide = half.astype(F32)
    square = wide * wide
    high = square.astype(BF16)
    low = (square - high.astype(F32)).astype(BF16)
    ones = jnp.ones((8, half.shape[1]), BF16)
    return contract(ones, high, 1, 1) + contract(ones, low, 1, 1)


def square_sums_as_col(half):
    wide = half.astype(F32)
    return jnp.sum(wide * wide, axis=1, keepdims=True)


def terms(dots, qq_col, pp_row, ids_row, pos_col, weight):
    live = ids_row >= 0.0
    labels = jnp.where(ids_row == pos_col, 1.0, 0.0)
    a = lax.rsqrt(qq_col + EPS)
    b = jnp.where(live, lax.rsqrt(pp_row + EPS), 0.0)
    scale = (a * INV_TEMP) * b
    logits = dots * scale
    exponent = jnp.where(live, jnp.exp(logits), 0.0)
    total = jnp.sum(exponent, axis=1, keepdims=True)
    entropy = jnp.log(total) - jnp.sum(labels * logits, axis=1, keepdims=True)
    gradient = weight * (exponent * (1.0 / total) - labels)
    inner = gradient * logits
    row = (a * a) * jnp.sum(inner, axis=1, keepdims=True)
    col = (b * b) * jnp.sum(inner, axis=0, keepdims=True)
    return gradient * scale, row, col, weight * entropy


def take_blocks(pool_ref, slot_ref, block, count, out_ref):
    for n in range(count):
        slot = slot_ref[block * count + n]
        out_ref[n * PBLK : (n + 1) * PBLK, :] = pool_ref[pl.ds(slot * PBLK, PBLK), :]


def pack_kernel(wanted_ref, block_ref, out_ref):
    def step(d, carry):
        out_ref[d] = block_ref[jnp.maximum(wanted_ref[d], 0)]
        return carry

    lax.fori_loop(0, out_ref.shape[0], step, 0, unroll=8)


def dots_kernel(shards, per_shard, rows, slot_ref, shard_ref, query_ref, pool_ref, *refs):
    outs, cand_ref = refs[:-1], refs[-1]
    count = cand_ref.shape[0] // PBLK
    shard = shard_ref[0]
    for shift in range(shards):
        out_ref = outs[shift]
        target = lax.rem(shard + shift, shards)
        for k in range(per_shard):
            block = target * per_shard + k
            take_blocks(pool_ref, slot_ref, block, count, cand_ref)
            query = query_ref[pl.ds(block * rows, rows), :]
            cand = cand_ref[...]
            out_ref[k * rows : (k + 1) * rows, :] = contract(query, cand, 1, 1)
            base = per_shard * rows
            out_ref[base + k : base + k + 1, :] = square_sums_as_row(cand)[0:1, :]
            out_ref[base + per_shard : base + per_shard + 1, k * rows : (k + 1) * rows] = to_row(
                square_sums_as_col(query)
            )


def low_kernel(
    bounds, rows, slot_ref, shard_ref, query_ref, pool_ref, ids_ref, pos_ref,
    coef_ref, row_ref, col_ref, loss_ref, cand_ref, term_ref,
):
    count = cand_ref.shape[0] // PBLK
    levels = len(bounds)

    @pl.when(shard_ref[0] == 0)
    def _():
        row_ref[...] = jnp.zeros_like(row_ref)
        col_ref[...] = jnp.zeros_like(col_ref)

        def step(block, carry):
            take_blocks(pool_ref, slot_ref, block, count, cand_ref)
            ids = ids_ref[pl.ds(block, 1), :]
            pos = to_col(pos_ref[pl.ds(block, 1), :])
            dots = jnp.zeros((rows, cand_ref.shape[0]), F32)
            qq = jnp.zeros((rows, 1), F32)
            pp = jnp.zeros((8, cand_ref.shape[0]), F32)
            loss = jnp.zeros((rows, 1), F32)
            row_terms, col_terms = [], []
            for level, (low, high) in enumerate(bounds):
                query = query_ref[pl.ds(block * rows, rows), low:high]
                cand = cand_ref[:, low:high]
                dots = dots + contract(query, cand, 1, 1)
                qq = qq + square_sums_as_col(query)
                pp = pp + square_sums_as_row(cand)
                coef, row, col, part = terms(dots, qq, pp[0:1, :], ids, pos, float(high // MINP))
                term_ref[level] = coef
                row_terms.append(to_row(row))
                col_terms.append(col)
                loss = loss + part
            coef = jnp.zeros((rows, cand_ref.shape[0]), F32)
            row = jnp.zeros((1, rows), F32)
            col = jnp.zeros((1, cand_ref.shape[0]), F32)
            for level in reversed(range(levels)):
                coef = coef + term_ref[level]
                row = row + row_terms[level]
                col = col + col_terms[level]
                coef_ref[level, pl.ds(block * rows, rows), :] = coef
                row_ref[block, level : level + 1, :] = row
                col_ref[block, level : level + 1, :] = col
            loss_ref[pl.ds(block, 1), :] = to_row(loss)
            return carry

        lax.fori_loop(0, loss_ref.shape[0], step, 0)

    @pl.when(shard_ref[0] != 0)
    def _():
        loss_ref[...] = jnp.zeros_like(loss_ref)


def high_kernel(shards, per_shard, rows, weights, shard_ref, ids_ref, pos_ref, low_loss_ref, *refs):
    ins, outs = refs[:shards], refs[shards:]
    shard = shard_ref[0]
    base = per_shard * rows
    half_rows, half_cols, full_rows, full_cols = [], [], [], []
    losses = []
    width = ins[0].shape[1]
    coefs = []
    in_half = [
        jnp.where(lax.rem(shard - shift + shards, shards) < shards // 2, 1.0, 0.0)
        for shift in range(shards)
    ]
    aux_full = sum(ref[base : base + AUX, :] for ref in ins)
    aux_half = sum(ref[base : base + AUX, :] * keep for ref, keep in zip(ins, in_half))
    for k in range(per_shard):
        block = shard * per_shard + k
        ids = ids_ref[pl.ds(block, 1), :]
        pos = to_col(pos_ref[pl.ds(block, 1), :])
        span = slice(k * rows, (k + 1) * rows)
        dots_full = sum(ref[span, :] for ref in ins)
        dots_half = sum(ref[span, :] * keep for ref, keep in zip(ins, in_half))
        results = []
        for dots, aux, weight in (
            (dots_half, aux_half, weights[0]),
            (dots_full, aux_full, weights[1]),
        ):
            qq = to_col(aux[per_shard : per_shard + 1, span])
            results.append(terms(dots, qq, aux[k : k + 1, :], ids, pos, weight))
        (coef_h, row_h, col_h, loss_h), (coef_f, row_f, col_f, loss_f) = results
        coefs.append((coef_h + coef_f, coef_f))
        half_rows.append(to_row(row_h + row_f))
        full_rows.append(to_row(row_f))
        half_cols.append(col_h + col_f)
        full_cols.append(col_f)
        losses.append(to_row(loss_h + loss_f))
    per_row = width // rows
    low = [
        jnp.concatenate([low_loss_ref[r * per_row + j : r * per_row + j + 1, :] for j in range(per_row)], axis=1)
        for r in range(low_loss_ref.shape[0] // per_row)
    ]

    def aux_rows(rows_list, cols_list):
        line = jnp.concatenate(rows_list + losses, axis=1)
        table = jnp.concatenate(cols_list + [line] + low, axis=0)
        table = jnp.concatenate([table, jnp.zeros((AUX - table.shape[0], width), F32)], axis=0)
        first = table.astype(BF16).astype(F32)
        second = (table - first).astype(BF16).astype(F32)
        third = table - first - second
        return jnp.concatenate([first, second, third, jnp.zeros_like(table)], axis=0).astype(BF16)

    aux = (aux_rows(half_rows, half_cols), aux_rows(full_rows, full_cols))
    for shift in range(shards):
        out_ref = outs[shift]
        high_target = lax.rem(shard + shift, shards) >= shards // 2

        @pl.when(high_target)
        def _():
            for k in range(per_shard):
                out_ref[k * rows : (k + 1) * rows, :] = coefs[k][1].astype(BF16)
            out_ref[base : base + COEF_AUX, :] = aux[1]

        @pl.when(jnp.logical_not(high_target))
        def _():
            for k in range(per_shard):
                out_ref[k * rows : (k + 1) * rows, :] = coefs[k][0].astype(BF16)
            out_ref[base : base + COEF_AUX, :] = aux[0]


def grads_kernel(
    bounds, shards, per_shard, rows, loss_scale, slot_ref, shard_ref, query_ref, pool_ref, low_row_ref,
    low_col_ref, low_coef_hbm, *refs,
):
    ins = refs[:shards]
    query_grad_ref, slot_grad_ref, loss_ref = refs[shards : shards + 3]
    cand_ref, coef_ref, row_ref, col_ref, sum_ref, scale_ref, low_coef_ref, sem = refs[shards + 3 :]
    shard = shard_ref[0]
    base = per_shard * rows
    blocks = shards * per_shard
    count = cand_ref.shape[0] // PBLK
    width = query_ref.shape[1]
    cands = cand_ref.shape[0]
    copy = pltpu.make_async_copy(low_coef_hbm, low_coef_ref, sem)

    @pl.when(shard == 0)
    def _():
        copy.start()

    sum_ref[...] = jnp.zeros_like(sum_ref)
    scale_ref[...] = jnp.zeros_like(scale_ref)
    loss_low = jnp.zeros((AUX, cands), F32)
    for shift in range(shards):
        source = lax.rem(shard - shift + shards, shards)
        coef_ref[pl.ds(source * base, base), :] = ins[shift][:base, :]
        packed = ins[shift][base : base + COEF_AUX, :].astype(F32)
        aux = packed[:AUX] + packed[AUX : 2 * AUX] + packed[2 * AUX : 3 * AUX]
        for k in range(per_shard):
            col_ref[source * per_shard + k] = aux[k : k + 1, :]
            row_ref[source * per_shard + k] = aux[per_shard : per_shard + 1, k * rows : (k + 1) * rows]
        loss_ref[pl.ds(source, 1), :] = aux[per_shard : per_shard + 1, base:]
        loss_low = loss_low + jnp.where(source == 0, aux, 0.0)
    per_row = cands // base
    for r in range(shards):
        low = loss_low[per_shard + 1 + r // per_row : per_shard + 2 + r // per_row, :]
        low = low[:, (r % per_row) * base : (r % per_row + 1) * base]
        loss_ref[r : r + 1, :] = (loss_ref[r : r + 1, :] + low) * loss_scale

    def run(spans, low):
        levels = len(spans)

        def step(block, carry):
            take_blocks(pool_ref, slot_ref, block, count, cand_ref)
            rows_here = jnp.broadcast_to(row_ref[block], (8, rows))
            cols_here = jnp.broadcast_to(col_ref[block], (8, cands))
            if low:
                rows_here = rows_here + low_row_ref[block]
                cols_here = cols_here + low_col_ref[block]
            row_cols = jnp.concatenate(
                [jnp.concatenate([rows_here, jnp.zeros((8, 128 - rows), F32)], axis=1), jnp.zeros((120, 128), F32)],
                axis=0,
            ).T
            col_cols = jnp.concatenate([cols_here, jnp.zeros((120, cands), F32)], axis=0).T
            here = pl.ds(block * rows, rows)
            for n in range(count):
                slot = slot_ref[block * count + n]
                target = pl.ds(slot * PBLK, PBLK)
                scale_ref[target, :] = scale_ref[target, :] + col_cols[n * PBLK : (n + 1) * PBLK, :]
            for level, (lo, hi) in enumerate(spans):
                coef = coef_ref[here, :]
                if low:
                    coef = (coef.astype(F32) + low_coef_ref[level, here, :]).astype(BF16)
                query = query_ref[here, lo:hi]
                cand = cand_ref[:, lo:hi]
                grad = contract(coef, cand, 1, 0) - row_cols[:rows, level : level + 1] * query.astype(F32)
                query_grad_ref[here, lo:hi] = grad.astype(BF16)
                cand_grad = contract(coef, query, 0, 0)
                for n in range(count):
                    slot = slot_ref[block * count + n]
                    target = pl.ds(slot * PBLK, PBLK)
                    sum_ref[target, lo:hi] = sum_ref[target, lo:hi] + cand_grad[n * PBLK : (n + 1) * PBLK, :]
            return carry

        lax.fori_loop(0, blocks, step, 0)

        def finish(i, carry):
            here = pl.ds(i * 64, 64)
            for level, (lo, hi) in enumerate(spans):
                part = sum_ref[here, lo:hi] - scale_ref[here, level : level + 1] * pool_ref[here, lo:hi].astype(F32)
                slot_grad_ref[here, lo:hi] = part.astype(BF16)
            return carry

        lax.fori_loop(0, slot_grad_ref.shape[0] // 64, finish, 0)

    @pl.when(shard == 0)
    def _():
        copy.wait()
        run(bounds, True)

    @pl.when(shard != 0)
    def _():
        run([(0, width)], False)


def gather_kernel(wanted_ref, back_ref, out_ref, sum_ref):
    sum_ref[...] = jnp.zeros_like(sum_ref)

    def step(d, carry):
        target = jnp.maximum(wanted_ref[d], 0)
        keep = jnp.where(wanted_ref[d] >= 0, 1.0, 0.0)
        sum_ref[target] = sum_ref[target] + back_ref[d].astype(F32) * keep
        return carry

    lax.fori_loop(0, back_ref.shape[0], step, 0, unroll=4)
    out_ref[...] = sum_ref[...].astype(BF16)


def per_device(queries, passages, neg_lists, positives):
    peers = lax.axis_size("dp")
    shards = lax.axis_size("tensor")
    total_rows, width = queries.shape
    blocks = neg_lists.shape[0] // peers
    count = neg_lists.shape[1]
    rows = total_rows // blocks
    local_blocks = passages.shape[0] // PBLK
    cands = count * PBLK
    per_shard = blocks // shards
    base = per_shard * rows
    slots = peers
    my_index = lax.axis_index("dp")
    shard = lax.axis_index("tensor")
    sizes = [MINP * 2**level for level in range(NPRE)]
    low_sizes = [size for size in sizes if size <= width]
    high_sizes = [size for size in sizes if size > width]
    assert high_sizes == [width * shards // 2, width * shards] and low_sizes[-1] == width
    bounds = list(zip([0] + low_sizes[:-1], low_sizes))
    levels = len(bounds)
    weight_total = sum(size / MINP for size in sizes)

    flat = neg_lists.reshape(peers, blocks * count)
    mine = (flat >= 0) & (flat // local_blocks == my_index)
    wanted = jnp.max(jnp.where(mine, flat % local_blocks, -1), axis=1)
    own = lax.dynamic_slice_in_dim(neg_lists, my_index * blocks, blocks, 0)
    valid = own >= 0
    slot = jnp.where(valid, own // local_blocks, 0).reshape(blocks * count)
    ids = jnp.where(
        valid[:, :, None], own[:, :, None] * PBLK + jnp.arange(PBLK, dtype=jnp.int32)[None, None, :], -1
    )
    ids = ids.reshape(blocks, cands).astype(F32)
    pos = positives.reshape(blocks, rows).astype(F32)
    shard_arr = shard.reshape(1).astype(jnp.int32)

    panels = pl.pallas_call(
        pack_kernel,
        out_shape=jax.ShapeDtypeStruct((peers, PBLK, width), BF16),
        in_specs=[smem(), vmem()],
        out_specs=vmem(),
        compiler_params=params(),
        name="pack",
    )(wanted, passages.reshape(local_blocks, PBLK, width))
    pool = lax.all_to_all(panels, "dp", split_axis=0, concat_axis=0, tiled=True)
    pool = pool.reshape(slots * PBLK, width)

    message = jax.ShapeDtypeStruct((base + AUX, cands), F32)
    dots = pl.pallas_call(
        partial(dots_kernel, shards, per_shard, rows),
        out_shape=[message] * shards,
        in_specs=[smem(), smem(), vmem(), vmem()],
        out_specs=[vmem()] * shards,
        scratch_shapes=[pltpu.VMEM((cands, width), BF16)],
        compiler_params=params(),
        name="dots",
    )(slot, shard_arr, queries, pool)

    def exchange(parts):
        return [parts[0]] + [
            lax.ppermute(parts[s], "tensor", [(i, (i + s) % shards) for i in range(shards)])
            for s in range(1, shards)
        ]

    arrived = exchange(dots)
    low_coef, low_row, low_col, low_loss = pl.pallas_call(
        partial(low_kernel, bounds, rows),
        out_shape=[
            jax.ShapeDtypeStruct((levels, total_rows, cands), F32),
            jax.ShapeDtypeStruct((blocks, 8, rows), F32),
            jax.ShapeDtypeStruct((blocks, 8, cands), F32),
            jax.ShapeDtypeStruct((blocks, rows), F32),
        ],
        in_specs=[smem(), smem(), vmem(), vmem(), vmem(), vmem()],
        out_specs=[vmem()] * 4,
        scratch_shapes=[pltpu.VMEM((cands, width), BF16), pltpu.VMEM((levels, rows, cands), F32)],
        compiler_params=params(),
        name="low",
    )(slot, shard_arr, queries, pool, ids, pos)

    coef_message = jax.ShapeDtypeStruct((base + COEF_AUX, cands), BF16)
    coefs = pl.pallas_call(
        partial(high_kernel, shards, per_shard, rows, [size / MINP for size in high_sizes]),
        out_shape=[coef_message] * shards,
        in_specs=[smem()] + [vmem()] * (3 + shards),
        out_specs=[vmem()] * shards,
        compiler_params=params(),
        name="high",
    )(shard_arr, ids, pos, low_loss, *arrived)
    coefs = exchange(coefs)

    query_grad, slot_grad, loss = pl.pallas_call(
        partial(grads_kernel, bounds, shards, per_shard, rows, 1.0 / weight_total),
        out_shape=[
            jax.ShapeDtypeStruct((total_rows, width), BF16),
            jax.ShapeDtypeStruct((slots * PBLK, width), BF16),
            jax.ShapeDtypeStruct((shards, base), F32),
        ],
        in_specs=[smem(), smem()] + [vmem()] * 4 + [pl.BlockSpec(memory_space=pl.ANY)] + [vmem()] * shards,
        out_specs=[vmem()] * 3,
        scratch_shapes=[
            pltpu.VMEM((cands, width), BF16),
            pltpu.VMEM((total_rows, cands), BF16),
            pltpu.VMEM((blocks, 1, rows), F32),
            pltpu.VMEM((blocks, 1, cands), F32),
            pltpu.VMEM((slots * PBLK, width), F32),
            pltpu.VMEM((slots * PBLK, 128), F32),
            pltpu.VMEM((levels, total_rows, cands), F32),
            pltpu.SemaphoreType.DMA(()),
        ],
        compiler_params=params(),
        name="grads",
    )(slot, shard_arr, queries, pool, low_row, low_col, low_coef, *coefs)

    back = lax.all_to_all(
        slot_grad.reshape(slots, PBLK, width), "dp", split_axis=0, concat_axis=0, tiled=True
    )
    passage_grad = pl.pallas_call(
        gather_kernel,
        out_shape=jax.ShapeDtypeStruct((local_blocks, PBLK, width), BF16),
        in_specs=[smem(), vmem()],
        out_specs=vmem(),
        scratch_shapes=[pltpu.VMEM((local_blocks, PBLK, width), F32)],
        compiler_params=params(),
        name="collect",
    )(wanted, back)
    return (
        query_grad,
        passage_grad.reshape(local_blocks * PBLK, width),
        loss.reshape(total_rows),
    )


def solution(mesh):
    return jax.shard_map(
        per_device,
        mesh=mesh,
        in_specs=(P("dp", "tensor"), P("dp", "tensor"), P(), P("dp")),
        out_specs=(P("dp", "tensor"), P("dp", "tensor"), P("dp")),
        check_vma=False,
    )
```

```python
from functools import partial

import jax
import jax.numpy as jnp
from jax import lax
from jax.experimental import pallas as pl
from jax.experimental.pallas import tpu as pltpu
from jax.sharding import PartitionSpec as P

MINP = 64
NPRE = 7
PBLK = 16

EPS = 1e-06
INV_TEMP = 20.0

F32 = jnp.float32
BF16 = jnp.bfloat16

AUX = 8
COEF_AUX = 32
LANES = 128
PIECE = 256
FULL = 4


def vmem():
    return pl.BlockSpec(memory_space=pltpu.VMEM)


def smem():
    return pl.BlockSpec(memory_space=pltpu.SMEM)


def hbm():
    return pl.BlockSpec(memory_space=pltpu.HBM)


def params():
    return pltpu.CompilerParams(vmem_limit_bytes=20 * 2**20)


def contract(a, b, da, db):
    return lax.dot_general(a, b, (((da,), (db,)), ((), ())), preferred_element_type=F32)


def eye(n):
    return lax.broadcasted_iota(jnp.int32, (n, n), 0) == lax.broadcasted_iota(jnp.int32, (n, n), 1)


def to_col(row):
    return jnp.sum(jnp.where(eye(row.shape[1]), row, 0.0), axis=1, keepdims=True)


def to_row(col):
    return jnp.sum(jnp.where(eye(col.shape[0]), col, 0.0), axis=0, keepdims=True)


def square_sums(half):
    wide = half.astype(F32)
    return jnp.sum(wide * wide, axis=1, keepdims=True)


def columns(table):
    table = jnp.concatenate([table, jnp.zeros((8, LANES - table.shape[1]), F32)], axis=1) if table.shape[1] < LANES else table
    return jnp.concatenate([table, jnp.zeros((LANES - 8, table.shape[1]), F32)], axis=0).T


def terms(dots, qq_col, pp_row, live, labels, weight):
    a = lax.rsqrt(qq_col + EPS)
    b = jnp.where(live, lax.rsqrt(pp_row + EPS), 0.0)
    scale = (a * INV_TEMP) * b
    logits = dots * scale
    exponent = jnp.where(live, jnp.exp(logits), 0.0)
    total = jnp.sum(exponent, axis=1, keepdims=True)
    gradient = weight * (exponent * (1.0 / total) - labels)
    inner = gradient * logits
    row = (a * a) * jnp.sum(inner, axis=1, keepdims=True)
    col = (b * b) * jnp.sum(inner, axis=0, keepdims=True)
    return gradient * scale, row, col, weight * jnp.log(total), weight * logits


def take_blocks(pool_ref, slot_ref, block, count, out_ref):
    for n in range(count):
        out_ref[n] = pool_ref[slot_ref[block * count + n]]


def pool_norms(pool_ref, norm_ref, bounds):
    step_slots = 8
    lane = lax.broadcasted_iota(jnp.int32, (step_slots * PBLK, LANES), 1)

    def step(i, carry):
        here = pl.ds(i * step_slots, step_slots)
        block = pool_ref[here]
        wide = block.reshape(step_slots * PBLK, block.shape[2]).astype(F32)
        square = wide * wide
        total = jnp.zeros((step_slots * PBLK, 1), F32)
        result = jnp.zeros((step_slots * PBLK, LANES), F32)
        for level, (low, high) in enumerate(bounds):
            total = total + jnp.sum(square[:, low:high], axis=1, keepdims=True)
            result = jnp.where(lane == level, total, result)
        norm_ref[here] = result.reshape(step_slots, PBLK, LANES)
        return carry

    lax.fori_loop(0, pool_ref.shape[0] // step_slots, step, 0)


def norm_rows(norm_ref, slot_ref, block, count):
    table = jnp.concatenate([norm_ref[slot_ref[block * count + n]] for n in range(count)], axis=0)
    return table.T[:8, :]


def pack_kernel(wanted_ref, block_ref, out_ref, sem):
    def step(d, carry):
        source = block_ref.at[jnp.maximum(wanted_ref[d], 0)]
        pltpu.make_async_copy(source, out_ref.at[d], sem).start()
        return carry

    lax.fori_loop(0, out_ref.shape[0], step, 0, unroll=8)
    pltpu.make_async_copy(out_ref, out_ref, sem).wait()


def dots_kernel(shards, per_shard, rows, shifts, slot_ref, shard_ref, query_ref, pool_ref, norm_ref, *refs):
    outs, cand_ref = refs[:-1], refs[-1]
    count, _, width = cand_ref.shape
    shard = shard_ref[0]
    base = per_shard * rows
    for shift, out_ref in zip(shifts, outs):
        target = lax.rem(shard + shift, shards)
        for k in range(per_shard):
            block = target * per_shard + k
            take_blocks(pool_ref, slot_ref, block, count, cand_ref)
            query = query_ref[pl.ds(block * rows, rows), :]
            cand = cand_ref[...].reshape(count * PBLK, width)
            out_ref[k * rows : (k + 1) * rows, :] = contract(query, cand, 1, 1)
            norms = norm_rows(norm_ref, slot_ref, block, count)
            out_ref[base + k : base + k + 1, :] = norms[FULL : FULL + 1, :]
            out_ref[base + per_shard : base + per_shard + 1, k * rows : (k + 1) * rows] = to_row(square_sums(query))


def first_dots_kernel(bounds, shards, per_shard, rows, shifts, slot_ref, shard_ref, query_ref, pool_ref, norm_ref, *refs):
    pool_norms(pool_ref, norm_ref, bounds)
    dots_kernel(shards, per_shard, rows, shifts, slot_ref, shard_ref, query_ref, pool_ref, norm_ref, *refs)


def prefix_dots(bounds, rows, block, query_ref, cand_ref, count):
    dots = None
    for low, high in bounds:
        query = query_ref[pl.ds(block * rows, rows), low:high]
        cand = cand_ref[:, :, low:high]
        part = contract(query, cand.reshape(count * PBLK, high - low), 1, 1)
        dots = part if dots is None else dots + part
        yield dots


def low_kernel(
    bounds, rows, slot_ref, shard_ref, query_ref, pool_ref, norm_ref, ids_ref, pos_ref,
    coef_hbm, row_ref, col_ref, loss_ref, cand_ref, term_ref, coef_ref, sem,
):
    count = cand_ref.shape[0]
    levels = len(bounds)
    cands = coef_hbm.shape[2]

    @pl.when(shard_ref[0] == 0)
    def _():
        row_ref[...] = jnp.zeros_like(row_ref)
        col_ref[...] = jnp.zeros_like(col_ref)

        def step(block, carry):
            take_blocks(pool_ref, slot_ref, block, count, cand_ref)
            pp = norm_rows(norm_ref, slot_ref, block, count)
            ids = ids_ref[pl.ds(block, 1), :]
            live = ids >= 0.0
            labels = jnp.where(ids == to_col(pos_ref[pl.ds(block, 1), :]), 1.0, 0.0)
            here = pl.ds(block * rows, rows)
            qq = jnp.zeros((rows, 1), F32)
            entropy = jnp.zeros((rows, 1), F32)
            logit_sum = jnp.zeros((rows, cands), F32)
            row_terms, col_terms = [], []
            sums = prefix_dots(bounds, rows, block, query_ref, cand_ref, count)
            for level, ((low, high), dots) in enumerate(zip(bounds, sums)):
                qq = qq + square_sums(query_ref[here, low:high])
                coef, row, col, part, logits = terms(
                    dots, qq, pp[level : level + 1, :], live, labels, float(high // MINP)
                )
                term_ref[level] = coef
                row_terms.append(row)
                col_terms.append(col)
                entropy = entropy + part
                logit_sum = logit_sum + logits
            loss = entropy - jnp.sum(labels * logit_sum, axis=1, keepdims=True)
            coef = jnp.zeros((rows, cands), F32)
            row = jnp.zeros((rows, 1), F32)
            col = jnp.zeros((1, cands), F32)
            for level in reversed(range(levels)):
                coef = coef + term_ref[level]
                row = row + row_terms[level]
                col = col + col_terms[level]
                coef_ref[level, here, :] = coef
                row_ref[block, level : level + 1, :] = to_row(row)
                col_ref[block, level : level + 1, :] = col
            loss_ref[pl.ds(block, 1), :] = to_row(loss)
            pltpu.make_async_copy(coef_ref.at[:, here], coef_hbm.at[:, here], sem).start()
            return carry

        lax.fori_loop(0, loss_ref.shape[0], step, 0)
        pltpu.make_async_copy(coef_ref, coef_hbm, sem).wait()

    @pl.when(shard_ref[0] != 0)
    def _():
        loss_ref[...] = jnp.zeros_like(loss_ref)


def high_kernel(shards, per_shard, rows, weights, shard_ref, ids_ref, pos_ref, low_loss_ref, *refs):
    ins, outs = refs[:shards], refs[shards:]
    shard = shard_ref[0]
    base = per_shard * rows
    width = ids_ref.shape[1]
    in_half = [
        jnp.where(lax.rem(shard - shift + shards, shards) < shards // 2, 1.0, 0.0)
        for shift in range(shards)
    ]

    def total(span, keep):
        pieces = [ref[span, :] * scale if keep else ref[span, :] for ref, scale in zip(ins, in_half)]
        return (pieces[0] + pieces[1]) + (pieces[2] + pieces[3])

    below = slice(base, base + AUX)
    half_rows, half_cols, full_rows, full_cols, losses, coefs = [], [], [], [], [], []
    aux_half, aux_full = total(below, True), total(below, False)
    for k in range(per_shard):
        block = shard * per_shard + k
        ids = ids_ref[pl.ds(block, 1), :]
        live = ids >= 0.0
        labels = jnp.where(ids == to_col(pos_ref[pl.ds(block, 1), :]), 1.0, 0.0)
        span = slice(k * rows, (k + 1) * rows)
        results = []
        for keep, aux, weight in ((True, aux_half, weights[0]), (False, aux_full, weights[1])):
            qq = to_col(aux[per_shard : per_shard + 1, span])
            results.append(terms(total(span, keep), qq, aux[k : k + 1, :], live, labels, weight))
        (coef_h, row_h, col_h, part_h, logit_h), (coef_f, row_f, col_f, part_f, logit_f) = results
        loss = part_h + part_f - jnp.sum(labels * (logit_h + logit_f), axis=1, keepdims=True)
        coefs.append(((coef_h + coef_f).astype(BF16), coef_f.astype(BF16)))
        half_rows.append(to_row(row_h + row_f))
        full_rows.append(to_row(row_f))
        half_cols.append(col_h + col_f)
        full_cols.append(col_f)
        losses.append(to_row(loss))
    per_row = width // rows
    low = [
        jnp.concatenate([low_loss_ref[r * per_row + j : r * per_row + j + 1, :] for j in range(per_row)], axis=1)
        for r in range(low_loss_ref.shape[0] // per_row)
    ]

    def aux_rows(rows_list, cols_list):
        line = jnp.concatenate(rows_list + losses, axis=1)
        table = jnp.concatenate(cols_list + [line] + low, axis=0)
        table = jnp.concatenate([table, jnp.zeros((AUX - table.shape[0], width), F32)], axis=0)
        first = table.astype(BF16).astype(F32)
        second = (table - first).astype(BF16).astype(F32)
        third = table - first - second
        return jnp.concatenate([first, second, third, jnp.zeros_like(table)], axis=0).astype(BF16)

    aux = (aux_rows(half_rows, half_cols), aux_rows(full_rows, full_cols))
    for shift in range(shards):
        out_ref = outs[shift]
        high_target = lax.rem(shard + shift, shards) >= shards // 2
        for which, chosen in ((1, high_target), (0, jnp.logical_not(high_target))):

            @pl.when(chosen)
            def _():
                for k in range(per_shard):
                    out_ref[k * rows : (k + 1) * rows, :] = coefs[k][which]
                out_ref[base : base + COEF_AUX, :] = aux[which]


def unpack_aux(ref, base):
    packed = ref[base : base + COEF_AUX, :].astype(F32)
    return packed[:AUX] + packed[AUX : 2 * AUX] + packed[2 * AUX : 3 * AUX]


def passage_kernel(
    bounds, shards, per_shard, rows, slot_ref, shard_ref, query_ref, pool_ref, low_col_ref, low_coef_hbm, *refs
):
    ins = refs[:shards]
    out_hbm, half_hbm, coef_ref, col_ref, spread_ref, scale_ref, out_ref, half_ref, low_coef_ref = refs[shards:-3]
    out_sem, half_sem, low_sem = refs[-3:]
    shard = shard_ref[0]
    base = per_shard * rows
    blocks = shards * per_shard
    slots, _, width = pool_ref.shape
    cands = coef_ref.shape[1]
    count = cands // PBLK

    load = pltpu.make_async_copy(low_coef_hbm, low_coef_ref, low_sem)

    @pl.when(shard == 0)
    def _():
        load.start()

    spread_ref[...] = jnp.zeros_like(spread_ref)
    scale_ref[...] = jnp.zeros_like(scale_ref)
    for shift in range(shards):
        source = lax.rem(shard - shift + shards, shards)
        coef_ref[pl.ds(source * base, base), :] = ins[shift][:base, :]
        aux = unpack_aux(ins[shift], base)
        for k in range(per_shard):
            col_ref[source * per_shard + k] = aux[k : k + 1, :]

    def run(spans, low):
        for block in range(blocks):
            cols = jnp.broadcast_to(col_ref[block], (8, cands))
            if low:
                cols = cols + low_col_ref[block]
            col_cols = columns(cols)
            for n in range(count):
                slot = slot_ref[block * count + n]
                scale_ref[slot] = scale_ref[slot] + col_cols[n * PBLK : (n + 1) * PBLK, :]
        for level, (lo, hi) in enumerate(spans):
            for block in range(blocks):
                here = pl.ds(block * rows, rows)
                coef = coef_ref[here, :].astype(F32)
                if low:
                    coef = coef + low_coef_ref[level, here, :]
                    half_ref[level, here, :] = coef.astype(BF16)
                turned = coef.T.astype(BF16)
                for n in range(count):
                    spread_ref[slot_ref[block * count + n], :, block * rows : (block + 1) * rows] = turned[
                        n * PBLK : (n + 1) * PBLK, :
                    ]
            spread = spread_ref[0:slots].reshape(slots * PBLK, blocks * rows)
            scale = scale_ref[0:slots].reshape(slots * PBLK, LANES)[:, level : level + 1]
            for start in range(lo, hi, PIECE):
                end = min(start + PIECE, hi)
                grad = contract(spread, query_ref[:, start:end], 1, 0)
                pool = pool_ref[:, :, start:end].reshape(slots * PBLK, end - start).astype(F32)
                out_ref[:, :, start:end] = (grad - scale * pool).astype(BF16).reshape(slots, PBLK, end - start)
                if end % LANES == 0:
                    done = pl.ds(start // LANES * LANES, end - start // LANES * LANES)
                    pltpu.make_async_copy(out_ref.at[:, :, done], out_hbm.at[:, :, done], out_sem).start()
        if low:
            copy = pltpu.make_async_copy(half_ref, half_hbm, half_sem)
            copy.start()
            copy.wait()
        pltpu.make_async_copy(out_ref, out_hbm, out_sem).wait()

    @pl.when(shard == 0)
    def _():
        load.wait()
        run(bounds, True)

    @pl.when(shard != 0)
    def _():
        run([(0, width)], False)


def query_kernel(
    bounds, shards, per_shard, rows, loss_scale, slot_ref, shard_ref, query_ref, pool_ref, low_row_ref,
    low_half_hbm, *refs,
):
    ins = refs[:shards]
    query_grad_ref, loss_ref = refs[shards : shards + 2]
    cand_ref, coef_ref, row_ref, low_half_ref, sem = refs[shards + 2 :]
    shard = shard_ref[0]
    base = per_shard * rows
    blocks = shards * per_shard
    count = cand_ref.shape[0]
    width = query_ref.shape[1]
    cands = coef_ref.shape[1]

    copy = pltpu.make_async_copy(low_half_hbm, low_half_ref, sem)

    @pl.when(shard == 0)
    def _():
        copy.start()

    loss_low = jnp.zeros((AUX, cands), F32)
    for shift in range(shards):
        source = lax.rem(shard - shift + shards, shards)
        coef_ref[pl.ds(source * base, base), :] = ins[shift][:base, :]
        aux = unpack_aux(ins[shift], base)
        for k in range(per_shard):
            row_ref[source * per_shard + k] = aux[per_shard : per_shard + 1, k * rows : (k + 1) * rows]
        loss_ref[pl.ds(source, 1), :] = aux[per_shard : per_shard + 1, base:]
        loss_low = loss_low + jnp.where(source == 0, aux, 0.0)
    per_row = cands // base
    for r in range(shards):
        low = loss_low[per_shard + 1 + r // per_row : per_shard + 2 + r // per_row, :]
        low = low[:, (r % per_row) * base : (r % per_row + 1) * base]
        loss_ref[r : r + 1, :] = (loss_ref[r : r + 1, :] + low) * loss_scale

    def run(spans, low):
        def step(block, carry):
            take_blocks(pool_ref, slot_ref, block, count, cand_ref)
            rows_here = jnp.broadcast_to(row_ref[block], (8, rows))
            if low:
                rows_here = rows_here + low_row_ref[block]
            row_cols = columns(rows_here)
            here = pl.ds(block * rows, rows)
            for level, (lo, hi) in enumerate(spans):
                coef = low_half_ref[level, here, :] if low else coef_ref[here, :]
                query = query_ref[here, lo:hi].astype(F32)
                cand = cand_ref[:, :, lo:hi].reshape(cands, hi - lo)
                grad = contract(coef, cand, 1, 0) - row_cols[:rows, level : level + 1] * query
                query_grad_ref[here, lo:hi] = grad.astype(BF16)
            return carry

        lax.fori_loop(0, blocks, step, 0)

    @pl.when(shard == 0)
    def _():
        copy.wait()
        run(bounds, True)

    @pl.when(shard != 0)
    def _():
        run([(0, width)], False)


def collect_kernel(target_ref, back_ref, out_ref):
    rows = out_ref.shape[0]
    here = lax.broadcasted_iota(jnp.int32, (rows, target_ref.shape[1]), 0)
    choose = jnp.where(here == target_ref[...], 1.0, 0.0).astype(BF16)
    out_ref[...] = contract(choose, back_ref[...], 1, 0).astype(BF16)


def per_device(queries, passages, neg_lists, positives):
    peers = lax.axis_size("dp")
    shards = lax.axis_size("tensor")
    total_rows, width = queries.shape
    blocks = neg_lists.shape[0] // peers
    count = neg_lists.shape[1]
    rows = total_rows // blocks
    local_blocks = passages.shape[0] // PBLK
    cands = count * PBLK
    per_shard = blocks // shards
    base = per_shard * rows
    slots = peers
    my_index = lax.axis_index("dp")
    shard = lax.axis_index("tensor")
    sizes = [MINP * 2**level for level in range(NPRE)]
    low_sizes = [size for size in sizes if size <= width]
    high_sizes = [size for size in sizes if size > width]
    assert high_sizes == [width * shards // 2, width * shards] and low_sizes[-1] == width
    assert shards == 4 and base == LANES and len(low_sizes) == FULL + 1
    bounds = list(zip([0] + low_sizes[:-1], low_sizes))
    levels = len(bounds)
    weight_total = sum(size / MINP for size in sizes)

    flat = neg_lists.reshape(peers, blocks * count)
    mine = (flat >= 0) & (flat // local_blocks == my_index)
    wanted = jnp.max(jnp.where(mine, flat % local_blocks, -1), axis=1)
    own = lax.dynamic_slice_in_dim(neg_lists, my_index * blocks, blocks, 0)
    valid = own >= 0
    slot = jnp.where(valid, own // local_blocks, 0).reshape(blocks * count)
    spare_slot = jnp.where(valid, own // local_blocks, slots).reshape(blocks * count)
    within = jnp.arange(PBLK, dtype=jnp.int32)
    ids = jnp.where(valid[:, :, None], own[:, :, None] * PBLK + within[None, None, :], -1)
    ids = ids.reshape(blocks, cands).astype(F32)
    target = jnp.where(wanted[:, None] >= 0, wanted[:, None] * PBLK + within[None, :], -1).reshape(1, slots * PBLK)
    pos = positives.reshape(blocks, rows).astype(F32)
    shard_arr = shard.reshape(1).astype(jnp.int32)
    pool_shape = (slots, PBLK, width)

    panels = pl.pallas_call(
        pack_kernel,
        out_shape=pltpu.HBM(pool_shape, BF16),
        in_specs=[smem(), hbm()],
        out_specs=hbm(),
        scratch_shapes=[pltpu.SemaphoreType.DMA(())],
        compiler_params=params(),
        name="pack",
    )(wanted, pltpu.with_memory_space_constraint(passages.reshape(local_blocks, PBLK, width), pltpu.HBM))
    pool = lax.all_to_all(panels, "dp", split_axis=0, concat_axis=0, tiled=True)

    def shift_by(part, s):
        return lax.ppermute(part, "tensor", [(i, (i + s) % shards) for i in range(shards)])

    cand_scratch = pltpu.VMEM((count, PBLK, width), BF16)
    message = jax.ShapeDtypeStruct((base + AUX, cands), F32)
    norms, far = pl.pallas_call(
        partial(first_dots_kernel, bounds, shards, per_shard, rows, (2,)),
        out_shape=[jax.ShapeDtypeStruct((slots, PBLK, LANES), F32), message],
        in_specs=[smem(), smem(), vmem(), vmem()],
        out_specs=[vmem()] * 2,
        scratch_shapes=[cand_scratch],
        compiler_params=params(),
        name="dots_far",
    )(slot, shard_arr, queries, pool)

    def more_dots(shifts, name):
        return pl.pallas_call(
            partial(dots_kernel, shards, per_shard, rows, shifts),
            out_shape=[message] * len(shifts),
            in_specs=[smem(), smem(), vmem(), vmem(), vmem()],
            out_specs=[vmem()] * len(shifts),
            scratch_shapes=[cand_scratch],
            compiler_params=params(),
            name=name,
        )(slot, shard_arr, queries, pool, norms)

    right, left = more_dots((1, 3), "dots_near")
    (here,) = more_dots((0,), "dots_own")
    arrived = [here, shift_by(right, 1), shift_by(far, 2), shift_by(left, 3)]
    low_coef, low_row, low_col, low_loss = pl.pallas_call(
        partial(low_kernel, bounds, rows),
        out_shape=[
            pltpu.HBM((levels, total_rows, cands), F32),
            jax.ShapeDtypeStruct((blocks, 8, rows), F32),
            jax.ShapeDtypeStruct((blocks, 8, cands), F32),
            jax.ShapeDtypeStruct((blocks, rows), F32),
        ],
        in_specs=[smem(), smem()] + [vmem()] * 5,
        out_specs=[hbm()] + [vmem()] * 3,
        scratch_shapes=[
            cand_scratch,
            pltpu.VMEM((levels, rows, cands), F32),
            pltpu.VMEM((levels, total_rows, cands), F32),
            pltpu.SemaphoreType.DMA(()),
        ],
        compiler_params=params(),
        name="low",
    )(slot, shard_arr, queries, pool, norms, ids, pos)

    coefs = pl.pallas_call(
        partial(high_kernel, shards, per_shard, rows, [size / MINP for size in high_sizes]),
        out_shape=[jax.ShapeDtypeStruct((base + COEF_AUX, cands), BF16)] * shards,
        in_specs=[smem()] + [vmem()] * (3 + shards),
        out_specs=[vmem()] * shards,
        compiler_params=params(),
        name="high",
    )(shard_arr, ids, pos, low_loss, *arrived)
    coefs = [coefs[0]] + [shift_by(coefs[s], s) for s in range(1, shards)]

    slot_grad, low_half = pl.pallas_call(
        partial(passage_kernel, bounds, shards, per_shard, rows),
        out_shape=[pltpu.HBM(pool_shape, BF16), pltpu.HBM((levels, total_rows, cands), BF16)],
        in_specs=[smem(), smem()] + [vmem()] * 3 + [hbm()] + [vmem()] * shards,
        out_specs=[hbm()] * 2,
        scratch_shapes=[
            pltpu.VMEM((total_rows, cands), BF16),
            pltpu.VMEM((blocks, 1, cands), F32),
            pltpu.VMEM((slots + 1, PBLK, total_rows), BF16),
            pltpu.VMEM((slots + 1, PBLK, LANES), F32),
            pltpu.VMEM(pool_shape, BF16),
            pltpu.VMEM((levels, total_rows, cands), BF16),
            pltpu.VMEM((levels, total_rows, cands), F32),
            pltpu.SemaphoreType.DMA(()),
            pltpu.SemaphoreType.DMA(()),
            pltpu.SemaphoreType.DMA(()),
        ],
        compiler_params=params(),
        name="passage",
    )(
        spare_slot, shard_arr, queries, pool, low_col,
        pltpu.with_memory_space_constraint(low_coef, pltpu.HBM), *coefs,
    )
    back = lax.all_to_all(slot_grad, "dp", split_axis=0, concat_axis=0, tiled=True)

    query_grad, loss = pl.pallas_call(
        partial(query_kernel, bounds, shards, per_shard, rows, 1.0 / weight_total),
        out_shape=[
            jax.ShapeDtypeStruct((total_rows, width), BF16),
            jax.ShapeDtypeStruct((shards, base), F32),
        ],
        in_specs=[smem(), smem()] + [vmem()] * 3 + [hbm()] + [vmem()] * shards,
        out_specs=[vmem()] * 2,
        scratch_shapes=[
            cand_scratch,
            pltpu.VMEM((total_rows, cands), BF16),
            pltpu.VMEM((blocks, 1, rows), F32),
            pltpu.VMEM((levels, total_rows, cands), BF16),
            pltpu.SemaphoreType.DMA(()),
        ],
        compiler_params=params(),
        name="query",
    )(
        slot, shard_arr, queries, pool, low_row,
        pltpu.with_memory_space_constraint(low_half, pltpu.HBM), *coefs,
    )

    passage_grad = pl.pallas_call(
        collect_kernel,
        out_shape=jax.ShapeDtypeStruct((local_blocks * PBLK, width), BF16),
        in_specs=[vmem(), vmem()],
        out_specs=vmem(),
        compiler_params=params(),
        name="collect",
    )(target, back.reshape(slots * PBLK, width))
    return (
        query_grad,
        passage_grad,
        loss.reshape(total_rows),
    )


def solution(mesh):
    return jax.shard_map(
        per_device,
        mesh=mesh,
        in_specs=(P("dp", "tensor"), P("dp", "tensor"), P(), P("dp")),
        out_specs=(P("dp", "tensor"), P("dp", "tensor"), P("dp")),
        check_vma=False,
    )
```

```python
from functools import partial

import jax
import jax.numpy as jnp
from jax import lax
from jax.experimental import pallas as pl
from jax.experimental.pallas import tpu as pltpu
from jax.sharding import PartitionSpec as P

MINP = 64
NPRE = 7
PBLK = 16

EPS = 1e-06
INV_TEMP = 20.0

F32 = jnp.float32
BF16 = jnp.bfloat16

AUX = 8
COEF_AUX = 32
LANES = 128
PIECE = 256


def vmem():
    return pl.BlockSpec(memory_space=pltpu.VMEM)


def smem():
    return pl.BlockSpec(memory_space=pltpu.SMEM)


def hbm():
    return pl.BlockSpec(memory_space=pltpu.HBM)


def params():
    return pltpu.CompilerParams(vmem_limit_bytes=20 * 2**20)


def contract(a, b, da, db):
    return lax.dot_general(a, b, (((da,), (db,)), ((), ())), preferred_element_type=F32)


def eye(n):
    return lax.broadcasted_iota(jnp.int32, (n, n), 0) == lax.broadcasted_iota(jnp.int32, (n, n), 1)


def to_col(row):
    return jnp.sum(jnp.where(eye(row.shape[1]), row, 0.0), axis=1, keepdims=True)


def to_row(col):
    return jnp.sum(jnp.where(eye(col.shape[0]), col, 0.0), axis=0, keepdims=True)


def square_sums(half):
    wide = half.astype(F32)
    return jnp.sum(wide * wide, axis=1, keepdims=True)


def columns(table):
    table = jnp.concatenate([table, jnp.zeros((8, LANES - table.shape[1]), F32)], axis=1) if table.shape[1] < LANES else table
    return jnp.concatenate([table, jnp.zeros((LANES - 8, table.shape[1]), F32)], axis=0).T


def terms(dots, qq_col, pp_row, live, labels, weight):
    a = lax.rsqrt(qq_col + EPS)
    b = jnp.where(live, lax.rsqrt(pp_row + EPS), 0.0)
    scale = (a * INV_TEMP) * b
    logits = dots * scale
    exponent = jnp.where(live, jnp.exp(logits), 0.0)
    total = jnp.sum(exponent, axis=1, keepdims=True)
    gradient = weight * (exponent * (1.0 / total) - labels)
    inner = gradient * logits
    row = (a * a) * jnp.sum(inner, axis=1, keepdims=True)
    col = (b * b) * jnp.sum(inner, axis=0, keepdims=True)
    return gradient * scale, row, col, weight * jnp.log(total), weight * logits


def take_blocks(pool_ref, slot_ref, block, count, out_ref):
    for n in range(count):
        out_ref[n] = pool_ref[slot_ref[block * count + n]]


def pool_norms(pool_ref, norm_ref, bounds):
    step_slots = 8
    lane = lax.broadcasted_iota(jnp.int32, (step_slots * PBLK, LANES), 1)

    def step(i, carry):
        here = pl.ds(i * step_slots, step_slots)
        block = pool_ref[here]
        wide = block.reshape(step_slots * PBLK, block.shape[2]).astype(F32)
        square = wide * wide
        total = jnp.zeros((step_slots * PBLK, 1), F32)
        result = jnp.zeros((step_slots * PBLK, LANES), F32)
        for level, (low, high) in enumerate(bounds):
            total = total + jnp.sum(square[:, low:high], axis=1, keepdims=True)
            result = jnp.where(lane == level, total, result)
        norm_ref[here] = result.reshape(step_slots, PBLK, LANES)
        return carry

    lax.fori_loop(0, pool_ref.shape[0] // step_slots, step, 0)


def norm_rows(norm_ref, slot_ref, block, count):
    table = jnp.concatenate([norm_ref[slot_ref[block * count + n]] for n in range(count)], axis=0)
    return table.T[:8, :]


def pack_kernel(wanted_ref, block_ref, out_ref, sem):
    def step(d, carry):
        source = block_ref.at[jnp.maximum(wanted_ref[d], 0)]
        pltpu.make_async_copy(source, out_ref.at[d], sem).start()
        return carry

    lax.fori_loop(0, out_ref.shape[0], step, 0, unroll=8)
    pltpu.make_async_copy(out_ref, out_ref, sem).wait()


def dots_kernel(shards, per_shard, rows, shifts, slot_ref, shard_ref, query_ref, pool_ref, norm_ref, *refs):
    outs, cand_ref = refs[:-1], refs[-1]
    count, _, width = cand_ref.shape
    shard = shard_ref[0]
    base = per_shard * rows
    for shift, out_ref in zip(shifts, outs):
        target = lax.rem(shard + shift, shards)
        for k in range(per_shard):
            block = target * per_shard + k
            take_blocks(pool_ref, slot_ref, block, count, cand_ref)
            query = query_ref[pl.ds(block * rows, rows), :]
            cand = cand_ref[...].reshape(count * PBLK, width)
            out_ref[k * rows : (k + 1) * rows, :] = contract(query, cand, 1, 1)
            out_ref[base + k : base + k + 1, :] = norm_rows(norm_ref, slot_ref, block, count)[0:1, :]
            out_ref[base + per_shard : base + per_shard + 1, k * rows : (k + 1) * rows] = to_row(square_sums(query))


def first_dots_kernel(shards, per_shard, rows, shifts, slot_ref, shard_ref, query_ref, pool_ref, norm_ref, *refs):
    pool_norms(pool_ref, norm_ref, [(0, pool_ref.shape[2])])
    dots_kernel(shards, per_shard, rows, shifts, slot_ref, shard_ref, query_ref, pool_ref, norm_ref, *refs)


def prefix_dots(bounds, rows, block, query_ref, cand_ref, count):
    dots = None
    for low, high in bounds:
        query = query_ref[pl.ds(block * rows, rows), low:high]
        cand = cand_ref[:, :, low:high]
        part = contract(query, cand.reshape(count * PBLK, high - low), 1, 1)
        dots = part if dots is None else dots + part
        yield dots


def low_kernel(
    bounds, rows, first, renorm, slot_ref, shard_ref, query_ref, pool_ref, ids_ref, pos_ref, norm_in_ref, after_ref,
    coef_hbm, row_ref, col_ref, loss_ref, norm_ref, cand_ref, term_ref, coef_ref, sem,
):
    del after_ref
    count = cand_ref.shape[0]
    levels, pairs, cands, _ = coef_ref.shape
    per_pair = LANES // rows

    @pl.when(shard_ref[0] == 0)
    def _():
        if renorm:
            pool_norms(pool_ref, norm_ref, bounds)
        norms = norm_ref if renorm else norm_in_ref
        row_ref[...] = jnp.zeros_like(row_ref)
        col_ref[...] = jnp.zeros_like(col_ref)

        def step(pair, carry):
            row_sums, col_sums = [], []
            for j in range(per_pair):
                local = pair * per_pair + j
                block = first + local
                take_blocks(pool_ref, slot_ref, block, count, cand_ref)
                pp = norm_rows(norms, slot_ref, block, count)
                ids = ids_ref[pl.ds(block, 1), :]
                live = ids >= 0.0
                labels = jnp.where(ids == to_col(pos_ref[pl.ds(block, 1), :]), 1.0, 0.0)
                here = pl.ds(block * rows, rows)
                qq = jnp.zeros((rows, 1), F32)
                entropy = jnp.zeros((rows, 1), F32)
                logit_sum = jnp.zeros((rows, cands), F32)
                sums = prefix_dots(bounds, rows, block, query_ref, cand_ref, count)
                for level, ((low, high), dots) in enumerate(zip(bounds, sums)):
                    qq = qq + square_sums(query_ref[here, low:high])
                    coef, row, col, part, logits = terms(
                        dots, qq, pp[level : level + 1, :], live, labels, float(high // MINP)
                    )
                    term_ref[level, j * rows : (j + 1) * rows, :] = coef
                    row_sums.append(row)
                    col_sums.append(col)
                    entropy = entropy + part
                    logit_sum = logit_sum + logits
                loss = entropy - jnp.sum(labels * logit_sum, axis=1, keepdims=True)
                loss_ref[pl.ds(local, 1), :] = to_row(loss)
                row = jnp.zeros((rows, 1), F32)
                col = jnp.zeros((1, cands), F32)
                for level in reversed(range(levels)):
                    row = row + row_sums[level]
                    col = col + col_sums[level]
                    row_ref[local, level : level + 1, :] = to_row(row)
                    col_ref[local, level : level + 1, :] = col
                row_sums, col_sums = [], []
            coef = jnp.zeros((LANES, cands), F32)
            for level in reversed(range(levels)):
                coef = coef + term_ref[level]
                coef_ref[level, pair] = coef.T
            pltpu.make_async_copy(coef_ref.at[:, pair], coef_hbm.at[:, pair], sem).start()
            return carry

        lax.fori_loop(0, pairs, step, 0)
        pltpu.make_async_copy(coef_ref, coef_hbm, sem).wait()

    @pl.when(shard_ref[0] != 0)
    def _():
        loss_ref[...] = jnp.zeros_like(loss_ref)


def high_kernel(shards, per_shard, rows, weights, shard_ref, ids_ref, pos_ref, after_ref, *refs):
    del after_ref
    ins, outs, loss_ref = refs[:shards], refs[shards:-1], refs[-1]
    shard = shard_ref[0]
    base = per_shard * rows
    width = ids_ref.shape[1]
    in_half = [
        jnp.where(lax.rem(shard - shift + shards, shards) < shards // 2, 1.0, 0.0)
        for shift in range(shards)
    ]

    def total(span, keep):
        pieces = [ref[span, :] * scale if keep else ref[span, :] for ref, scale in zip(ins, in_half)]
        return (pieces[0] + pieces[1]) + (pieces[2] + pieces[3])

    below = slice(base, base + AUX)
    half_rows, half_cols, full_rows, full_cols, losses, coefs = [], [], [], [], [], []
    aux_half, aux_full = total(below, True), total(below, False)
    for k in range(per_shard):
        block = shard * per_shard + k
        ids = ids_ref[pl.ds(block, 1), :]
        live = ids >= 0.0
        labels = jnp.where(ids == to_col(pos_ref[pl.ds(block, 1), :]), 1.0, 0.0)
        span = slice(k * rows, (k + 1) * rows)
        results = []
        for keep, aux, weight in ((True, aux_half, weights[0]), (False, aux_full, weights[1])):
            qq = to_col(aux[per_shard : per_shard + 1, span])
            results.append(terms(total(span, keep), qq, aux[k : k + 1, :], live, labels, weight))
        (coef_h, row_h, col_h, part_h, logit_h), (coef_f, row_f, col_f, part_f, logit_f) = results
        loss = part_h + part_f - jnp.sum(labels * (logit_h + logit_f), axis=1, keepdims=True)
        coefs.append(((coef_h + coef_f).astype(BF16), coef_f.astype(BF16)))
        half_rows.append(to_row(row_h + row_f))
        full_rows.append(to_row(row_f))
        half_cols.append(col_h + col_f)
        full_cols.append(col_f)
        losses.append(to_row(loss))
    loss_ref[...] = jnp.concatenate(losses, axis=1)

    def aux_rows(rows_list, cols_list):
        line = jnp.concatenate(rows_list + [jnp.zeros((1, width - base), F32)], axis=1)
        table = jnp.concatenate(cols_list + [line], axis=0)
        table = jnp.concatenate([table, jnp.zeros((AUX - table.shape[0], width), F32)], axis=0)
        first = table.astype(BF16).astype(F32)
        second = (table - first).astype(BF16).astype(F32)
        third = table - first - second
        return jnp.concatenate([first, second, third, jnp.zeros_like(table)], axis=0).astype(BF16)

    aux = (aux_rows(half_rows, half_cols), aux_rows(full_rows, full_cols))
    for shift in range(shards):
        out_ref = outs[shift]
        high_target = lax.rem(shard + shift, shards) >= shards // 2
        for which, chosen in ((1, high_target), (0, jnp.logical_not(high_target))):

            @pl.when(chosen)
            def _():
                for k in range(per_shard):
                    out_ref[k * rows : (k + 1) * rows, :] = coefs[k][which]
                out_ref[base : base + COEF_AUX, :] = aux[which]


def unpack_aux(ref, base):
    packed = ref[base : base + COEF_AUX, :].astype(F32)
    return packed[:AUX] + packed[AUX : 2 * AUX] + packed[2 * AUX : 3 * AUX]


def passage_kernel(
    bounds, shards, per_shard, rows, slot_ref, shard_ref, query_ref, pool_ref, low_col_a_ref, low_col_b_ref,
    low_coef_a_hbm, low_coef_b_hbm, *refs
):
    ins = refs[:shards]
    out_hbm, half_hbm, turned_ref, col_ref, spread_ref, scale_ref, out_ref, half_ref, low_coef_ref = refs[shards:-3]
    out_sem, half_sem, low_sem = refs[-3:]
    shard = shard_ref[0]
    base = per_shard * rows
    blocks = shards * per_shard
    slots, _, width = pool_ref.shape
    pairs, cands, _ = turned_ref.shape
    per_pair = LANES // rows
    count = cands // PBLK
    split = low_coef_a_hbm.shape[1]
    loads = [
        pltpu.make_async_copy(low_coef_a_hbm, low_coef_ref.at[:, pl.ds(0, split)], low_sem.at[0]),
        pltpu.make_async_copy(low_coef_b_hbm, low_coef_ref.at[:, pl.ds(split, pairs - split)], low_sem.at[1]),
    ]

    @pl.when(shard == 0)
    def _():
        for load in loads:
            load.start()

    spread_ref[...] = jnp.zeros_like(spread_ref)
    scale_ref[...] = jnp.zeros_like(scale_ref)
    for shift in range(shards):
        source = lax.rem(shard - shift + shards, shards)
        turned_ref[source] = ins[shift][:base, :].astype(F32).T
        aux = unpack_aux(ins[shift], base)
        for k in range(per_shard):
            col_ref[source * per_shard + k] = aux[k : k + 1, :]

    def run(spans, low):
        for block in range(blocks):
            cols = jnp.broadcast_to(col_ref[block], (8, cands))
            if low:
                half = blocks // 2
                cols = cols + (low_col_a_ref[block] if block < half else low_col_b_ref[block - half])
            col_cols = columns(cols)
            for n in range(count):
                slot = slot_ref[block * count + n]
                scale_ref[slot] = scale_ref[slot] + col_cols[n * PBLK : (n + 1) * PBLK, :]
        for level, (lo, hi) in enumerate(spans):
            for pair in range(pairs):
                coef = turned_ref[pair]
                if low:
                    coef = coef + low_coef_ref[level, pair]
                coef = coef.astype(BF16)
                if low:
                    half_ref[level, pair] = coef
                for j in range(per_pair):
                    block = pair * per_pair + j
                    lanes = slice(j * rows, (j + 1) * rows)
                    for n in range(count):
                        spread_ref[slot_ref[block * count + n], :, block * rows : (block + 1) * rows] = coef[
                            n * PBLK : (n + 1) * PBLK, lanes
                        ]
            if low:
                pltpu.make_async_copy(half_ref.at[level], half_hbm.at[level], half_sem).start()
            spread = spread_ref[0:slots].reshape(slots * PBLK, blocks * rows)
            scale = scale_ref[0:slots].reshape(slots * PBLK, LANES)[:, level : level + 1]
            for start in range(lo, hi, PIECE):
                end = min(start + PIECE, hi)
                grad = contract(spread, query_ref[:, start:end], 1, 0)
                pool = pool_ref[:, :, start:end].reshape(slots * PBLK, end - start).astype(F32)
                out_ref[:, :, start:end] = (grad - scale * pool).astype(BF16).reshape(slots, PBLK, end - start)
                if end % LANES == 0:
                    done = pl.ds(start // LANES * LANES, end - start // LANES * LANES)
                    pltpu.make_async_copy(out_ref.at[:, :, done], out_hbm.at[:, :, done], out_sem).start()
        if low:
            pltpu.make_async_copy(half_ref, half_hbm, half_sem).wait()
        pltpu.make_async_copy(out_ref, out_hbm, out_sem).wait()

    @pl.when(shard == 0)
    def _():
        for load in loads:
            load.wait()
        run(bounds, True)

    @pl.when(shard != 0)
    def _():
        run([(0, width)], False)


def query_kernel(
    bounds, shards, per_shard, rows, loss_scale, slot_ref, shard_ref, query_ref, pool_ref, low_row_a_ref, low_row_b_ref,
    low_loss_a_ref, low_loss_b_ref, high_loss_ref, low_half_hbm, *refs
):
    ins = refs[:shards]
    query_grad_ref, loss_ref = refs[shards : shards + 2]
    cand_ref, coef_ref, row_ref, low_half_ref, sem = refs[shards + 2 :]
    shard = shard_ref[0]
    base = per_shard * rows
    blocks = shards * per_shard
    count = cand_ref.shape[0]
    width = query_ref.shape[1]
    cands = coef_ref.shape[1]
    per_pair = LANES // rows
    copy = pltpu.make_async_copy(low_half_hbm, low_half_ref, sem)

    @pl.when(shard == 0)
    def _():
        copy.start()

    for shift in range(shards):
        source = lax.rem(shard - shift + shards, shards)
        coef_ref[pl.ds(source * base, base), :] = ins[shift][:base, :]
        aux = unpack_aux(ins[shift], base)
        for k in range(per_shard):
            row_ref[source * per_shard + k] = aux[per_shard : per_shard + 1, k * rows : (k + 1) * rows]
    half = blocks // 2
    for block in range(blocks):
        line = low_loss_a_ref[block : block + 1, :] if block < half else low_loss_b_ref[block - half : block - half + 1, :]
        loss_ref[block // per_pair : block // per_pair + 1, block % per_pair * rows : (block % per_pair + 1) * rows] = line
    loss_ref[pl.ds(shard, 1), :] = loss_ref[pl.ds(shard, 1), :] + high_loss_ref[...]
    loss_ref[...] = loss_ref[...] * loss_scale

    def run(spans, low):
        def one(pair, low_row_ref, first):
            for j in range(per_pair):
                local = pair * per_pair + j
                block = first * per_pair + local
                take_blocks(pool_ref, slot_ref, block, count, cand_ref)
                rows_here = jnp.broadcast_to(row_ref[block], (8, rows))
                if low:
                    rows_here = rows_here + low_row_ref[local]
                row_cols = columns(rows_here)
                here = pl.ds(block * rows, rows)
                for level, (lo, hi) in enumerate(spans):
                    query = query_ref[here, lo:hi].astype(F32)
                    cand = cand_ref[:, :, lo:hi].reshape(cands, hi - lo)
                    if low:
                        coef = low_half_ref[level, first + pair][:, j * rows : (j + 1) * rows]
                        grad = contract(coef, cand, 0, 0)
                    else:
                        grad = contract(coef_ref[here, :], cand, 1, 0)
                    grad = grad - row_cols[:rows, level : level + 1] * query
                    query_grad_ref[here, lo:hi] = grad.astype(BF16)

        def step(pair, carry):
            one(pair, low_row_a_ref, 0)
            one(pair, low_row_b_ref, half // per_pair)
            return carry

        lax.fori_loop(0, half // per_pair, step, 0)

    @pl.when(shard == 0)
    def _():
        copy.wait()
        run(bounds, True)

    @pl.when(shard != 0)
    def _():
        run([(0, width)], False)


def collect_kernel(target_ref, back_ref, out_ref, choose_ref):
    rows, count = choose_ref.shape

    @pl.when(pl.program_id(0) == 0)
    def _():
        here = lax.broadcasted_iota(jnp.int32, (rows, count), 0)
        choose_ref[...] = jnp.where(here == target_ref[...], 1.0, 0.0).astype(BF16)

    out_ref[...] = contract(choose_ref[...], back_ref[...], 1, 0).astype(BF16)


def per_device(queries, passages, neg_lists, positives):
    peers = lax.axis_size("dp")
    shards = lax.axis_size("tensor")
    total_rows, width = queries.shape
    blocks = neg_lists.shape[0] // peers
    count = neg_lists.shape[1]
    rows = total_rows // blocks
    local_blocks = passages.shape[0] // PBLK
    cands = count * PBLK
    per_shard = blocks // shards
    base = per_shard * rows
    slots = peers
    my_index = lax.axis_index("dp")
    shard = lax.axis_index("tensor")
    sizes = [MINP * 2**level for level in range(NPRE)]
    low_sizes = [size for size in sizes if size <= width]
    high_sizes = [size for size in sizes if size > width]
    assert high_sizes == [width * shards // 2, width * shards] and low_sizes[-1] == width
    assert shards == 4 and base == LANES and blocks % 4 == 0
    bounds = list(zip([0] + low_sizes[:-1], low_sizes))
    levels = len(bounds)
    weight_total = sum(size / MINP for size in sizes)

    flat = neg_lists.reshape(peers, blocks * count)
    mine = (flat >= 0) & (flat // local_blocks == my_index)
    wanted = jnp.max(jnp.where(mine, flat % local_blocks, -1), axis=1)
    own = lax.dynamic_slice_in_dim(neg_lists, my_index * blocks, blocks, 0)
    valid = own >= 0
    slot = jnp.where(valid, own // local_blocks, 0).reshape(blocks * count)
    spare_slot = jnp.where(valid, own // local_blocks, slots).reshape(blocks * count)
    within = jnp.arange(PBLK, dtype=jnp.int32)
    ids = jnp.where(valid[:, :, None], own[:, :, None] * PBLK + within[None, None, :], -1)
    ids = ids.reshape(blocks, cands).astype(F32)
    target = jnp.where(wanted[:, None] >= 0, wanted[:, None] * PBLK + within[None, :], -1).reshape(1, slots * PBLK)
    pos = positives.reshape(blocks, rows).astype(F32)
    shard_arr = shard.reshape(1).astype(jnp.int32)
    pool_shape = (slots, PBLK, width)

    panels = pl.pallas_call(
        pack_kernel,
        out_shape=pltpu.HBM(pool_shape, BF16),
        in_specs=[smem(), vmem()],
        out_specs=hbm(),
        scratch_shapes=[pltpu.SemaphoreType.DMA(())],
        compiler_params=params(),
        name="pack",
    )(wanted, passages.reshape(local_blocks, PBLK, width))
    pool = lax.all_to_all(panels, "dp", split_axis=0, concat_axis=0, tiled=True)

    def shift_by(part, s):
        return lax.ppermute(part, "tensor", [(i, (i + s) % shards) for i in range(shards)])

    cand_scratch = pltpu.VMEM((count, PBLK, width), BF16)
    message = jax.ShapeDtypeStruct((base + AUX, cands), F32)
    norm_shape = (slots, PBLK, LANES)
    norms, far, right, left = pl.pallas_call(
        partial(first_dots_kernel, shards, per_shard, rows, (2, 1, 3)),
        out_shape=[jax.ShapeDtypeStruct(norm_shape, F32)] + [message] * 3,
        in_specs=[smem(), smem(), vmem(), vmem()],
        out_specs=[vmem()] * 4,
        scratch_shapes=[cand_scratch],
        compiler_params=params(),
        name="dots",
    )(slot, shard_arr, queries, pool)
    (here,) = pl.pallas_call(
        partial(dots_kernel, shards, per_shard, rows, (0,)),
        out_shape=[message],
        in_specs=[smem(), smem(), vmem(), vmem(), vmem()],
        out_specs=[vmem()],
        scratch_shapes=[cand_scratch],
        compiler_params=params(),
        name="dots_own",
    )(slot, shard_arr, queries, pool, norms)
    arrived = [here, shift_by(right, 1), shift_by(far, 2), shift_by(left, 3)]

    pairs = total_rows // LANES
    half_pairs, half_blocks = pairs // 2, blocks // 2

    def low_terms(first, renorm, norm_table, after, name):
        return pl.pallas_call(
            partial(low_kernel, bounds, rows, first, renorm),
            out_shape=[
                pltpu.HBM((levels, half_pairs, cands, LANES), F32),
                jax.ShapeDtypeStruct((half_blocks, 8, rows), F32),
                jax.ShapeDtypeStruct((half_blocks, 8, cands), F32),
                jax.ShapeDtypeStruct((half_blocks, rows), F32),
                jax.ShapeDtypeStruct(norm_shape if renorm else (8, LANES), F32),
            ],
            in_specs=[smem(), smem()] + [vmem()] * 5 + [pl.BlockSpec(memory_space=pl.ANY)],
            out_specs=[hbm()] + [vmem()] * 4,
            scratch_shapes=[
                cand_scratch,
                pltpu.VMEM((levels, LANES, cands), F32),
                pltpu.VMEM((levels, half_pairs, cands, LANES), F32),
                pltpu.SemaphoreType.DMA(()),
            ],
            compiler_params=params(),
            name=name,
        )(slot, shard_arr, queries, pool, ids, pos, norm_table, after)

    coef_a, row_a, col_a, loss_a, level_norms = low_terms(0, True, ids, here, "low_a")
    *coefs, high_loss = pl.pallas_call(
        partial(high_kernel, shards, per_shard, rows, [size / MINP for size in high_sizes]),
        out_shape=[jax.ShapeDtypeStruct((base + COEF_AUX, cands), BF16)] * shards
        + [jax.ShapeDtypeStruct((1, base), F32)],
        in_specs=[smem()] + [vmem()] * 2 + [pl.BlockSpec(memory_space=pl.ANY)] + [vmem()] * shards,
        out_specs=[vmem()] * (shards + 1),
        compiler_params=params(),
        name="high",
    )(shard_arr, ids, pos, loss_a, *arrived)
    coef_b, row_b, col_b, loss_b, _ = low_terms(half_blocks, False, level_norms, high_loss, "low_b")
    coefs = [coefs[0]] + [shift_by(coefs[s], s) for s in range(1, shards)]

    pinned = partial(pltpu.with_memory_space_constraint, memory_space=pltpu.HBM)
    half_shape = (levels, pairs, cands, LANES)
    slot_grad, low_half = pl.pallas_call(
        partial(passage_kernel, bounds, shards, per_shard, rows),
        out_shape=[pltpu.HBM(pool_shape, BF16), pltpu.HBM(half_shape, BF16)],
        in_specs=[smem(), smem()] + [vmem()] * 4 + [hbm()] * 2 + [vmem()] * shards,
        out_specs=[hbm()] * 2,
        scratch_shapes=[
            pltpu.VMEM((pairs, cands, LANES), F32),
            pltpu.VMEM((blocks, 1, cands), F32),
            pltpu.VMEM((slots + 1, PBLK, total_rows), BF16),
            pltpu.VMEM((slots + 1, PBLK, LANES), F32),
            pltpu.VMEM(pool_shape, BF16),
            pltpu.VMEM(half_shape, BF16),
            pltpu.VMEM(half_shape, F32),
            pltpu.SemaphoreType.DMA(()),
            pltpu.SemaphoreType.DMA(()),
            pltpu.SemaphoreType.DMA((2,)),
        ],
        compiler_params=params(),
        name="passage",
    )(spare_slot, shard_arr, queries, pool, col_a, col_b, pinned(coef_a), pinned(coef_b), *coefs)
    back = lax.all_to_all(slot_grad, "dp", split_axis=0, concat_axis=0, tiled=True)

    query_grad, loss = pl.pallas_call(
        partial(query_kernel, bounds, shards, per_shard, rows, 1.0 / weight_total),
        out_shape=[
            jax.ShapeDtypeStruct((total_rows, width), BF16),
            jax.ShapeDtypeStruct((shards, base), F32),
        ],
        in_specs=[smem(), smem()] + [vmem()] * 7 + [hbm()] + [vmem()] * shards,
        out_specs=[vmem()] * 2,
        scratch_shapes=[
            cand_scratch,
            pltpu.VMEM((total_rows, cands), BF16),
            pltpu.VMEM((blocks, 1, rows), F32),
            pltpu.VMEM(half_shape, BF16),
            pltpu.SemaphoreType.DMA(()),
        ],
        compiler_params=params(),
        name="query",
    )(slot, shard_arr, queries, pool, row_a, row_b, loss_a, loss_b, high_loss, pinned(low_half), *coefs)
    loss = lax.psum(loss, "tensor")

    piece = width // 4
    passage_grad = pl.pallas_call(
        collect_kernel,
        grid=(width // piece,),
        out_shape=jax.ShapeDtypeStruct((local_blocks * PBLK, width), BF16),
        in_specs=[
            pl.BlockSpec((1, slots * PBLK), lambda i: (0, 0)),
            pl.BlockSpec((slots * PBLK, piece), lambda i: (0, i)),
        ],
        out_specs=pl.BlockSpec((local_blocks * PBLK, piece), lambda i: (0, i)),
        scratch_shapes=[pltpu.VMEM((local_blocks * PBLK, slots * PBLK), BF16)],
        compiler_params=params(),
        name="collect",
    )(target, back.reshape(slots * PBLK, width))
    return (
        query_grad,
        passage_grad,
        loss.reshape(total_rows),
    )


def solution(mesh):
    return jax.shard_map(
        per_device,
        mesh=mesh,
        in_specs=(P("dp", "tensor"), P("dp", "tensor"), P(), P("dp")),
        out_specs=(P("dp", "tensor"), P("dp", "tensor"), P("dp")),
        check_vma=False,
    )
```

```python
from functools import partial

import jax
import jax.numpy as jnp
from jax import lax
from jax.experimental import pallas as pl
from jax.experimental.pallas import tpu as pltpu
from jax.sharding import PartitionSpec as P

MINP = 64
NPRE = 7
PBLK = 16

EPS = 1e-06
INV_TEMP = 20.0

F32 = jnp.float32
BF16 = jnp.bfloat16

AUX = 8
COEF_AUX = 32
LANES = 128
PIECE = 256
CHUNKS = 4


def vmem():
    return pl.BlockSpec(memory_space=pltpu.VMEM)


def smem():
    return pl.BlockSpec(memory_space=pltpu.SMEM)


def hbm():
    return pl.BlockSpec(memory_space=pltpu.HBM)


def params():
    return pltpu.CompilerParams(vmem_limit_bytes=20 * 2**20)


def contract(a, b, da, db):
    return lax.dot_general(a, b, (((da,), (db,)), ((), ())), preferred_element_type=F32)


def eye(n):
    return lax.broadcasted_iota(jnp.int32, (n, n), 0) == lax.broadcasted_iota(jnp.int32, (n, n), 1)


def to_col(row):
    return jnp.sum(jnp.where(eye(row.shape[1]), row, 0.0), axis=1, keepdims=True)


def to_row(col):
    return jnp.sum(jnp.where(eye(col.shape[0]), col, 0.0), axis=0, keepdims=True)


def square_sums(half):
    wide = half.astype(F32)
    return jnp.sum(wide * wide, axis=1, keepdims=True)


def columns(table):
    table = jnp.concatenate([table, jnp.zeros((8, LANES - table.shape[1]), F32)], axis=1) if table.shape[1] < LANES else table
    return jnp.concatenate([table, jnp.zeros((LANES - 8, table.shape[1]), F32)], axis=0).T


def terms(dots, a, pp_row, live, labels, weight):
    b = jnp.where(live, lax.rsqrt(pp_row + EPS), 0.0)
    scale = (a * INV_TEMP) * b
    logits = dots * scale
    exponent = jnp.where(live, jnp.exp(logits), 0.0)
    total = jnp.sum(exponent, axis=1, keepdims=True)
    gradient = weight * (exponent * (1.0 / total) - labels)
    inner = gradient * logits
    row = jnp.square(a[:, :1]) * jnp.sum(inner, axis=1, keepdims=True)
    col = (b * b) * jnp.sum(inner, axis=0, keepdims=True)
    return gradient * scale, row, col, weight * jnp.log(total), weight * logits


def take_blocks(pool_ref, slot_ref, block, count, out_ref):
    for n in range(count):
        out_ref[n] = pool_ref[slot_ref[block * count + n]]


def pool_norms(pool_ref, norm_ref, bounds):
    step_slots = 4
    rows = step_slots * PBLK
    lane = lax.broadcasted_iota(jnp.int32, (rows, LANES), 1)

    def lane_sum(part):
        return jnp.sum(part, axis=1, keepdims=True)

    def step(i, carry):
        here = pl.ds(i * step_slots, step_slots)
        wide = pool_ref[here].reshape(rows, pool_ref.shape[2]).astype(F32)
        square = wide * wide
        result, before, inside = None, None, None
        for level, (low, high) in enumerate(bounds):
            if high < LANES:
                total = lane_sum(jnp.where(lane < high, square[:, :LANES], 0.0))
            else:
                start = low // LANES * LANES
                parts = [square[:, j : j + LANES] for j in range(start, high, LANES)]
                while len(parts) > 1:
                    parts = [x + y for x, y in zip(parts[::2], parts[1::2])]
                total = lane_sum(parts[0])
                if start:
                    total = total + before
            before = total
            result = jnp.broadcast_to(total, (rows, LANES)) if result is None else jnp.where(lane == level, total, result)
        norm_ref[here] = result.reshape(step_slots, PBLK, LANES)
        return carry

    lax.fori_loop(0, pool_ref.shape[0] // step_slots, step, 0, unroll=4)


def norm_rows(norm_ref, slot_ref, block, count):
    table = jnp.concatenate([norm_ref[slot_ref[block * count + n]] for n in range(count)], axis=0)
    return table.T[:8, :]


def pack_kernel(wanted_ref, block_hbm, out_hbm, block_ref, out_ref, in_sem, out_sem):
    load = pltpu.make_async_copy(block_hbm, block_ref, in_sem)
    load.start()
    load.wait()
    size = out_ref.shape[0] // CHUNKS
    for chunk in range(CHUNKS):

        def step(i, carry):
            d = chunk * size + i
            out_ref[d] = block_ref[jnp.maximum(wanted_ref[d], 0)]
            return carry

        lax.fori_loop(0, size, step, 0, unroll=8)
        part = pl.ds(chunk * size, size)
        pltpu.make_async_copy(out_ref.at[part], out_hbm.at[part], out_sem).start()
    pltpu.make_async_copy(out_ref, out_hbm, out_sem).wait()


def prep_kernel(bounds, rows, query_ref, ids_ref, pos_ref, scale_ref, full_ref, label_ref, mask_ref):
    blocks, cands = ids_ref.shape
    lane = lax.broadcasted_iota(jnp.int32, (rows, LANES), 1)

    def step(block, carry):
        here = pl.ds(block * rows, rows)
        total = jnp.zeros((rows, 1), F32)
        for level, (low, high) in enumerate(bounds):
            total = total + square_sums(query_ref[here, low:high])
            scale_ref[level, here, :] = jnp.broadcast_to(lax.rsqrt(total + EPS), (rows, LANES))
        full_ref[block] = to_row(total)
        first = query_ref[here, :LANES].astype(F32)
        split = bounds[0][1]
        mask_ref[0, here, :] = jnp.where(lane < split, first, 0.0).astype(BF16)
        mask_ref[1, here, :] = jnp.where(lane < split, 0.0, first).astype(BF16)
        label_ref[here, :] = jnp.where(ids_ref[pl.ds(block, 1), :] == to_col(pos_ref[pl.ds(block, 1), :]), 1.0, 0.0)
        return carry

    lax.fori_loop(0, blocks, step, 0)


def dots_kernel(
    shards, per_shard, rows, level, shifts, slot_ref, shard_ref, query_ref, pool_ref, full_ref, norm_ref, *refs
):
    outs, cand_ref = refs[:-1], refs[-1]
    count, _, width = cand_ref.shape
    shard = shard_ref[0]
    base = per_shard * rows
    for shift, out_ref in zip(shifts, outs):
        target = lax.rem(shard + shift, shards)
        for k in range(per_shard):
            block = target * per_shard + k
            take_blocks(pool_ref, slot_ref, block, count, cand_ref)
            query = query_ref[pl.ds(block * rows, rows), :]
            cand = cand_ref[...].reshape(count * PBLK, width)
            out_ref[k * rows : (k + 1) * rows, :] = contract(query, cand, 1, 1)
            out_ref[base + k : base + k + 1, :] = norm_rows(norm_ref, slot_ref, block, count)[level : level + 1, :]
            out_ref[base + per_shard : base + per_shard + 1, k * rows : (k + 1) * rows] = full_ref[block]


def first_dots_kernel(
    bounds, shards, per_shard, rows, shifts, slot_ref, shard_ref, query_ref, pool_ref, full_ref, norm_ref, *refs
):
    pool_norms(pool_ref, norm_ref, bounds)
    dots_kernel(
        shards, per_shard, rows, len(bounds) - 1, shifts, slot_ref, shard_ref, query_ref, pool_ref, full_ref, norm_ref, *refs
    )


def prefix_dots(bounds, rows, block, query_ref, mask_ref, cand_ref):
    here = pl.ds(block * rows, rows)
    cands = cand_ref.shape[0] * PBLK
    first = jnp.concatenate([mask_ref[0, here, :], query_ref[here, :LANES]], axis=0)
    both = contract(first, cand_ref[:, :, :LANES].reshape(cands, LANES), 1, 1)
    yield both[:rows]
    dots = both[rows:]
    yield dots
    for low, high in bounds[2:]:
        dots = dots + contract(query_ref[here, low:high], cand_ref[:, :, low:high].reshape(cands, high - low), 1, 1)
        yield dots


def low_kernel(
    bounds, rows, slot_ref, shard_ref, query_ref, pool_ref, norm_ref, ids_ref, scale_ref, label_ref, mask_ref, after_ref,
    coef_ref, row_ref, col_ref, loss_ref, cand_ref, term_ref,
):
    del after_ref
    count = cand_ref.shape[0]
    levels, _, cands = coef_ref.shape
    blocks = loss_ref.shape[0]

    @pl.when(shard_ref[0] == 0)
    def _():
        row_ref[...] = jnp.zeros_like(row_ref)
        col_ref[...] = jnp.zeros_like(col_ref)

        def step(block, carry):
            here = pl.ds(block * rows, rows)
            take_blocks(pool_ref, slot_ref, block, count, cand_ref)
            pp = norm_rows(norm_ref, slot_ref, block, count)
            live = ids_ref[pl.ds(block, 1), :] >= 0.0
            labels = label_ref[here, :]
            entropy = jnp.zeros((rows, 1), F32)
            logit_sum = jnp.zeros((rows, cands), F32)
            row_terms, col_terms = [], []
            sums = prefix_dots(bounds, rows, block, query_ref, mask_ref, cand_ref)
            for level, ((low, high), dots) in enumerate(zip(bounds, sums)):
                scale = scale_ref[level, here, :]
                scale = jnp.concatenate([scale] * (cands // LANES), axis=1)
                coef, row, col, part, logits = terms(
                    dots, scale, pp[level : level + 1, :], live, labels, float(high // MINP)
                )
                term_ref[level] = coef
                row_terms.append(row)
                col_terms.append(col)
                entropy = entropy + part
                logit_sum = logit_sum + logits
            loss = entropy - jnp.sum(labels * logit_sum, axis=1, keepdims=True)
            coef = jnp.zeros((rows, cands), F32)
            row = jnp.zeros((rows, 1), F32)
            col = jnp.zeros((1, cands), F32)
            for level in reversed(range(levels)):
                coef = coef + term_ref[level]
                row = row + row_terms[level]
                col = col + col_terms[level]
                coef_ref[level, here, :] = coef
                row_ref[block, level : level + 1, :] = to_row(row)
                col_ref[block, level : level + 1, :] = col
            loss_ref[pl.ds(block, 1), :] = to_row(loss)
            return carry

        lax.fori_loop(0, blocks, step, 0)

    @pl.when(shard_ref[0] != 0)
    def _():
        loss_ref[...] = jnp.zeros_like(loss_ref)


def high_kernel(shards, per_shard, rows, weights, shard_ref, ids_ref, label_ref, *refs):
    ins, outs, loss_ref = refs[:shards], refs[shards:-1], refs[-1]
    shard = shard_ref[0]
    base = per_shard * rows
    width = ids_ref.shape[1]
    in_half = [
        jnp.where(lax.rem(shard - shift + shards, shards) < shards // 2, 1.0, 0.0)
        for shift in range(shards)
    ]

    def total(span, keep):
        pieces = [ref[span, :] * scale if keep else ref[span, :] for ref, scale in zip(ins, in_half)]
        return (pieces[0] + pieces[1]) + (pieces[2] + pieces[3])

    below = slice(base, base + AUX)
    half_rows, half_cols, full_rows, full_cols, losses, coefs = [], [], [], [], [], []
    aux_half, aux_full = total(below, True), total(below, False)
    for k in range(per_shard):
        block = shard * per_shard + k
        ids = ids_ref[pl.ds(block, 1), :]
        live = ids >= 0.0
        labels = label_ref[pl.ds(block * rows, rows), :]
        span = slice(k * rows, (k + 1) * rows)
        results = []
        for keep, aux, weight in ((True, aux_half, weights[0]), (False, aux_full, weights[1])):
            scale = to_col(lax.rsqrt(aux[per_shard : per_shard + 1, span] + EPS))
            results.append(terms(total(span, keep), scale, aux[k : k + 1, :], live, labels, weight))
        (coef_h, row_h, col_h, part_h, logit_h), (coef_f, row_f, col_f, part_f, logit_f) = results
        loss = part_h + part_f - jnp.sum(labels * (logit_h + logit_f), axis=1, keepdims=True)
        coefs.append(((coef_h + coef_f).astype(BF16), coef_f.astype(BF16)))
        half_rows.append(to_row(row_h + row_f))
        full_rows.append(to_row(row_f))
        half_cols.append(col_h + col_f)
        full_cols.append(col_f)
        losses.append(to_row(loss))
    loss_ref[...] = jnp.concatenate(losses, axis=1)

    def aux_rows(rows_list, cols_list):
        line = jnp.concatenate(rows_list + [jnp.zeros((1, width - base), F32)], axis=1)
        table = jnp.concatenate(cols_list + [line], axis=0)
        table = jnp.concatenate([table, jnp.zeros((AUX - table.shape[0], width), F32)], axis=0)
        first = table.astype(BF16).astype(F32)
        second = (table - first).astype(BF16).astype(F32)
        third = table - first - second
        return jnp.concatenate([first, second, third, jnp.zeros_like(table)], axis=0).astype(BF16)

    aux = (aux_rows(half_rows, half_cols), aux_rows(full_rows, full_cols))
    for shift in range(shards):
        out_ref = outs[shift]
        high_target = lax.rem(shard + shift, shards) >= shards // 2
        for which, chosen in ((1, high_target), (0, jnp.logical_not(high_target))):

            @pl.when(chosen)
            def _():
                for k in range(per_shard):
                    out_ref[k * rows : (k + 1) * rows, :] = coefs[k][which]
                out_ref[base : base + COEF_AUX, :] = aux[which]


def unpack_aux(ref, base):
    packed = ref[base : base + COEF_AUX, :].astype(F32)
    return packed[:AUX] + packed[AUX : 2 * AUX] + packed[2 * AUX : 3 * AUX]


def passage_kernel(
    bounds, shards, per_shard, rows, slot_ref, shard_ref, query_ref, pool_ref, mask_ref, low_col_ref, low_coef_ref, *refs
):
    ins = refs[:shards]
    out_hbm, half_hbm, coef_ref, col_ref, spread_ref, sum_ref, scale_ref, out_ref, half_ref, out_sem, half_sem = refs[shards:]
    shard = shard_ref[0]
    base = per_shard * rows
    blocks = shards * per_shard
    slots, _, width = pool_ref.shape
    cands = coef_ref.shape[1]
    count = cands // PBLK

    scale_ref[...] = jnp.zeros_like(scale_ref)
    for shift in range(shards):
        source = lax.rem(shard - shift + shards, shards)
        coef_ref[pl.ds(source * base, base), :] = ins[shift][:base, :]
        aux = unpack_aux(ins[shift], base)
        for k in range(per_shard):
            col_ref[source * per_shard + k] = aux[k : k + 1, :]

    def add_scales(block, low):
        cols = jnp.broadcast_to(col_ref[block], (8, cands))
        if low:
            cols = cols + low_col_ref[block]
        col_cols = columns(cols)
        for n in range(count):
            slot = slot_ref[block * count + n]
            scale_ref[slot] = scale_ref[slot] + col_cols[n * PBLK : (n + 1) * PBLK, :]

    def send(start, end):
        done = pl.ds(start, end - start)
        pltpu.make_async_copy(out_ref.at[:, :, done], out_hbm.at[:, :, done], out_sem).start()

    @pl.when(shard == 0)
    def _():
        sum_ref[...] = jnp.zeros_like(sum_ref)
        levels = len(bounds)

        def step(block, carry):
            here = pl.ds(block * rows, rows)
            add_scales(block, True)
            base_coef = coef_ref[here, :].astype(F32)
            coefs = [(base_coef + low_coef_ref[level, here, :]).astype(BF16) for level in range(levels)]
            for level in range(levels):
                half_ref[level, here, :] = coefs[level]
            grads = [contract(coefs[0], mask_ref[0, here, :], 0, 0) + contract(coefs[1], mask_ref[1, here, :], 0, 0)]
            starts = [0]
            for level in range(2, levels):
                lo, hi = bounds[level]
                grads.append(contract(coefs[level], query_ref[here, lo:hi], 0, 0))
                starts.append(lo)
            for n in range(count):
                slot = slot_ref[block * count + n]
                for start, grad in zip(starts, grads):
                    lanes = slice(start, start + grad.shape[1])
                    sum_ref[slot, :, lanes] = sum_ref[slot, :, lanes] + grad[n * PBLK : (n + 1) * PBLK, :]
            return carry

        lax.fori_loop(0, blocks, step, 0)
        copy = pltpu.make_async_copy(half_ref, half_hbm, half_sem)
        copy.start()
        first = lax.broadcasted_iota(jnp.int32, (1, LANES), 1) < bounds[0][1]
        step_slots = slots // CHUNKS
        for chunk in range(CHUNKS):
            part = pl.ds(chunk * step_slots, step_slots)

            def finish(i, carry):
                slot = chunk * step_slots + i
                scale = scale_ref[slot]
                wide = [jnp.where(first, scale[:, 0:1], scale[:, 1:2])]
                for level in range(2, levels):
                    lo, hi = bounds[level]
                    wide.append(jnp.broadcast_to(scale[:, level : level + 1], (PBLK, hi - lo)))
                pool = pool_ref[slot].astype(F32)
                out_ref[slot] = (sum_ref[slot] - jnp.concatenate(wide, axis=1) * pool).astype(BF16)
                return carry

            lax.fori_loop(0, step_slots, finish, 0, unroll=4)
            pltpu.make_async_copy(out_ref.at[part], out_hbm.at[part], out_sem).start()
        copy.wait()
        pltpu.make_async_copy(out_ref, out_hbm, out_sem).wait()

    @pl.when(shard != 0)
    def _():
        spread_ref[...] = jnp.zeros_like(spread_ref)
        for block in range(blocks):
            add_scales(block, False)
            turned = coef_ref[pl.ds(block * rows, rows), :].astype(F32).T.astype(BF16)
            for n in range(count):
                spread_ref[slot_ref[block * count + n], :, block * rows : (block + 1) * rows] = turned[
                    n * PBLK : (n + 1) * PBLK, :
                ]
        spread = spread_ref[0:slots].reshape(slots * PBLK, blocks * rows)
        scale = scale_ref[0:slots].reshape(slots * PBLK, LANES)[:, 0:1]
        for start in range(0, width, PIECE):
            end = start + PIECE
            grad = contract(spread, query_ref[:, start:end], 1, 0)
            pool = pool_ref[:, :, start:end].reshape(slots * PBLK, end - start).astype(F32)
            out_ref[:, :, start:end] = (grad - scale * pool).astype(BF16).reshape(slots, PBLK, end - start)
            send(start, end)
        pltpu.make_async_copy(out_ref, out_hbm, out_sem).wait()


def query_kernel(
    bounds, shards, per_shard, rows, loss_scale, slot_ref, shard_ref, query_ref, pool_ref, low_row_ref, low_loss_ref,
    high_loss_ref, low_half_hbm, *refs
):
    ins = refs[:shards]
    query_grad_ref, loss_ref = refs[shards : shards + 2]
    cand_ref, coef_ref, row_ref, low_half_ref, sem = refs[shards + 2 :]
    shard = shard_ref[0]
    base = per_shard * rows
    blocks = shards * per_shard
    count = cand_ref.shape[0]
    width = query_ref.shape[1]
    cands = coef_ref.shape[1]
    copy = pltpu.make_async_copy(low_half_hbm, low_half_ref, sem)

    @pl.when(shard == 0)
    def _():
        copy.start()

    for shift in range(shards):
        source = lax.rem(shard - shift + shards, shards)
        coef_ref[pl.ds(source * base, base), :] = ins[shift][:base, :]
        aux = unpack_aux(ins[shift], base)
        for k in range(per_shard):
            row_ref[source * per_shard + k] = aux[per_shard : per_shard + 1, k * rows : (k + 1) * rows]
    for block in range(blocks):
        j = block % per_shard
        loss_ref[block // per_shard : block // per_shard + 1, j * rows : (j + 1) * rows] = low_loss_ref[block : block + 1, :]
    loss_ref[pl.ds(shard, 1), :] = loss_ref[pl.ds(shard, 1), :] + high_loss_ref[...]
    loss_ref[...] = loss_ref[...] * loss_scale

    def run(spans, low):
        def step(block, carry):
            take_blocks(pool_ref, slot_ref, block, count, cand_ref)
            rows_here = jnp.broadcast_to(row_ref[block], (8, rows))
            if low:
                rows_here = rows_here + low_row_ref[block]
            row_cols = columns(rows_here)
            here = pl.ds(block * rows, rows)
            for level, (lo, hi) in enumerate(spans):
                coef = low_half_ref[level, here, :] if low else coef_ref[here, :]
                query = query_ref[here, lo:hi].astype(F32)
                cand = cand_ref[:, :, lo:hi].reshape(cands, hi - lo)
                grad = contract(coef, cand, 1, 0) - row_cols[:rows, level : level + 1] * query
                query_grad_ref[here, lo:hi] = grad.astype(BF16)
            return carry

        lax.fori_loop(0, blocks, step, 0)

    @pl.when(shard == 0)
    def _():
        copy.wait()
        run(bounds, True)

    @pl.when(shard != 0)
    def _():
        run([(0, width)], False)


def collect_kernel(target_ref, back_hbm, out_ref, back_ref, sem):
    rows = out_ref.shape[0]
    count = back_ref.shape[0]
    copy = pltpu.make_async_copy(back_hbm, back_ref, sem)
    copy.start()
    here = lax.broadcasted_iota(jnp.int32, (rows, count), 0)
    choose = jnp.where(here == target_ref[...], 1.0, 0.0).astype(BF16)
    copy.wait()
    out_ref[...] = contract(choose, back_ref[...], 1, 0).astype(BF16)


def per_device(queries, passages, neg_lists, positives):
    peers = lax.axis_size("dp")
    shards = lax.axis_size("tensor")
    total_rows, width = queries.shape
    blocks = neg_lists.shape[0] // peers
    count = neg_lists.shape[1]
    rows = total_rows // blocks
    local_blocks = passages.shape[0] // PBLK
    cands = count * PBLK
    per_shard = blocks // shards
    base = per_shard * rows
    slots = peers
    my_index = lax.axis_index("dp")
    shard = lax.axis_index("tensor")
    sizes = [MINP * 2**level for level in range(NPRE)]
    low_sizes = [size for size in sizes if size <= width]
    high_sizes = [size for size in sizes if size > width]
    assert high_sizes == [width * shards // 2, width * shards] and low_sizes[-1] == width
    assert shards == 4 and base == LANES
    bounds = list(zip([0] + low_sizes[:-1], low_sizes))
    levels = len(bounds)
    weight_total = sum(size / MINP for size in sizes)

    flat = neg_lists.reshape(peers, blocks * count)
    mine = (flat >= 0) & (flat // local_blocks == my_index)
    wanted = jnp.max(jnp.where(mine, flat % local_blocks, -1), axis=1)
    own = lax.dynamic_slice_in_dim(neg_lists, my_index * blocks, blocks, 0)
    valid = own >= 0
    slot = jnp.where(valid, own // local_blocks, 0).reshape(blocks * count)
    spare_slot = jnp.where(valid, own // local_blocks, slots).reshape(blocks * count)
    within = jnp.arange(PBLK, dtype=jnp.int32)
    ids = jnp.where(valid[:, :, None], own[:, :, None] * PBLK + within[None, None, :], -1)
    ids = ids.reshape(blocks, cands).astype(F32)
    target = jnp.where(wanted[:, None] >= 0, wanted[:, None] * PBLK + within[None, :], -1).reshape(1, slots * PBLK)
    pos = positives.reshape(blocks, rows).astype(F32)
    shard_arr = shard.reshape(1).astype(jnp.int32)
    pool_shape = (slots, PBLK, width)

    pinned = partial(pltpu.with_memory_space_constraint, memory_space=pltpu.HBM)
    panels = pl.pallas_call(
        pack_kernel,
        out_shape=pltpu.HBM(pool_shape, BF16),
        in_specs=[smem(), hbm()],
        out_specs=hbm(),
        scratch_shapes=[
            pltpu.VMEM((local_blocks, PBLK, width), BF16),
            pltpu.VMEM(pool_shape, BF16),
            pltpu.SemaphoreType.DMA(()),
            pltpu.SemaphoreType.DMA(()),
        ],
        compiler_params=params(),
        name="pack",
    )(wanted, pinned(passages.reshape(local_blocks, PBLK, width)))
    pool = lax.all_to_all(panels, "dp", split_axis=0, concat_axis=0, tiled=True)
    scales, full_norms, labels, masked = pl.pallas_call(
        partial(prep_kernel, bounds, rows),
        out_shape=[
            jax.ShapeDtypeStruct((levels, total_rows, LANES), F32),
            jax.ShapeDtypeStruct((blocks, 1, rows), F32),
            jax.ShapeDtypeStruct((total_rows, cands), F32),
            jax.ShapeDtypeStruct((2, total_rows, LANES), BF16),
        ],
        in_specs=[vmem()] * 3,
        out_specs=[vmem()] * 4,
        compiler_params=params(),
        name="prep",
    )(queries, ids, pos)

    def shift_by(part, s):
        return lax.ppermute(part, "tensor", [(i, (i + s) % shards) for i in range(shards)])

    cand_scratch = pltpu.VMEM((count, PBLK, width), BF16)
    message = jax.ShapeDtypeStruct((base + AUX, cands), F32)
    norm_shape = (slots, PBLK, LANES)
    norms, far, right, left = pl.pallas_call(
        partial(first_dots_kernel, bounds, shards, per_shard, rows, (2, 1, 3)),
        out_shape=[jax.ShapeDtypeStruct(norm_shape, F32)] + [message] * 3,
        in_specs=[smem(), smem(), vmem(), vmem(), vmem()],
        out_specs=[vmem()] * 4,
        scratch_shapes=[cand_scratch],
        compiler_params=params(),
        name="dots",
    )(slot, shard_arr, queries, pool, full_norms)
    (here,) = pl.pallas_call(
        partial(dots_kernel, shards, per_shard, rows, levels - 1, (0,)),
        out_shape=[message],
        in_specs=[smem(), smem()] + [vmem()] * 4,
        out_specs=[vmem()],
        scratch_shapes=[cand_scratch],
        compiler_params=params(),
        name="dots_own",
    )(slot, shard_arr, queries, pool, full_norms, norms)
    arrived = [here, shift_by(right, 1), shift_by(far, 2), shift_by(left, 3)]

    *coefs, high_loss = pl.pallas_call(
        partial(high_kernel, shards, per_shard, rows, [size / MINP for size in high_sizes]),
        out_shape=[jax.ShapeDtypeStruct((base + COEF_AUX, cands), BF16)] * shards
        + [jax.ShapeDtypeStruct((1, base), F32)],
        in_specs=[smem()] + [vmem()] * (2 + shards),
        out_specs=[vmem()] * (shards + 1),
        compiler_params=params(),
        name="high",
    )(shard_arr, ids, labels, *arrived)
    low_coef, low_row, low_col, low_loss = pl.pallas_call(
        partial(low_kernel, bounds, rows),
        out_shape=[
            jax.ShapeDtypeStruct((levels, total_rows, cands), F32),
            jax.ShapeDtypeStruct((blocks, 8, rows), F32),
            jax.ShapeDtypeStruct((blocks, 8, cands), F32),
            jax.ShapeDtypeStruct((blocks, rows), F32),
        ],
        in_specs=[smem(), smem()] + [vmem()] * 7 + [pl.BlockSpec(memory_space=pl.ANY)],
        out_specs=[vmem()] * 4,
        scratch_shapes=[cand_scratch, pltpu.VMEM((levels, rows, cands), F32)],
        compiler_params=params(),
        name="low",
    )(slot, shard_arr, queries, pool, norms, ids, scales, labels, masked, high_loss)
    coefs = [coefs[0]] + [shift_by(coefs[s], s) for s in range(1, shards)]

    half_shape = (levels, total_rows, cands)
    slot_grad, low_half = pl.pallas_call(
        partial(passage_kernel, bounds, shards, per_shard, rows),
        out_shape=[pltpu.HBM(pool_shape, BF16), pltpu.HBM(half_shape, BF16)],
        in_specs=[smem(), smem()] + [vmem()] * (5 + shards),
        out_specs=[hbm()] * 2,
        scratch_shapes=[
            pltpu.VMEM((total_rows, cands), BF16),
            pltpu.VMEM((blocks, 1, cands), F32),
            pltpu.VMEM((slots + 1, PBLK, total_rows), BF16),
            pltpu.VMEM((slots + 1, PBLK, width), F32),
            pltpu.VMEM((slots + 1, PBLK, LANES), F32),
            pltpu.VMEM(pool_shape, BF16),
            pltpu.VMEM(half_shape, BF16),
            pltpu.SemaphoreType.DMA(()),
            pltpu.SemaphoreType.DMA(()),
        ],
        compiler_params=params(),
        name="passage",
    )(spare_slot, shard_arr, queries, pool, masked, low_col, low_coef, *coefs)
    back = lax.all_to_all(slot_grad, "dp", split_axis=0, concat_axis=0, tiled=True)

    query_grad, loss = pl.pallas_call(
        partial(query_kernel, bounds, shards, per_shard, rows, 1.0 / weight_total),
        out_shape=[
            jax.ShapeDtypeStruct((total_rows, width), BF16),
            jax.ShapeDtypeStruct((shards, base), F32),
        ],
        in_specs=[smem(), smem()] + [vmem()] * 5 + [hbm()] + [vmem()] * shards,
        out_specs=[vmem()] * 2,
        scratch_shapes=[
            cand_scratch,
            pltpu.VMEM((total_rows, cands), BF16),
            pltpu.VMEM((blocks, 1, rows), F32),
            pltpu.VMEM(half_shape, BF16),
            pltpu.SemaphoreType.DMA(()),
        ],
        compiler_params=params(),
        name="query",
    )(slot, shard_arr, queries, pool, low_row, low_loss, high_loss, pinned(low_half), *coefs)
    loss = lax.psum(loss, "tensor")

    passage_grad = pl.pallas_call(
        collect_kernel,
        out_shape=jax.ShapeDtypeStruct((local_blocks * PBLK, width), BF16),
        in_specs=[vmem(), hbm()],
        out_specs=vmem(),
        scratch_shapes=[pltpu.VMEM((slots * PBLK, width), BF16), pltpu.SemaphoreType.DMA(())],
        compiler_params=params(),
        name="collect",
    )(target, pinned(back.reshape(slots * PBLK, width)))
    return (
        query_grad,
        passage_grad,
        loss.reshape(total_rows),
    )


def solution(mesh):
    return jax.shard_map(
        per_device,
        mesh=mesh,
        in_specs=(P("dp", "tensor"), P("dp", "tensor"), P(), P("dp")),
        out_specs=(P("dp", "tensor"), P("dp", "tensor"), P("dp")),
        check_vma=False,
    )
```

```python
from functools import partial

import jax
import jax.numpy as jnp
from jax import lax
from jax.experimental import pallas as pl
from jax.experimental.pallas import tpu as pltpu
from jax.sharding import PartitionSpec as P

MINP = 64
NPRE = 7
PBLK = 16

EPS = 1e-06
INV_TEMP = 20.0

F32 = jnp.float32
BF16 = jnp.bfloat16

AUX = 8
COEF_AUX = 32
LANES = 128
PIECE = 256
CHUNKS = 4


def vmem():
    return pl.BlockSpec(memory_space=pltpu.VMEM)


def smem():
    return pl.BlockSpec(memory_space=pltpu.SMEM)


def hbm():
    return pl.BlockSpec(memory_space=pltpu.HBM)


def params():
    return pltpu.CompilerParams(vmem_limit_bytes=20 * 2**20)


def contract(a, b, da, db):
    return lax.dot_general(a, b, (((da,), (db,)), ((), ())), preferred_element_type=F32)


def eye(n):
    return lax.broadcasted_iota(jnp.int32, (n, n), 0) == lax.broadcasted_iota(jnp.int32, (n, n), 1)


def to_col(row):
    return jnp.sum(jnp.where(eye(row.shape[1]), row, 0.0), axis=1, keepdims=True)


def to_row(col):
    return jnp.sum(jnp.where(eye(col.shape[0]), col, 0.0), axis=0, keepdims=True)


def square_sums(half):
    wide = half.astype(F32)
    return jnp.sum(wide * wide, axis=1, keepdims=True)


def columns(table):
    table = jnp.concatenate([table, jnp.zeros((8, LANES - table.shape[1]), F32)], axis=1) if table.shape[1] < LANES else table
    return jnp.concatenate([table, jnp.zeros((LANES - 8, table.shape[1]), F32)], axis=0).T


def terms(dots, a, pp_row, live, labels, weight):
    b = jnp.where(live, lax.rsqrt(pp_row + EPS), 0.0)
    scale = (a * INV_TEMP) * b
    logits = dots * scale
    exponent = jnp.where(live, jnp.exp(logits), 0.0)
    total = jnp.sum(exponent, axis=1, keepdims=True)
    gradient = weight * (exponent * (1.0 / total) - labels)
    inner = gradient * logits
    row = jnp.square(a[:, :1]) * jnp.sum(inner, axis=1, keepdims=True)
    col = (b * b) * jnp.sum(inner, axis=0, keepdims=True)
    return gradient * scale, row, col, weight * jnp.log(total), weight * logits


def take_blocks(pool_ref, slot_ref, block, count, out_ref):
    for n in range(count):
        out_ref[n] = pool_ref[slot_ref[block * count + n]]


def pool_norms(pool_ref, norm_ref, bounds):
    step_slots = 4
    rows = step_slots * PBLK
    lane = lax.broadcasted_iota(jnp.int32, (rows, LANES), 1)

    def lane_sum(part):
        return jnp.sum(part, axis=1, keepdims=True)

    def step(i, carry):
        here = pl.ds(i * step_slots, step_slots)
        wide = pool_ref[here].reshape(rows, pool_ref.shape[2]).astype(F32)
        square = wide * wide
        result, before, inside = None, None, None
        for level, (low, high) in enumerate(bounds):
            if high < LANES:
                total = lane_sum(jnp.where(lane < high, square[:, :LANES], 0.0))
            else:
                start = low // LANES * LANES
                parts = [square[:, j : j + LANES] for j in range(start, high, LANES)]
                while len(parts) > 1:
                    parts = [x + y for x, y in zip(parts[::2], parts[1::2])]
                total = lane_sum(parts[0])
                if start:
                    total = total + before
            before = total
            result = jnp.broadcast_to(total, (rows, LANES)) if result is None else jnp.where(lane == level, total, result)
        norm_ref[here] = result.reshape(step_slots, PBLK, LANES)
        return carry

    lax.fori_loop(0, pool_ref.shape[0] // step_slots, step, 0, unroll=4)


def norm_rows(norm_ref, slot_ref, block, count):
    table = jnp.concatenate([norm_ref[slot_ref[block * count + n]] for n in range(count)], axis=0)
    return table.T[:8, :]


def pack_kernel(wanted_ref, block_hbm, out_hbm, block_ref, out_ref, in_sem, out_sem):
    load = pltpu.make_async_copy(block_hbm, block_ref, in_sem)
    load.start()
    load.wait()
    size = out_ref.shape[0] // CHUNKS
    for chunk in range(CHUNKS):

        def step(i, carry):
            d = chunk * size + i
            out_ref[d] = block_ref[jnp.maximum(wanted_ref[d], 0)]
            return carry

        lax.fori_loop(0, size, step, 0, unroll=8)
        part = pl.ds(chunk * size, size)
        pltpu.make_async_copy(out_ref.at[part], out_hbm.at[part], out_sem).start()
    pltpu.make_async_copy(out_ref, out_hbm, out_sem).wait()


def prep_kernel(split, rows, query_ref, full_ref, mask_ref):
    lane = lax.broadcasted_iota(jnp.int32, (rows, LANES), 1)

    def step(block, carry):
        here = pl.ds(block * rows, rows)
        full_ref[block] = to_row(square_sums(query_ref[here, :]))
        first = query_ref[here, :LANES].astype(F32)
        mask_ref[0, here, :] = jnp.where(lane < split, first, 0.0).astype(BF16)
        mask_ref[1, here, :] = jnp.where(lane < split, 0.0, first).astype(BF16)
        return carry

    lax.fori_loop(0, full_ref.shape[0], step, 0)


def dots_kernel(
    shards, per_shard, rows, level, shifts, slot_ref, shard_ref, query_ref, pool_ref, full_ref, norm_ref, *refs
):
    outs, cand_ref = refs[:-1], refs[-1]
    count, _, width = cand_ref.shape
    shard = shard_ref[0]
    base = per_shard * rows
    for shift, out_ref in zip(shifts, outs):
        target = lax.rem(shard + shift, shards)
        for k in range(per_shard):
            block = target * per_shard + k
            take_blocks(pool_ref, slot_ref, block, count, cand_ref)
            query = query_ref[pl.ds(block * rows, rows), :]
            cand = cand_ref[...].reshape(count * PBLK, width)
            out_ref[k * rows : (k + 1) * rows, :] = contract(query, cand, 1, 1)
            out_ref[base + k : base + k + 1, :] = norm_rows(norm_ref, slot_ref, block, count)[level : level + 1, :]
            out_ref[base + per_shard : base + per_shard + 1, k * rows : (k + 1) * rows] = full_ref[block]


def first_dots_kernel(
    bounds, shards, per_shard, rows, shifts, slot_ref, shard_ref, query_ref, pool_ref, full_ref, norm_ref, *refs
):
    pool_norms(pool_ref, norm_ref, bounds)
    dots_kernel(
        shards, per_shard, rows, len(bounds) - 1, shifts, slot_ref, shard_ref, query_ref, pool_ref, full_ref, norm_ref, *refs
    )


def prefix_dots(bounds, rows, block, query_ref, cand_ref):
    here = pl.ds(block * rows, rows)
    cands = cand_ref.shape[0] * PBLK
    lane = lax.broadcasted_iota(jnp.int32, (rows, LANES), 1)
    first = query_ref[here, :LANES]
    short = jnp.where(lane < bounds[0][1], first.astype(F32), 0.0).astype(BF16)
    both = contract(
        jnp.concatenate([short, first], axis=0), cand_ref[:, :, :LANES].reshape(cands, LANES), 1, 1
    )
    yield both[:rows]
    dots = both[rows:]
    yield dots
    for low, high in bounds[2:]:
        dots = dots + contract(query_ref[here, low:high], cand_ref[:, :, low:high].reshape(cands, high - low), 1, 1)
        yield dots


def low_kernel(
    bounds, rows, slot_ref, shard_ref, query_ref, pool_ref, norm_ref, ids_ref, pos_ref,
    coef_hbm, row_hbm, col_hbm, loss_ref, cand_ref, term_ref, coef_ref, row_ref, col_ref, sem, row_sem, col_sem,
):
    count = cand_ref.shape[1]
    levels, _, cands = coef_ref.shape
    blocks = loss_ref.shape[0]

    @pl.when(shard_ref[0] == 0)
    def _():
        row_ref[...] = jnp.zeros_like(row_ref)
        col_ref[...] = jnp.zeros_like(col_ref)

        def one(block, cand_ref, term_ref):
            here = pl.ds(block * rows, rows)
            take_blocks(pool_ref, slot_ref, block, count, cand_ref)
            pp = norm_rows(norm_ref, slot_ref, block, count)
            ids = ids_ref[pl.ds(block, 1), :]
            live = ids >= 0.0
            labels = jnp.where(ids == to_col(pos_ref[pl.ds(block, 1), :]), 1.0, 0.0)
            qq = jnp.zeros((rows, 1), F32)
            entropy = jnp.zeros((rows, 1), F32)
            logit_sum = jnp.zeros((rows, cands), F32)
            row_terms, col_terms = [], []
            sums = prefix_dots(bounds, rows, block, query_ref, cand_ref)
            for level, ((low, high), dots) in enumerate(zip(bounds, sums)):
                qq = qq + square_sums(query_ref[here, low:high])
                coef, row, col, part, logits = terms(
                    dots, lax.rsqrt(qq + EPS), pp[level : level + 1, :], live, labels, float(high // MINP)
                )
                term_ref[level] = coef
                row_terms.append(row)
                col_terms.append(col)
                entropy = entropy + part
                logit_sum = logit_sum + logits
            loss = entropy - jnp.sum(labels * logit_sum, axis=1, keepdims=True)
            coef = jnp.zeros((rows, cands), F32)
            row = jnp.zeros((rows, 1), F32)
            col = jnp.zeros((1, cands), F32)
            for level in reversed(range(levels)):
                coef = coef + term_ref[level]
                row = row + row_terms[level]
                col = col + col_terms[level]
                coef_ref[level, here, :] = coef
                row_ref[block, level : level + 1, :] = to_row(row)
                col_ref[block, level : level + 1, :] = col
            loss_ref[pl.ds(block, 1), :] = to_row(loss)

        def step(pair, carry):
            for j in range(2):
                one(pair * 2 + j, cand_ref.at[j], term_ref.at[j])
            here = pl.ds(pair * 2 * rows, 2 * rows)
            pltpu.make_async_copy(coef_ref.at[:, here], coef_hbm.at[:, here], sem).start()
            return carry

        lax.fori_loop(0, blocks // 2, step, 0)
        copies = [
            pltpu.make_async_copy(row_ref, row_hbm, row_sem),
            pltpu.make_async_copy(col_ref, col_hbm, col_sem),
        ]
        for copy in copies:
            copy.start()
        for copy in copies:
            copy.wait()
        pltpu.make_async_copy(coef_ref, coef_hbm, sem).wait()

    @pl.when(shard_ref[0] != 0)
    def _():
        loss_ref[...] = jnp.zeros_like(loss_ref)


def high_kernel(shards, per_shard, rows, weights, shard_ref, ids_ref, pos_ref, after_ref, *refs):
    del after_ref
    ins, outs, loss_ref = refs[:shards], refs[shards:-1], refs[-1]
    shard = shard_ref[0]
    base = per_shard * rows
    width = ids_ref.shape[1]
    in_half = [
        jnp.where(lax.rem(shard - shift + shards, shards) < shards // 2, 1.0, 0.0)
        for shift in range(shards)
    ]

    def total(span, keep):
        pieces = [ref[span, :] * scale if keep else ref[span, :] for ref, scale in zip(ins, in_half)]
        return (pieces[0] + pieces[1]) + (pieces[2] + pieces[3])

    below = slice(base, base + AUX)
    half_rows, half_cols, full_rows, full_cols, losses, coefs = [], [], [], [], [], []
    aux_half, aux_full = total(below, True), total(below, False)
    for k in range(per_shard):
        block = shard * per_shard + k
        ids = ids_ref[pl.ds(block, 1), :]
        live = ids >= 0.0
        labels = jnp.where(ids == to_col(pos_ref[pl.ds(block, 1), :]), 1.0, 0.0)
        span = slice(k * rows, (k + 1) * rows)
        results = []
        for keep, aux, weight in ((True, aux_half, weights[0]), (False, aux_full, weights[1])):
            scale = to_col(lax.rsqrt(aux[per_shard : per_shard + 1, span] + EPS))
            results.append(terms(total(span, keep), scale, aux[k : k + 1, :], live, labels, weight))
        (coef_h, row_h, col_h, part_h, logit_h), (coef_f, row_f, col_f, part_f, logit_f) = results
        loss = part_h + part_f - jnp.sum(labels * (logit_h + logit_f), axis=1, keepdims=True)
        coefs.append(((coef_h + coef_f).astype(BF16), coef_f.astype(BF16)))
        half_rows.append(to_row(row_h + row_f))
        full_rows.append(to_row(row_f))
        half_cols.append(col_h + col_f)
        full_cols.append(col_f)
        losses.append(to_row(loss))
    loss_ref[...] = jnp.concatenate(losses, axis=1)

    def aux_rows(rows_list, cols_list):
        line = jnp.concatenate(rows_list + [jnp.zeros((1, width - base), F32)], axis=1)
        table = jnp.concatenate(cols_list + [line], axis=0)
        table = jnp.concatenate([table, jnp.zeros((AUX - table.shape[0], width), F32)], axis=0)
        first = table.astype(BF16).astype(F32)
        second = (table - first).astype(BF16).astype(F32)
        third = table - first - second
        return jnp.concatenate([first, second, third, jnp.zeros_like(table)], axis=0).astype(BF16)

    aux = (aux_rows(half_rows, half_cols), aux_rows(full_rows, full_cols))
    for shift in range(shards):
        out_ref = outs[shift]
        high_target = lax.rem(shard + shift, shards) >= shards // 2
        for which, chosen in ((1, high_target), (0, jnp.logical_not(high_target))):

            @pl.when(chosen)
            def _():
                for k in range(per_shard):
                    out_ref[k * rows : (k + 1) * rows, :] = coefs[k][which]
                out_ref[base : base + COEF_AUX, :] = aux[which]


def unpack_aux(ref, base):
    packed = ref[base : base + COEF_AUX, :].astype(F32)
    return packed[:AUX] + packed[AUX : 2 * AUX] + packed[2 * AUX : 3 * AUX]


def passage_kernel(
    bounds, shards, per_shard, rows, slot_ref, shard_ref, query_ref, pool_ref, mask_ref, low_row_hbm, low_col_hbm,
    low_coef_hbm, *refs
):
    ins = refs[:shards]
    out_hbm, half_hbm, row_hbm, coef_ref, row_ref, col_ref, spread_ref, sum_ref, scale_ref, out_ref, half_ref = refs[shards:-7]
    low_row_ref, low_col_ref, low_coef_ref, out_sem, half_sem, row_sem, low_sem = refs[-7:]
    shard = shard_ref[0]
    base = per_shard * rows
    blocks = shards * per_shard
    slots, _, width = pool_ref.shape
    cands = coef_ref.shape[1]
    count = cands // PBLK

    loads = [
        pltpu.make_async_copy(low_row_hbm, low_row_ref, low_sem.at[0]),
        pltpu.make_async_copy(low_col_hbm, low_col_ref, low_sem.at[1]),
        pltpu.make_async_copy(low_coef_hbm, low_coef_ref, low_sem.at[2]),
    ]
    row_copy = pltpu.make_async_copy(row_ref, row_hbm, row_sem)

    @pl.when(shard == 0)
    def _():
        for load in loads:
            load.start()
        sum_ref[...] = jnp.zeros_like(sum_ref)

    scale_ref[...] = jnp.zeros_like(scale_ref)
    for shift in range(shards):
        source = lax.rem(shard - shift + shards, shards)
        coef_ref[pl.ds(source * base, base), :] = ins[shift][:base, :]
        aux = unpack_aux(ins[shift], base)
        for k in range(per_shard):
            col_ref[source * per_shard + k] = aux[k : k + 1, :]
            line = aux[per_shard : per_shard + 1, k * rows : (k + 1) * rows]
            row_ref[source * per_shard + k] = jnp.broadcast_to(line, (8, rows))

    def add_scales(block, low):
        cols = jnp.broadcast_to(col_ref[block], (8, cands))
        if low:
            cols = cols + low_col_ref[block]
        col_cols = columns(cols)
        for n in range(count):
            slot = slot_ref[block * count + n]
            scale_ref[slot] = scale_ref[slot] + col_cols[n * PBLK : (n + 1) * PBLK, :]

    def send(start, end):
        done = pl.ds(start, end - start)
        pltpu.make_async_copy(out_ref.at[:, :, done], out_hbm.at[:, :, done], out_sem).start()

    @pl.when(shard == 0)
    def _():
        levels = len(bounds)
        for load in loads:
            load.wait()
        row_ref[...] = row_ref[...] + low_row_ref[...]
        row_copy.start()

        def one(block):
            here = pl.ds(block * rows, rows)
            add_scales(block, True)
            base_coef = coef_ref[here, :].astype(F32)
            coefs = [(base_coef + low_coef_ref[level, here, :]).astype(BF16) for level in range(levels)]
            for level in range(levels):
                half_ref[level, here, :] = coefs[level]
            grads = [contract(coefs[0], mask_ref[0, here, :], 0, 0) + contract(coefs[1], mask_ref[1, here, :], 0, 0)]
            starts = [0]
            for level in range(2, levels):
                lo, hi = bounds[level]
                grads.append(contract(coefs[level], query_ref[here, lo:hi], 0, 0))
                starts.append(lo)
            for n in range(count):
                slot = slot_ref[block * count + n]
                for start, grad in zip(starts, grads):
                    lanes = slice(start, start + grad.shape[1])
                    sum_ref[slot, :, lanes] = sum_ref[slot, :, lanes] + grad[n * PBLK : (n + 1) * PBLK, :]

        def step(pair, carry):
            for j in range(2):
                one(pair * 2 + j)
            return carry

        lax.fori_loop(0, blocks // 2, step, 0)
        copy = pltpu.make_async_copy(half_ref, half_hbm, half_sem)
        copy.start()
        first = lax.broadcasted_iota(jnp.int32, (1, LANES), 1) < bounds[0][1]
        step_slots = slots // CHUNKS
        for chunk in range(CHUNKS):
            part = pl.ds(chunk * step_slots, step_slots)

            def finish(i, carry):
                slot = chunk * step_slots + i
                scale = scale_ref[slot]
                wide = [jnp.where(first, scale[:, 0:1], scale[:, 1:2])]
                for level in range(2, levels):
                    lo, hi = bounds[level]
                    wide.append(jnp.broadcast_to(scale[:, level : level + 1], (PBLK, hi - lo)))
                pool = pool_ref[slot].astype(F32)
                out_ref[slot] = (sum_ref[slot] - jnp.concatenate(wide, axis=1) * pool).astype(BF16)
                return carry

            lax.fori_loop(0, step_slots, finish, 0, unroll=4)
            pltpu.make_async_copy(out_ref.at[part], out_hbm.at[part], out_sem).start()
        copy.wait()
        row_copy.wait()
        pltpu.make_async_copy(out_ref, out_hbm, out_sem).wait()

    @pl.when(shard != 0)
    def _():
        row_copy.start()
        copy = pltpu.make_async_copy(coef_ref, half_hbm.at[0], half_sem)
        copy.start()
        spread_ref[...] = jnp.zeros_like(spread_ref)
        for block in range(blocks):
            add_scales(block, False)
            turned = coef_ref[pl.ds(block * rows, rows), :].astype(F32).T.astype(BF16)
            for n in range(count):
                spread_ref[slot_ref[block * count + n], :, block * rows : (block + 1) * rows] = turned[
                    n * PBLK : (n + 1) * PBLK, :
                ]
        spread = spread_ref[0:slots].reshape(slots * PBLK, blocks * rows)
        scale = scale_ref[0:slots].reshape(slots * PBLK, LANES)[:, 0:1]
        for start in range(0, width, PIECE):
            end = start + PIECE
            grad = contract(spread, query_ref[:, start:end], 1, 0)
            pool = pool_ref[:, :, start:end].reshape(slots * PBLK, end - start).astype(F32)
            out_ref[:, :, start:end] = (grad - scale * pool).astype(BF16).reshape(slots, PBLK, end - start)
            send(start, end)
        copy.wait()
        row_copy.wait()
        pltpu.make_async_copy(out_ref, out_hbm, out_sem).wait()


def query_kernel(
    bounds, rows, loss_scale, slot_ref, shard_ref, query_ref, pool_ref, row_ref, low_loss_ref, high_loss_ref, half_hbm,
    query_grad_ref, loss_ref, cand_ref, half_ref, sem,
):
    shard = shard_ref[0]
    blocks, cands = low_loss_ref.shape[0], half_ref.shape[2]
    count = cand_ref.shape[0]
    width = query_ref.shape[1]
    per_line = LANES // rows
    first = pltpu.make_async_copy(half_hbm.at[0], half_ref.at[0], sem.at[0])
    rest = pl.ds(1, half_ref.shape[0] - 1)
    others = pltpu.make_async_copy(half_hbm.at[rest], half_ref.at[rest], sem.at[1])
    first.start()

    @pl.when(shard == 0)
    def _():
        others.start()

    for block in range(blocks):
        j = block % per_line
        loss_ref[block // per_line : block // per_line + 1, j * rows : (j + 1) * rows] = low_loss_ref[block : block + 1, :]
    loss_ref[pl.ds(shard, 1), :] = loss_ref[pl.ds(shard, 1), :] + high_loss_ref[...]
    loss_ref[...] = loss_ref[...] * loss_scale

    def run(spans):
        def step(block, carry):
            take_blocks(pool_ref, slot_ref, block, count, cand_ref)
            row_cols = columns(row_ref[block])
            here = pl.ds(block * rows, rows)
            for level, (lo, hi) in enumerate(spans):
                query = query_ref[here, lo:hi].astype(F32)
                cand = cand_ref[:, :, lo:hi].reshape(cands, hi - lo)
                grad = contract(half_ref[level, here, :], cand, 1, 0) - row_cols[:rows, level : level + 1] * query
                query_grad_ref[here, lo:hi] = grad.astype(BF16)
            return carry

        lax.fori_loop(0, blocks, step, 0)

    first.wait()

    @pl.when(shard == 0)
    def _():
        others.wait()
        run(bounds)

    @pl.when(shard != 0)
    def _():
        run([(0, width)])


def collect_kernel(target_ref, back_hbm, out_ref, back_ref, sem):
    rows = out_ref.shape[0]
    count = back_ref.shape[0]
    copy = pltpu.make_async_copy(back_hbm, back_ref, sem)
    copy.start()
    here = lax.broadcasted_iota(jnp.int32, (rows, count), 0)
    choose = jnp.where(here == target_ref[...], 1.0, 0.0).astype(BF16)
    copy.wait()
    out_ref[...] = contract(choose, back_ref[...], 1, 0).astype(BF16)


def per_device(queries, passages, neg_lists, positives):
    peers = lax.axis_size("dp")
    shards = lax.axis_size("tensor")
    total_rows, width = queries.shape
    blocks = neg_lists.shape[0] // peers
    count = neg_lists.shape[1]
    rows = total_rows // blocks
    local_blocks = passages.shape[0] // PBLK
    cands = count * PBLK
    per_shard = blocks // shards
    base = per_shard * rows
    slots = peers
    my_index = lax.axis_index("dp")
    shard = lax.axis_index("tensor")
    sizes = [MINP * 2**level for level in range(NPRE)]
    low_sizes = [size for size in sizes if size <= width]
    high_sizes = [size for size in sizes if size > width]
    assert high_sizes == [width * shards // 2, width * shards] and low_sizes[-1] == width
    assert shards == 4 and base == LANES
    bounds = list(zip([0] + low_sizes[:-1], low_sizes))
    levels = len(bounds)
    weight_total = sum(size / MINP for size in sizes)

    flat = neg_lists.reshape(peers, blocks * count)
    mine = (flat >= 0) & (flat // local_blocks == my_index)
    wanted = jnp.max(jnp.where(mine, flat % local_blocks, -1), axis=1)
    own = lax.dynamic_slice_in_dim(neg_lists, my_index * blocks, blocks, 0)
    valid = own >= 0
    slot = jnp.where(valid, own // local_blocks, 0).reshape(blocks * count)
    spare_slot = jnp.where(valid, own // local_blocks, slots).reshape(blocks * count)
    within = jnp.arange(PBLK, dtype=jnp.int32)
    ids = jnp.where(valid[:, :, None], own[:, :, None] * PBLK + within[None, None, :], -1)
    ids = ids.reshape(blocks, cands).astype(F32)
    target = jnp.where(wanted[:, None] >= 0, wanted[:, None] * PBLK + within[None, :], -1).reshape(1, slots * PBLK)
    pos = positives.reshape(blocks, rows).astype(F32)
    shard_arr = shard.reshape(1).astype(jnp.int32)
    pool_shape = (slots, PBLK, width)

    pinned = partial(pltpu.with_memory_space_constraint, memory_space=pltpu.HBM)
    panels = pl.pallas_call(
        pack_kernel,
        out_shape=pltpu.HBM(pool_shape, BF16),
        in_specs=[smem(), hbm()],
        out_specs=hbm(),
        scratch_shapes=[
            pltpu.VMEM((local_blocks, PBLK, width), BF16),
            pltpu.VMEM(pool_shape, BF16),
            pltpu.SemaphoreType.DMA(()),
            pltpu.SemaphoreType.DMA(()),
        ],
        compiler_params=params(),
        name="pack",
    )(wanted, pinned(passages.reshape(local_blocks, PBLK, width)))
    pool = lax.all_to_all(panels, "dp", split_axis=0, concat_axis=0, tiled=True)
    full_norms, masked = pl.pallas_call(
        partial(prep_kernel, bounds[0][1], rows),
        out_shape=[
            jax.ShapeDtypeStruct((blocks, 1, rows), F32),
            jax.ShapeDtypeStruct((2, total_rows, LANES), BF16),
        ],
        in_specs=[vmem()],
        out_specs=[vmem()] * 2,
        compiler_params=params(),
        name="prep",
    )(queries)

    def shift_by(part, s):
        return lax.ppermute(part, "tensor", [(i, (i + s) % shards) for i in range(shards)])

    cand_scratch = pltpu.VMEM((count, PBLK, width), BF16)
    message = jax.ShapeDtypeStruct((base + AUX, cands), F32)
    norm_shape = (slots, PBLK, LANES)
    norms, far, right, left = pl.pallas_call(
        partial(first_dots_kernel, bounds, shards, per_shard, rows, (2, 1, 3)),
        out_shape=[jax.ShapeDtypeStruct(norm_shape, F32)] + [message] * 3,
        in_specs=[smem(), smem(), vmem(), vmem(), vmem()],
        out_specs=[vmem()] * 4,
        scratch_shapes=[cand_scratch],
        compiler_params=params(),
        name="dots",
    )(slot, shard_arr, queries, pool, full_norms)
    (here,) = pl.pallas_call(
        partial(dots_kernel, shards, per_shard, rows, levels - 1, (0,)),
        out_shape=[message],
        in_specs=[smem(), smem()] + [vmem()] * 4,
        out_specs=[vmem()],
        scratch_shapes=[cand_scratch],
        compiler_params=params(),
        name="dots_own",
    )(slot, shard_arr, queries, pool, full_norms, norms)
    arrived = [here, shift_by(right, 1), shift_by(far, 2), shift_by(left, 3)]

    low_coef, low_row, low_col, low_loss = pl.pallas_call(
        partial(low_kernel, bounds, rows),
        out_shape=[
            pltpu.HBM((levels, total_rows, cands), F32),
            pltpu.HBM((blocks, 8, rows), F32),
            pltpu.HBM((blocks, 8, cands), F32),
            jax.ShapeDtypeStruct((blocks, rows), F32),
        ],
        in_specs=[smem(), smem()] + [vmem()] * 5,
        out_specs=[hbm()] * 3 + [vmem()],
        scratch_shapes=[
            pltpu.VMEM((2, count, PBLK, width), BF16),
            pltpu.VMEM((2, levels, rows, cands), F32),
            pltpu.VMEM((levels, total_rows, cands), F32),
            pltpu.VMEM((blocks, 8, rows), F32),
            pltpu.VMEM((blocks, 8, cands), F32),
            pltpu.SemaphoreType.DMA(()),
            pltpu.SemaphoreType.DMA(()),
            pltpu.SemaphoreType.DMA(()),
        ],
        compiler_params=params(),
        name="low",
    )(slot, shard_arr, queries, pool, norms, ids, pos)
    *coefs, high_loss = pl.pallas_call(
        partial(high_kernel, shards, per_shard, rows, [size / MINP for size in high_sizes]),
        out_shape=[jax.ShapeDtypeStruct((base + COEF_AUX, cands), BF16)] * shards
        + [jax.ShapeDtypeStruct((1, base), F32)],
        in_specs=[smem()] + [vmem()] * 2 + [hbm()] + [vmem()] * shards,
        out_specs=[vmem()] * (shards + 1),
        compiler_params=params(),
        name="high",
    )(shard_arr, ids, pos, pinned(low_row), *arrived)
    coefs = [coefs[0]] + [shift_by(coefs[s], s) for s in range(1, shards)]

    half_shape = (levels, total_rows, cands)
    slot_grad, half, row_table = pl.pallas_call(
        partial(passage_kernel, bounds, shards, per_shard, rows),
        out_shape=[pltpu.HBM(pool_shape, BF16), pltpu.HBM(half_shape, BF16), pltpu.HBM((blocks, 8, rows), F32)],
        in_specs=[smem(), smem()] + [vmem()] * 3 + [hbm()] * 3 + [vmem()] * shards,
        out_specs=[hbm()] * 3,
        scratch_shapes=[
            pltpu.VMEM((total_rows, cands), BF16),
            pltpu.VMEM((blocks, 8, rows), F32),
            pltpu.VMEM((blocks, 1, cands), F32),
            pltpu.VMEM((slots + 1, PBLK, total_rows), BF16),
            pltpu.VMEM((slots + 1, PBLK, width), F32),
            pltpu.VMEM((slots + 1, PBLK, LANES), F32),
            pltpu.VMEM(pool_shape, BF16),
            pltpu.VMEM(half_shape, BF16),
            pltpu.VMEM((blocks, 8, rows), F32),
            pltpu.VMEM((blocks, 8, cands), F32),
            pltpu.VMEM((levels, total_rows, cands), F32),
            pltpu.SemaphoreType.DMA(()),
            pltpu.SemaphoreType.DMA(()),
            pltpu.SemaphoreType.DMA(()),
            pltpu.SemaphoreType.DMA((3,)),
        ],
        compiler_params=params(),
        name="passage",
    )(
        spare_slot, shard_arr, queries, pool, masked,
        pinned(low_row), pinned(low_col), pinned(low_coef), *coefs,
    )
    back = lax.all_to_all(slot_grad, "dp", split_axis=0, concat_axis=0, tiled=True)

    query_grad, loss = pl.pallas_call(
        partial(query_kernel, bounds, rows, 1.0 / weight_total),
        out_shape=[
            jax.ShapeDtypeStruct((total_rows, width), BF16),
            jax.ShapeDtypeStruct((shards, base), F32),
        ],
        in_specs=[smem(), smem()] + [vmem()] * 5 + [hbm()],
        out_specs=[vmem()] * 2,
        scratch_shapes=[cand_scratch, pltpu.VMEM(half_shape, BF16), pltpu.SemaphoreType.DMA((2,))],
        compiler_params=params(),
        name="query",
    )(slot, shard_arr, queries, pool, row_table, low_loss, high_loss, pinned(half))
    loss = lax.psum(loss, "tensor")

    passage_grad = pl.pallas_call(
        collect_kernel,
        out_shape=jax.ShapeDtypeStruct((local_blocks * PBLK, width), BF16),
        in_specs=[vmem(), hbm()],
        out_specs=vmem(),
        scratch_shapes=[pltpu.VMEM((slots * PBLK, width), BF16), pltpu.SemaphoreType.DMA(())],
        compiler_params=params(),
        name="collect",
    )(target, pinned(back.reshape(slots * PBLK, width)))
    return (
        query_grad,
        passage_grad,
        loss.reshape(total_rows),
    )


def solution(mesh):
    return jax.shard_map(
        per_device,
        mesh=mesh,
        in_specs=(P("dp", "tensor"), P("dp", "tensor"), P(), P("dp")),
        out_specs=(P("dp", "tensor"), P("dp", "tensor"), P("dp")),
        check_vma=False,
    )
```

```python
from functools import partial

import jax
import jax.numpy as jnp
from jax import lax
from jax.experimental import pallas as pl
from jax.experimental.pallas import tpu as pltpu
from jax.sharding import PartitionSpec as P

MINP = 64
NPRE = 7
PBLK = 16

EPS = 1e-06
INV_TEMP = 20.0

F32 = jnp.float32
BF16 = jnp.bfloat16

AUX = 8
COEF_AUX = 32
LANES = 128
PIECE = 256
CHUNKS = 4


def vmem():
    return pl.BlockSpec(memory_space=pltpu.VMEM)


def smem():
    return pl.BlockSpec(memory_space=pltpu.SMEM)


def hbm():
    return pl.BlockSpec(memory_space=pltpu.HBM)


def params():
    return pltpu.CompilerParams(vmem_limit_bytes=20 * 2**20)


def contract(a, b, da, db):
    return lax.dot_general(a, b, (((da,), (db,)), ((), ())), preferred_element_type=F32)


def eye(n):
    return lax.broadcasted_iota(jnp.int32, (n, n), 0) == lax.broadcasted_iota(jnp.int32, (n, n), 1)


def to_col(row):
    return jnp.sum(jnp.where(eye(row.shape[1]), row, 0.0), axis=1, keepdims=True)


def to_row(col):
    return jnp.sum(jnp.where(eye(col.shape[0]), col, 0.0), axis=0, keepdims=True)


def square_sums(half):
    wide = half.astype(F32)
    return jnp.sum(wide * wide, axis=1, keepdims=True)


def columns(table):
    table = jnp.concatenate([table, jnp.zeros((8, LANES - table.shape[1]), F32)], axis=1) if table.shape[1] < LANES else table
    return jnp.concatenate([table, jnp.zeros((LANES - 8, table.shape[1]), F32)], axis=0).T


def terms(dots, a, pp_row, live, labels, weight):
    b = jnp.where(live, lax.rsqrt(pp_row + EPS), 0.0)
    scale = (a * INV_TEMP) * b
    logits = dots * scale
    exponent = jnp.where(live, jnp.exp(logits), 0.0)
    total = jnp.sum(exponent, axis=1, keepdims=True)
    gradient = weight * (exponent * (1.0 / total) - labels)
    inner = gradient * logits
    row = jnp.square(a[:, :1]) * jnp.sum(inner, axis=1, keepdims=True)
    col = (b * b) * jnp.sum(inner, axis=0, keepdims=True)
    return gradient * scale, row, col, weight * jnp.log(total), weight * logits


def take_blocks(pool_ref, slot_ref, block, count, out_ref):
    for n in range(count):
        out_ref[n] = pool_ref[slot_ref[block * count + n]]


def pool_norms(pool_ref, norm_ref, bounds):
    step_slots = 4
    rows = step_slots * PBLK
    lane = lax.broadcasted_iota(jnp.int32, (rows, LANES), 1)

    def lane_sum(part):
        return jnp.sum(part, axis=1, keepdims=True)

    def step(i, carry):
        here = pl.ds(i * step_slots, step_slots)
        wide = pool_ref[here].reshape(rows, pool_ref.shape[2]).astype(F32)
        square = wide * wide
        result, before, inside = None, None, None
        for level, (low, high) in enumerate(bounds):
            if high < LANES:
                total = lane_sum(jnp.where(lane < high, square[:, :LANES], 0.0))
            else:
                start = low // LANES * LANES
                parts = [square[:, j : j + LANES] for j in range(start, high, LANES)]
                while len(parts) > 1:
                    parts = [x + y for x, y in zip(parts[::2], parts[1::2])]
                total = lane_sum(parts[0])
                if start:
                    total = total + before
            before = total
            result = jnp.broadcast_to(total, (rows, LANES)) if result is None else jnp.where(lane == level, total, result)
        norm_ref[here] = result.reshape(step_slots, PBLK, LANES)
        return carry

    lax.fori_loop(0, pool_ref.shape[0] // step_slots, step, 0, unroll=4)


def norm_rows(norm_ref, slot_ref, block, count):
    table = jnp.concatenate([norm_ref[slot_ref[block * count + n]] for n in range(count)], axis=0)
    return table.T[:8, :]


def pack_kernel(
    first_ref, lists_hbm, block_hbm, out_hbm, lists_ref, block_ref, out_ref, row_ref, wanted_ref, lists_sem, in_sem, row_sem, out_sem
):
    load = pltpu.make_async_copy(block_hbm, block_ref, in_sem)
    lists = pltpu.make_async_copy(lists_hbm, lists_ref, lists_sem)
    lists.start()
    load.start()
    lists.wait()
    local = lists_ref[...] - first_ref[0]
    local = jnp.where((local >= 0) & (local < block_ref.shape[0]), local, 0).astype(F32)
    row = jnp.broadcast_to(jnp.max(local, axis=0, keepdims=True), row_ref.shape)
    size = row.shape[1]
    step = 1
    while step < size // out_ref.shape[0]:
        row = jnp.maximum(row, pltpu.roll(row, size - step, 1))
        step *= 2
    row_ref[...] = row.astype(jnp.int32)
    save = pltpu.make_async_copy(row_ref, wanted_ref, row_sem)
    save.start()
    save.wait()
    load.wait()
    share = size // out_ref.shape[0]
    part_size = out_ref.shape[0] // CHUNKS
    for chunk in range(CHUNKS):

        def one(i, carry):
            d = chunk * part_size + i
            out_ref[d] = block_ref[wanted_ref[0, d * share]]
            return carry

        lax.fori_loop(0, part_size, one, 0, unroll=8)
        part = pl.ds(chunk * part_size, part_size)
        pltpu.make_async_copy(out_ref.at[part], out_hbm.at[part], out_sem).start()
    pltpu.make_async_copy(out_ref, out_hbm, out_sem).wait()


def prep_kernel(split, rows, query_ref, full_ref, mask_ref):
    lane = lax.broadcasted_iota(jnp.int32, (rows, LANES), 1)

    def step(block, carry):
        here = pl.ds(block * rows, rows)
        full_ref[block] = to_row(square_sums(query_ref[here, :]))
        first = query_ref[here, :LANES].astype(F32)
        mask_ref[0, here, :] = jnp.where(lane < split, first, 0.0).astype(BF16)
        mask_ref[1, here, :] = jnp.where(lane < split, 0.0, first).astype(BF16)
        return carry

    lax.fori_loop(0, full_ref.shape[0], step, 0)


def dots_kernel(
    shards, per_shard, rows, level, shifts, slot_ref, shard_ref, query_ref, pool_ref, full_ref, norm_ref, *refs
):
    outs, cand_ref = refs[:-1], refs[-1]
    count, _, width = cand_ref.shape
    shard = shard_ref[0]
    base = per_shard * rows
    for shift, out_ref in zip(shifts, outs):
        target = lax.rem(shard + shift, shards)
        for k in range(per_shard):
            block = target * per_shard + k
            take_blocks(pool_ref, slot_ref, block, count, cand_ref)
            query = query_ref[pl.ds(block * rows, rows), :]
            cand = cand_ref[...].reshape(count * PBLK, width)
            out_ref[k * rows : (k + 1) * rows, :] = contract(query, cand, 1, 1)
            out_ref[base + k : base + k + 1, :] = norm_rows(norm_ref, slot_ref, block, count)[level : level + 1, :]
            out_ref[base + per_shard : base + per_shard + 1, k * rows : (k + 1) * rows] = full_ref[block]


def first_dots_kernel(
    bounds, shards, per_shard, rows, shifts, slot_ref, shard_ref, query_ref, pool_ref, full_ref, norm_ref, *refs
):
    pool_norms(pool_ref, norm_ref, bounds)
    dots_kernel(
        shards, per_shard, rows, len(bounds) - 1, shifts, slot_ref, shard_ref, query_ref, pool_ref, full_ref, norm_ref, *refs
    )


def prefix_dots(bounds, rows, block, query_ref, cand_ref):
    here = pl.ds(block * rows, rows)
    cands = cand_ref.shape[0] * PBLK
    lane = lax.broadcasted_iota(jnp.int32, (rows, LANES), 1)
    first = query_ref[here, :LANES]
    short = jnp.where(lane < bounds[0][1], first.astype(F32), 0.0).astype(BF16)
    both = contract(
        jnp.concatenate([short, first], axis=0), cand_ref[:, :, :LANES].reshape(cands, LANES), 1, 1
    )
    yield both[:rows]
    dots = both[rows:]
    yield dots
    for low, high in bounds[2:]:
        dots = dots + contract(query_ref[here, low:high], cand_ref[:, :, low:high].reshape(cands, high - low), 1, 1)
        yield dots


def low_kernel(
    bounds, rows, slot_ref, shard_ref, query_ref, pool_ref, norm_ref, ids_ref, pos_ref,
    coef_hbm, row_hbm, col_hbm, loss_ref, cand_ref, term_ref, coef_ref, row_ref, col_ref, sem, row_sem, col_sem,
):
    count = cand_ref.shape[1]
    levels, _, cands = coef_ref.shape
    blocks = loss_ref.shape[0]

    @pl.when(shard_ref[0] == 0)
    def _():
        row_ref[...] = jnp.zeros_like(row_ref)
        col_ref[...] = jnp.zeros_like(col_ref)

        def one(block, cand_ref, term_ref):
            here = pl.ds(block * rows, rows)
            take_blocks(pool_ref, slot_ref, block, count, cand_ref)
            pp = norm_rows(norm_ref, slot_ref, block, count)
            ids = ids_ref[pl.ds(block, 1), :]
            live = ids >= 0.0
            labels = jnp.where(ids == to_col(pos_ref[pl.ds(block, 1), :]), 1.0, 0.0)
            qq = jnp.zeros((rows, 1), F32)
            entropy = jnp.zeros((rows, 1), F32)
            logit_sum = jnp.zeros((rows, cands), F32)
            row_terms, col_terms = [], []
            sums = prefix_dots(bounds, rows, block, query_ref, cand_ref)
            for level, ((low, high), dots) in enumerate(zip(bounds, sums)):
                qq = qq + square_sums(query_ref[here, low:high])
                coef, row, col, part, logits = terms(
                    dots, lax.rsqrt(qq + EPS), pp[level : level + 1, :], live, labels, float(high // MINP)
                )
                term_ref[level] = coef
                row_terms.append(row)
                col_terms.append(col)
                entropy = entropy + part
                logit_sum = logit_sum + logits
            loss = entropy - jnp.sum(labels * logit_sum, axis=1, keepdims=True)
            coef = jnp.zeros((rows, cands), F32)
            row = jnp.zeros((rows, 1), F32)
            col = jnp.zeros((1, cands), F32)
            for level in reversed(range(levels)):
                coef = coef + term_ref[level]
                row = row + row_terms[level]
                col = col + col_terms[level]
                coef_ref[level, here, :] = coef
                row_ref[block, level : level + 1, :] = to_row(row)
                col_ref[block, level : level + 1, :] = col
            loss_ref[pl.ds(block, 1), :] = to_row(loss)

        def step(pair, carry):
            for j in range(2):
                one(pair * 2 + j, cand_ref.at[j], term_ref.at[j])
            here = pl.ds(pair * 2 * rows, 2 * rows)
            pltpu.make_async_copy(coef_ref.at[:, here], coef_hbm.at[:, here], sem).start()
            return carry

        lax.fori_loop(0, blocks // 2, step, 0)
        copies = [
            pltpu.make_async_copy(row_ref, row_hbm, row_sem),
            pltpu.make_async_copy(col_ref, col_hbm, col_sem),
        ]
        for copy in copies:
            copy.start()
        for copy in copies:
            copy.wait()
        pltpu.make_async_copy(coef_ref, coef_hbm, sem).wait()

    @pl.when(shard_ref[0] != 0)
    def _():
        loss_ref[...] = jnp.zeros_like(loss_ref)


def high_kernel(shards, per_shard, rows, weights, shard_ref, ids_ref, pos_ref, after_ref, *refs):
    del after_ref
    ins, outs, loss_ref = refs[:shards], refs[shards:-1], refs[-1]
    shard = shard_ref[0]
    base = per_shard * rows
    width = ids_ref.shape[1]
    in_half = [
        jnp.where(lax.rem(shard - shift + shards, shards) < shards // 2, 1.0, 0.0)
        for shift in range(shards)
    ]

    def total(span, keep):
        pieces = [ref[span, :] * scale if keep else ref[span, :] for ref, scale in zip(ins, in_half)]
        return (pieces[0] + pieces[1]) + (pieces[2] + pieces[3])

    below = slice(base, base + AUX)
    half_rows, half_cols, full_rows, full_cols, losses, coefs = [], [], [], [], [], []
    aux_half, aux_full = total(below, True), total(below, False)
    for k in range(per_shard):
        block = shard * per_shard + k
        ids = ids_ref[pl.ds(block, 1), :]
        live = ids >= 0.0
        labels = jnp.where(ids == to_col(pos_ref[pl.ds(block, 1), :]), 1.0, 0.0)
        span = slice(k * rows, (k + 1) * rows)
        results = []
        for keep, aux, weight in ((True, aux_half, weights[0]), (False, aux_full, weights[1])):
            scale = to_col(lax.rsqrt(aux[per_shard : per_shard + 1, span] + EPS))
            results.append(terms(total(span, keep), scale, aux[k : k + 1, :], live, labels, weight))
        (coef_h, row_h, col_h, part_h, logit_h), (coef_f, row_f, col_f, part_f, logit_f) = results
        loss = part_h + part_f - jnp.sum(labels * (logit_h + logit_f), axis=1, keepdims=True)
        coefs.append(((coef_h + coef_f).astype(BF16), coef_f.astype(BF16)))
        half_rows.append(to_row(row_h + row_f))
        full_rows.append(to_row(row_f))
        half_cols.append(col_h + col_f)
        full_cols.append(col_f)
        losses.append(to_row(loss))
    loss_ref[...] = jnp.concatenate(losses, axis=1)

    def aux_rows(rows_list, cols_list):
        line = jnp.concatenate(rows_list + [jnp.zeros((1, width - base), F32)], axis=1)
        table = jnp.concatenate(cols_list + [line], axis=0)
        table = jnp.concatenate([table, jnp.zeros((AUX - table.shape[0], width), F32)], axis=0)
        first = table.astype(BF16).astype(F32)
        second = (table - first).astype(BF16).astype(F32)
        third = table - first - second
        return jnp.concatenate([first, second, third, jnp.zeros_like(table)], axis=0).astype(BF16)

    aux = (aux_rows(half_rows, half_cols), aux_rows(full_rows, full_cols))
    for shift in range(shards):
        out_ref = outs[shift]
        high_target = lax.rem(shard + shift, shards) >= shards // 2
        for which, chosen in ((1, high_target), (0, jnp.logical_not(high_target))):

            @pl.when(chosen)
            def _():
                for k in range(per_shard):
                    out_ref[k * rows : (k + 1) * rows, :] = coefs[k][which]
                out_ref[base : base + COEF_AUX, :] = aux[which]


def unpack_aux(ref, base):
    packed = ref[base : base + COEF_AUX, :].astype(F32)
    return packed[:AUX] + packed[AUX : 2 * AUX] + packed[2 * AUX : 3 * AUX]


def passage_kernel(
    bounds, shards, per_shard, rows, slot_ref, shard_ref, query_ref, pool_ref, mask_ref, low_row_hbm, low_col_hbm,
    low_coef_hbm, *refs
):
    ins = refs[:shards]
    out_hbm, half_hbm, row_hbm, coef_ref, row_ref, col_ref, spread_ref, sum_ref, scale_ref, out_ref, half_ref = refs[shards:-8]
    low_row_ref, low_col_ref, low_coef_ref, out_sem, half_sem, row_sem, low_sem, pair_sem = refs[-8:]
    shard = shard_ref[0]
    base = per_shard * rows
    blocks = shards * per_shard
    slots, _, width = pool_ref.shape
    cands = coef_ref.shape[1]
    count = cands // PBLK

    loads = [
        pltpu.make_async_copy(low_row_hbm, low_row_ref, low_sem.at[0]),
        pltpu.make_async_copy(low_col_hbm, low_col_ref, low_sem.at[1]),
    ]
    pairs = blocks // 2

    def pair_rows(pair):
        return pl.ds(pair * 2 * rows, 2 * rows)

    def pair_load(pair):
        here = pair_rows(pair)
        return pltpu.make_async_copy(low_coef_hbm.at[:, here], low_coef_ref.at[:, here], pair_sem.at[pair])

    row_copy = pltpu.make_async_copy(row_ref, row_hbm, row_sem)

    @pl.when(shard == 0)
    def _():
        for load in loads:
            load.start()
        for pair in range(pairs):
            pair_load(pair).start()
        sum_ref[...] = jnp.zeros_like(sum_ref)

    scale_ref[...] = jnp.zeros_like(scale_ref)
    for shift in range(shards):
        source = lax.rem(shard - shift + shards, shards)
        coef_ref[pl.ds(source * base, base), :] = ins[shift][:base, :]
        aux = unpack_aux(ins[shift], base)
        for k in range(per_shard):
            col_ref[source * per_shard + k] = aux[k : k + 1, :]
            line = aux[per_shard : per_shard + 1, k * rows : (k + 1) * rows]
            row_ref[source * per_shard + k] = jnp.broadcast_to(line, (8, rows))

    def add_scales(block, low):
        cols = jnp.broadcast_to(col_ref[block], (8, cands))
        if low:
            cols = cols + low_col_ref[block]
        col_cols = columns(cols)
        for n in range(count):
            slot = slot_ref[block * count + n]
            scale_ref[slot] = scale_ref[slot] + col_cols[n * PBLK : (n + 1) * PBLK, :]

    def send(start, end):
        done = pl.ds(start, end - start)
        pltpu.make_async_copy(out_ref.at[:, :, done], out_hbm.at[:, :, done], out_sem).start()

    @pl.when(shard == 0)
    def _():
        levels = len(bounds)
        for load in loads:
            load.wait()
        row_ref[...] = row_ref[...] + low_row_ref[...]
        row_copy.start()

        def one(block):
            here = pl.ds(block * rows, rows)
            add_scales(block, True)
            base_coef = coef_ref[here, :].astype(F32)
            coefs = [(base_coef + low_coef_ref[level, here, :]).astype(BF16) for level in range(levels)]
            for level in range(levels):
                half_ref[level, here, :] = coefs[level]
            grads = [contract(coefs[0], mask_ref[0, here, :], 0, 0) + contract(coefs[1], mask_ref[1, here, :], 0, 0)]
            starts = [0]
            for level in range(2, levels):
                lo, hi = bounds[level]
                grads.append(contract(coefs[level], query_ref[here, lo:hi], 0, 0))
                starts.append(lo)
            for n in range(count):
                slot = slot_ref[block * count + n]
                for start, grad in zip(starts, grads):
                    lanes = slice(start, start + grad.shape[1])
                    sum_ref[slot, :, lanes] = sum_ref[slot, :, lanes] + grad[n * PBLK : (n + 1) * PBLK, :]

        def step(pair, carry):
            pair_load(pair).wait()
            for j in range(2):
                one(pair * 2 + j)
            here = pair_rows(pair)
            pltpu.make_async_copy(half_ref.at[:, here], half_hbm.at[:, here], half_sem).start()
            return carry

        lax.fori_loop(0, pairs, step, 0)
        copy = pltpu.make_async_copy(half_ref, half_hbm, half_sem)
        level_of = lax.broadcasted_iota(jnp.int32, (LANES, width), 0)
        column = lax.broadcasted_iota(jnp.int32, (LANES, width), 1)
        member = jnp.zeros((LANES, width), F32)
        for level, (lo, hi) in enumerate(bounds):
            member = jnp.where((level_of == level) & (column >= lo) & (column < hi), 1.0, member)
        member = member.astype(BF16)
        step_slots = slots // CHUNKS
        for chunk in range(CHUNKS):
            part = slice(chunk * step_slots, (chunk + 1) * step_slots)
            scale = scale_ref[part].reshape(step_slots * PBLK, LANES)
            high = scale.astype(BF16)
            rest = scale - high.astype(F32)
            middle = rest.astype(BF16)
            low = (rest - middle.astype(F32)).astype(BF16)
            wide = contract(high, member, 1, 0) + contract(middle, member, 1, 0) + contract(low, member, 1, 0)
            pool = pool_ref[part].reshape(step_slots * PBLK, width).astype(F32)
            total = sum_ref[part].reshape(step_slots * PBLK, width)
            out_ref[part] = (total - wide * pool).astype(BF16).reshape(step_slots, PBLK, width)
            pltpu.make_async_copy(out_ref.at[part], out_hbm.at[part], out_sem).start()
        copy.wait()
        row_copy.wait()
        pltpu.make_async_copy(out_ref, out_hbm, out_sem).wait()

    @pl.when(shard != 0)
    def _():
        row_copy.start()
        copy = pltpu.make_async_copy(coef_ref, half_hbm.at[0], half_sem)
        copy.start()
        spread_ref[...] = jnp.zeros_like(spread_ref)
        for block in range(blocks):
            add_scales(block, False)
            turned = coef_ref[pl.ds(block * rows, rows), :].astype(F32).T.astype(BF16)
            for n in range(count):
                spread_ref[slot_ref[block * count + n], :, block * rows : (block + 1) * rows] = turned[
                    n * PBLK : (n + 1) * PBLK, :
                ]
        spread = spread_ref[0:slots].reshape(slots * PBLK, blocks * rows)
        scale = scale_ref[0:slots].reshape(slots * PBLK, LANES)[:, 0:1]
        for start in range(0, width, PIECE):
            end = start + PIECE
            grad = contract(spread, query_ref[:, start:end], 1, 0)
            pool = pool_ref[:, :, start:end].reshape(slots * PBLK, end - start).astype(F32)
            out_ref[:, :, start:end] = (grad - scale * pool).astype(BF16).reshape(slots, PBLK, end - start)
            send(start, end)
        copy.wait()
        row_copy.wait()
        pltpu.make_async_copy(out_ref, out_hbm, out_sem).wait()


def query_kernel(
    bounds, rows, loss_scale, slot_ref, shard_ref, query_ref, pool_ref, row_ref, low_loss_ref, high_loss_ref, half_hbm,
    query_grad_ref, loss_ref, cand_ref, half_ref, sem,
):
    shard = shard_ref[0]
    blocks, cands = low_loss_ref.shape[0], half_ref.shape[2]
    count = cand_ref.shape[0]
    width = query_ref.shape[1]
    per_line = LANES // rows
    first = pltpu.make_async_copy(half_hbm.at[0], half_ref.at[0], sem.at[0])
    rest = pl.ds(1, half_ref.shape[0] - 1)
    others = pltpu.make_async_copy(half_hbm.at[rest], half_ref.at[rest], sem.at[1])
    first.start()

    @pl.when(shard == 0)
    def _():
        others.start()

    for block in range(blocks):
        j = block % per_line
        loss_ref[block // per_line : block // per_line + 1, j * rows : (j + 1) * rows] = low_loss_ref[block : block + 1, :]
    loss_ref[pl.ds(shard, 1), :] = loss_ref[pl.ds(shard, 1), :] + high_loss_ref[...]
    loss_ref[...] = loss_ref[...] * loss_scale

    def run(spans):
        def step(block, carry):
            take_blocks(pool_ref, slot_ref, block, count, cand_ref)
            row_cols = columns(row_ref[block])
            here = pl.ds(block * rows, rows)
            for level, (lo, hi) in enumerate(spans):
                query = query_ref[here, lo:hi].astype(F32)
                cand = cand_ref[:, :, lo:hi].reshape(cands, hi - lo)
                grad = contract(half_ref[level, here, :], cand, 1, 0) - row_cols[:rows, level : level + 1] * query
                query_grad_ref[here, lo:hi] = grad.astype(BF16)
            return carry

        lax.fori_loop(0, blocks, step, 0)

    first.wait()

    @pl.when(shard == 0)
    def _():
        others.wait()
        run(bounds)

    @pl.when(shard != 0)
    def _():
        run([(0, width)])


def collect_kernel(target_ref, back_hbm, out_ref, back_ref, sem):
    rows = out_ref.shape[0]
    size = back_ref.shape[0] // 2
    copies = []
    for half in range(2):
        part = pl.ds(half * size, size)
        copies.append(pltpu.make_async_copy(back_hbm.at[part], back_ref.at[part], sem.at[half]))
        copies[-1].start()
    here = lax.broadcasted_iota(jnp.int32, (rows, size), 0)
    total = None
    for half in range(2):
        part = slice(half * size, (half + 1) * size)
        choose = jnp.where(here == target_ref[:, part], 1.0, 0.0).astype(BF16)
        copies[half].wait()
        grad = contract(choose, back_ref[part, :], 1, 0)
        total = grad if total is None else total + grad
    out_ref[...] = total.astype(BF16)


def per_device(queries, passages, neg_lists, positives):
    peers = lax.axis_size("dp")
    shards = lax.axis_size("tensor")
    total_rows, width = queries.shape
    blocks = neg_lists.shape[0] // peers
    count = neg_lists.shape[1]
    rows = total_rows // blocks
    local_blocks = passages.shape[0] // PBLK
    cands = count * PBLK
    per_shard = blocks // shards
    base = per_shard * rows
    slots = peers
    my_index = lax.axis_index("dp")
    shard = lax.axis_index("tensor")
    sizes = [MINP * 2**level for level in range(NPRE)]
    low_sizes = [size for size in sizes if size <= width]
    high_sizes = [size for size in sizes if size > width]
    assert high_sizes == [width * shards // 2, width * shards] and low_sizes[-1] == width
    assert shards == 4 and base == LANES
    bounds = list(zip([0] + low_sizes[:-1], low_sizes))
    levels = len(bounds)
    weight_total = sum(size / MINP for size in sizes)

    flat = neg_lists.reshape(peers, blocks * count)
    mine = (flat >= 0) & (flat // local_blocks == my_index)
    wanted = jnp.max(jnp.where(mine, flat % local_blocks, -1), axis=1)
    own = lax.dynamic_slice_in_dim(neg_lists, my_index * blocks, blocks, 0)
    valid = own >= 0
    slot = jnp.where(valid, own // local_blocks, 0).reshape(blocks * count)
    spare_slot = jnp.where(valid, own // local_blocks, slots).reshape(blocks * count)
    within = jnp.arange(PBLK, dtype=jnp.int32)
    ids = jnp.where(valid[:, :, None], own[:, :, None] * PBLK + within[None, None, :], -1)
    ids = ids.reshape(blocks, cands).astype(F32)
    target = jnp.where(wanted[:, None] >= 0, wanted[:, None] * PBLK + within[None, :], -1).reshape(1, slots * PBLK)
    pos = positives.reshape(blocks, rows).astype(F32)
    shard_arr = shard.reshape(1).astype(jnp.int32)
    pool_shape = (slots, PBLK, width)

    pinned = partial(pltpu.with_memory_space_constraint, memory_space=pltpu.HBM)
    panels = pl.pallas_call(
        pack_kernel,
        out_shape=pltpu.HBM(pool_shape, BF16),
        in_specs=[smem(), hbm(), hbm()],
        out_specs=hbm(),
        scratch_shapes=[
            pltpu.VMEM((count, neg_lists.shape[0]), jnp.int32),
            pltpu.VMEM((local_blocks, PBLK, width), BF16),
            pltpu.VMEM(pool_shape, BF16),
            pltpu.VMEM((8, neg_lists.shape[0]), jnp.int32),
            pltpu.SMEM((8, neg_lists.shape[0]), jnp.int32),
            pltpu.SemaphoreType.DMA(()),
            pltpu.SemaphoreType.DMA(()),
            pltpu.SemaphoreType.DMA(()),
            pltpu.SemaphoreType.DMA(()),
        ],
        compiler_params=params(),
        name="pack",
    )(
        (my_index * local_blocks).reshape(1).astype(jnp.int32), pinned(neg_lists.T),
        pinned(passages.reshape(local_blocks, PBLK, width)),
    )
    pool = lax.all_to_all(panels, "dp", split_axis=0, concat_axis=0, tiled=True)
    full_norms, masked = pl.pallas_call(
        partial(prep_kernel, bounds[0][1], rows),
        out_shape=[
            jax.ShapeDtypeStruct((blocks, 1, rows), F32),
            jax.ShapeDtypeStruct((2, total_rows, LANES), BF16),
        ],
        in_specs=[vmem()],
        out_specs=[vmem()] * 2,
        compiler_params=params(),
        name="prep",
    )(queries)

    def shift_by(part, s):
        return lax.ppermute(part, "tensor", [(i, (i + s) % shards) for i in range(shards)])

    cand_scratch = pltpu.VMEM((count, PBLK, width), BF16)
    message = jax.ShapeDtypeStruct((base + AUX, cands), F32)
    norm_shape = (slots, PBLK, LANES)
    norms, far, right, left, here = pl.pallas_call(
        partial(first_dots_kernel, bounds, shards, per_shard, rows, (2, 1, 3, 0)),
        out_shape=[jax.ShapeDtypeStruct(norm_shape, F32)] + [message] * shards,
        in_specs=[smem(), smem(), vmem(), vmem(), vmem()],
        out_specs=[vmem()] * (shards + 1),
        scratch_shapes=[cand_scratch],
        compiler_params=params(),
        name="dots",
    )(slot, shard_arr, queries, pool, full_norms)
    arrived = [here, shift_by(right, 1), shift_by(far, 2), shift_by(left, 3)]

    low_coef, low_row, low_col, low_loss = pl.pallas_call(
        partial(low_kernel, bounds, rows),
        out_shape=[
            pltpu.HBM((levels, total_rows, cands), F32),
            pltpu.HBM((blocks, 8, rows), F32),
            pltpu.HBM((blocks, 8, cands), F32),
            jax.ShapeDtypeStruct((blocks, rows), F32),
        ],
        in_specs=[smem(), smem()] + [vmem()] * 5,
        out_specs=[hbm()] * 3 + [vmem()],
        scratch_shapes=[
            pltpu.VMEM((2, count, PBLK, width), BF16),
            pltpu.VMEM((2, levels, rows, cands), F32),
            pltpu.VMEM((levels, total_rows, cands), F32),
            pltpu.VMEM((blocks, 8, rows), F32),
            pltpu.VMEM((blocks, 8, cands), F32),
            pltpu.SemaphoreType.DMA(()),
            pltpu.SemaphoreType.DMA(()),
            pltpu.SemaphoreType.DMA(()),
        ],
        compiler_params=params(),
        name="low",
    )(slot, shard_arr, queries, pool, norms, ids, pos)
    *coefs, high_loss = pl.pallas_call(
        partial(high_kernel, shards, per_shard, rows, [size / MINP for size in high_sizes]),
        out_shape=[jax.ShapeDtypeStruct((base + COEF_AUX, cands), BF16)] * shards
        + [jax.ShapeDtypeStruct((1, base), F32)],
        in_specs=[smem()] + [vmem()] * 2 + [hbm()] + [vmem()] * shards,
        out_specs=[vmem()] * (shards + 1),
        compiler_params=params(),
        name="high",
    )(shard_arr, ids, pos, pinned(low_row), *arrived)
    coefs = [coefs[0]] + [shift_by(coefs[s], s) for s in range(1, shards)]

    half_shape = (levels, total_rows, cands)
    slot_grad, half, row_table = pl.pallas_call(
        partial(passage_kernel, bounds, shards, per_shard, rows),
        out_shape=[pltpu.HBM(pool_shape, BF16), pltpu.HBM(half_shape, BF16), pltpu.HBM((blocks, 8, rows), F32)],
        in_specs=[smem(), smem()] + [vmem()] * 3 + [hbm()] * 3 + [vmem()] * shards,
        out_specs=[hbm()] * 3,
        scratch_shapes=[
            pltpu.VMEM((total_rows, cands), BF16),
            pltpu.VMEM((blocks, 8, rows), F32),
            pltpu.VMEM((blocks, 1, cands), F32),
            pltpu.VMEM((slots + 1, PBLK, total_rows), BF16),
            pltpu.VMEM((slots + 1, PBLK, width), F32),
            pltpu.VMEM((slots + 1, PBLK, LANES), F32),
            pltpu.VMEM(pool_shape, BF16),
            pltpu.VMEM(half_shape, BF16),
            pltpu.VMEM((blocks, 8, rows), F32),
            pltpu.VMEM((blocks, 8, cands), F32),
            pltpu.VMEM((levels, total_rows, cands), F32),
            pltpu.SemaphoreType.DMA(()),
            pltpu.SemaphoreType.DMA(()),
            pltpu.SemaphoreType.DMA(()),
            pltpu.SemaphoreType.DMA((2,)),
            pltpu.SemaphoreType.DMA((blocks // 2,)),
        ],
        compiler_params=params(),
        name="passage",
    )(
        spare_slot, shard_arr, queries, pool, masked,
        pinned(low_row), pinned(low_col), pinned(low_coef), *coefs,
    )
    back = lax.all_to_all(slot_grad, "dp", split_axis=0, concat_axis=0, tiled=True)

    query_grad, loss = pl.pallas_call(
        partial(query_kernel, bounds, rows, 1.0 / weight_total),
        out_shape=[
            jax.ShapeDtypeStruct((total_rows, width), BF16),
            jax.ShapeDtypeStruct((shards, base), F32),
        ],
        in_specs=[smem(), smem()] + [vmem()] * 5 + [hbm()],
        out_specs=[vmem()] * 2,
        scratch_shapes=[cand_scratch, pltpu.VMEM(half_shape, BF16), pltpu.SemaphoreType.DMA((2,))],
        compiler_params=params(),
        name="query",
    )(slot, shard_arr, queries, pool, row_table, low_loss, high_loss, pinned(half))
    loss = lax.psum(loss, "tensor")

    passage_grad = pl.pallas_call(
        collect_kernel,
        out_shape=jax.ShapeDtypeStruct((local_blocks * PBLK, width), BF16),
        in_specs=[vmem(), hbm()],
        out_specs=vmem(),
        scratch_shapes=[pltpu.VMEM((slots * PBLK, width), BF16), pltpu.SemaphoreType.DMA((2,))],
        compiler_params=params(),
        name="collect",
    )(target, pinned(back.reshape(slots * PBLK, width)))
    return (
        query_grad,
        passage_grad,
        loss.reshape(total_rows),
    )


def solution(mesh):
    return jax.shard_map(
        per_device,
        mesh=mesh,
        in_specs=(P("dp", "tensor"), P("dp", "tensor"), P(), P("dp")),
        out_specs=(P("dp", "tensor"), P("dp", "tensor"), P("dp")),
        check_vma=False,
    )
```

```python
from functools import partial

import jax
import jax.numpy as jnp
from jax import lax
from jax.experimental import pallas as pl
from jax.experimental.pallas import tpu as pltpu
from jax.sharding import PartitionSpec as P

MINP = 64
NPRE = 7
PBLK = 16

EPS = 1e-06
INV_TEMP = 20.0

F32 = jnp.float32
BF16 = jnp.bfloat16

AUX = 8
COEF_AUX = 32
LANES = 128
PIECE = 256
CHUNKS = 4


def vmem():
    return pl.BlockSpec(memory_space=pltpu.VMEM)


def smem():
    return pl.BlockSpec(memory_space=pltpu.SMEM)


def hbm():
    return pl.BlockSpec(memory_space=pltpu.HBM)


def params():
    return pltpu.CompilerParams(vmem_limit_bytes=20 * 2**20)


def contract(a, b, da, db):
    return lax.dot_general(a, b, (((da,), (db,)), ((), ())), preferred_element_type=F32)


def eye(n):
    return lax.broadcasted_iota(jnp.int32, (n, n), 0) == lax.broadcasted_iota(jnp.int32, (n, n), 1)


def to_col(row):
    return jnp.sum(jnp.where(eye(row.shape[1]), row, 0.0), axis=1, keepdims=True)


def to_row(col):
    return jnp.sum(jnp.where(eye(col.shape[0]), col, 0.0), axis=0, keepdims=True)


def square_sums(half):
    wide = half.astype(F32)
    return jnp.sum(wide * wide, axis=1, keepdims=True)


def columns(table):
    table = jnp.concatenate([table, jnp.zeros((8, LANES - table.shape[1]), F32)], axis=1) if table.shape[1] < LANES else table
    return jnp.concatenate([table, jnp.zeros((LANES - 8, table.shape[1]), F32)], axis=0).T


def terms(dots, a, pp_row, live, labels, weight):
    b = jnp.where(live, lax.rsqrt(pp_row + EPS), 0.0)
    scale = (a * INV_TEMP) * b
    logits = dots * scale
    exponent = jnp.where(live, jnp.exp(logits), 0.0)
    total = jnp.sum(exponent, axis=1, keepdims=True)
    gradient = weight * (exponent * (1.0 / total) - labels)
    inner = gradient * logits
    row = jnp.square(a[:, :1]) * jnp.sum(inner, axis=1, keepdims=True)
    col = (b * b) * jnp.sum(inner, axis=0, keepdims=True)
    return gradient * scale, row, col, weight * jnp.log(total), weight * logits


def take_blocks(pool_ref, slot_ref, block, count, out_ref):
    for n in range(count):
        out_ref[n] = pool_ref[slot_ref[block * count + n]]


def pool_norms(pool_ref, norm_ref, bounds):
    step_slots = 4
    rows = step_slots * PBLK
    lane = lax.broadcasted_iota(jnp.int32, (rows, LANES), 1)

    def lane_sum(part):
        return jnp.sum(part, axis=1, keepdims=True)

    def step(i, carry):
        here = pl.ds(i * step_slots, step_slots)
        wide = pool_ref[here].reshape(rows, pool_ref.shape[2]).astype(F32)
        square = wide * wide
        result, before, inside = None, None, None
        for level, (low, high) in enumerate(bounds):
            if high < LANES:
                total = lane_sum(jnp.where(lane < high, square[:, :LANES], 0.0))
            else:
                start = low // LANES * LANES
                parts = [square[:, j : j + LANES] for j in range(start, high, LANES)]
                while len(parts) > 1:
                    parts = [x + y for x, y in zip(parts[::2], parts[1::2])]
                total = lane_sum(parts[0])
                if start:
                    total = total + before
            before = total
            result = jnp.broadcast_to(total, (rows, LANES)) if result is None else jnp.where(lane == level, total, result)
        norm_ref[here] = result.reshape(step_slots, PBLK, LANES)
        return carry

    lax.fori_loop(0, pool_ref.shape[0] // step_slots, step, 0, unroll=4)


def norm_rows(norm_ref, slot_ref, block, count):
    table = jnp.concatenate([norm_ref[slot_ref[block * count + n]] for n in range(count)], axis=0)
    return table.T[:8, :]


def pack_kernel(
    first_ref, lists_hbm, block_hbm, out_hbm, lists_ref, block_ref, row_ref, wanted_ref, lists_sem, in_sem, row_sem, out_sem
):
    load = pltpu.make_async_copy(block_hbm, block_ref, in_sem)
    lists = pltpu.make_async_copy(lists_hbm, lists_ref, lists_sem)
    lists.start()
    load.start()
    lists.wait()
    local = lists_ref[...] - first_ref[0]
    local = jnp.where((local >= 0) & (local < block_ref.shape[0]), local, 0).astype(F32)
    row = jnp.broadcast_to(jnp.max(local, axis=0, keepdims=True), row_ref.shape)
    size = row.shape[1]
    step = 1
    while step < size // out_hbm.shape[0]:
        row = jnp.maximum(row, pltpu.roll(row, size - step, 1))
        step *= 2
    row_ref[...] = row.astype(jnp.int32)
    save = pltpu.make_async_copy(row_ref, wanted_ref, row_sem)
    save.start()
    save.wait()
    load.wait()
    share = size // out_hbm.shape[0]

    def one(d, carry):
        pltpu.make_async_copy(block_ref.at[wanted_ref[0, d * share]], out_hbm.at[d], out_sem).start()
        return carry

    lax.fori_loop(0, out_hbm.shape[0], one, 0, unroll=8)
    pltpu.make_async_copy(out_hbm, out_hbm, out_sem).wait()


def prep_kernel(split, rows, query_ref, full_ref, mask_ref):
    lane = lax.broadcasted_iota(jnp.int32, (rows, LANES), 1)

    def step(block, carry):
        here = pl.ds(block * rows, rows)
        full_ref[block] = to_row(square_sums(query_ref[here, :]))
        first = query_ref[here, :LANES].astype(F32)
        mask_ref[0, here, :] = jnp.where(lane < split, first, 0.0).astype(BF16)
        mask_ref[1, here, :] = jnp.where(lane < split, 0.0, first).astype(BF16)
        return carry

    lax.fori_loop(0, full_ref.shape[0], step, 0)


def dots_kernel(
    bounds, shards, per_shard, rows, shifts, slot_ref, shard_ref, query_ref, pool_ref, full_ref, pp_ref, *refs
):
    outs, (norm_ref, cand_ref) = refs[:-2], refs[-2:]
    pool_norms(pool_ref, norm_ref, bounds)
    count, _, width = cand_ref.shape
    shard = shard_ref[0]
    base = per_shard * rows
    last = len(bounds) - 1
    for shift, out_ref in zip(shifts, outs):
        target = lax.rem(shard + shift, shards)
        for k in range(per_shard):
            block = target * per_shard + k
            take_blocks(pool_ref, slot_ref, block, count, cand_ref)
            query = query_ref[pl.ds(block * rows, rows), :]
            cand = cand_ref[...].reshape(count * PBLK, width)
            out_ref[k * rows : (k + 1) * rows, :] = contract(query, cand, 1, 1)
            pp = norm_rows(norm_ref, slot_ref, block, count)
            pp_ref[block] = pp
            out_ref[base + k : base + k + 1, :] = pp[last : last + 1, :]
            out_ref[base + per_shard : base + per_shard + 1, k * rows : (k + 1) * rows] = full_ref[block]


def prefix_dots(bounds, rows, block, query_ref, cand_ref):
    here = pl.ds(block * rows, rows)
    cands = cand_ref.shape[0] * PBLK
    lane = lax.broadcasted_iota(jnp.int32, (rows, LANES), 1)
    first = query_ref[here, :LANES]
    short = jnp.where(lane < bounds[0][1], first.astype(F32), 0.0).astype(BF16)
    both = contract(
        jnp.concatenate([short, first], axis=0), cand_ref[:, :, :LANES].reshape(cands, LANES), 1, 1
    )
    yield both[:rows]
    dots = both[rows:]
    yield dots
    for low, high in bounds[2:]:
        dots = dots + contract(query_ref[here, low:high], cand_ref[:, :, low:high].reshape(cands, high - low), 1, 1)
        yield dots


def low_kernel(
    bounds, rows, slot_ref, shard_ref, query_ref, pool_ref, pp_ref, ids_ref, pos_ref,
    coef_hbm, row_hbm, col_hbm, loss_ref, cand_ref, term_ref, coef_ref, row_ref, col_ref, sem, row_sem, col_sem,
):
    count = cand_ref.shape[1]
    levels, _, cands = coef_ref.shape
    blocks = loss_ref.shape[0]

    @pl.when(shard_ref[0] == 0)
    def _():
        row_ref[...] = jnp.zeros_like(row_ref)
        col_ref[...] = jnp.zeros_like(col_ref)

        def one(block, cand_ref, term_ref):
            here = pl.ds(block * rows, rows)
            take_blocks(pool_ref, slot_ref, block, count, cand_ref)
            pp = pp_ref[block]
            ids = ids_ref[pl.ds(block, 1), :]
            live = ids >= 0.0
            labels = jnp.where(ids == to_col(pos_ref[pl.ds(block, 1), :]), 1.0, 0.0)
            qq = jnp.zeros((rows, 1), F32)
            entropy = jnp.zeros((rows, 1), F32)
            logit_sum = jnp.zeros((rows, cands), F32)
            row_terms, col_terms = [], []
            sums = prefix_dots(bounds, rows, block, query_ref, cand_ref)
            for level, ((low, high), dots) in enumerate(zip(bounds, sums)):
                qq = qq + square_sums(query_ref[here, low:high])
                coef, row, col, part, logits = terms(
                    dots, lax.rsqrt(qq + EPS), pp[level : level + 1, :], live, labels, float(high // MINP)
                )
                term_ref[level] = coef
                row_terms.append(row)
                col_terms.append(col)
                entropy = entropy + part
                logit_sum = logit_sum + logits
            loss = entropy - jnp.sum(labels * logit_sum, axis=1, keepdims=True)
            coef = jnp.zeros((rows, cands), F32)
            row = jnp.zeros((rows, 1), F32)
            col = jnp.zeros((1, cands), F32)
            for level in reversed(range(levels)):
                coef = coef + term_ref[level]
                row = row + row_terms[level]
                col = col + col_terms[level]
                coef_ref[level, here, :] = coef
                row_ref[block, level : level + 1, :] = to_row(row)
                col_ref[block, level : level + 1, :] = col
            loss_ref[pl.ds(block, 1), :] = to_row(loss)

        def step(pair, carry):
            for j in range(2):
                one(pair * 2 + j, cand_ref.at[j], term_ref.at[j])
            here = pl.ds(pair * 2 * rows, 2 * rows)
            pltpu.make_async_copy(coef_ref.at[:, here], coef_hbm.at[:, here], sem).start()
            return carry

        lax.fori_loop(0, blocks // 2, step, 0)
        copies = [
            pltpu.make_async_copy(row_ref, row_hbm, row_sem),
            pltpu.make_async_copy(col_ref, col_hbm, col_sem),
        ]
        for copy in copies:
            copy.start()
        for copy in copies:
            copy.wait()
        pltpu.make_async_copy(coef_ref, coef_hbm, sem).wait()

    @pl.when(shard_ref[0] != 0)
    def _():
        loss_ref[...] = jnp.zeros_like(loss_ref)


def high_kernel(shards, per_shard, rows, weights, shard_ref, ids_ref, pos_ref, after_ref, *refs):
    del after_ref
    ins, outs, loss_ref = refs[:shards], refs[shards:-1], refs[-1]
    shard = shard_ref[0]
    base = per_shard * rows
    width = ids_ref.shape[1]
    in_half = [
        jnp.where(lax.rem(shard - shift + shards, shards) < shards // 2, 1.0, 0.0)
        for shift in range(shards)
    ]

    def total(span, keep):
        pieces = [ref[span, :] * scale if keep else ref[span, :] for ref, scale in zip(ins, in_half)]
        return (pieces[0] + pieces[1]) + (pieces[2] + pieces[3])

    below = slice(base, base + AUX)
    half_rows, half_cols, full_rows, full_cols, losses, coefs = [], [], [], [], [], []
    aux_half, aux_full = total(below, True), total(below, False)
    for k in range(per_shard):
        block = shard * per_shard + k
        ids = ids_ref[pl.ds(block, 1), :]
        live = ids >= 0.0
        labels = jnp.where(ids == to_col(pos_ref[pl.ds(block, 1), :]), 1.0, 0.0)
        span = slice(k * rows, (k + 1) * rows)
        results = []
        for keep, aux, weight in ((True, aux_half, weights[0]), (False, aux_full, weights[1])):
            scale = to_col(lax.rsqrt(aux[per_shard : per_shard + 1, span] + EPS))
            results.append(terms(total(span, keep), scale, aux[k : k + 1, :], live, labels, weight))
        (coef_h, row_h, col_h, part_h, logit_h), (coef_f, row_f, col_f, part_f, logit_f) = results
        loss = part_h + part_f - jnp.sum(labels * (logit_h + logit_f), axis=1, keepdims=True)
        coefs.append(((coef_h + coef_f).astype(BF16), coef_f.astype(BF16)))
        half_rows.append(to_row(row_h + row_f))
        full_rows.append(to_row(row_f))
        half_cols.append(col_h + col_f)
        full_cols.append(col_f)
        losses.append(to_row(loss))
    loss_ref[...] = jnp.concatenate(losses, axis=1)

    def aux_rows(rows_list, cols_list):
        line = jnp.concatenate(rows_list + [jnp.zeros((1, width - base), F32)], axis=1)
        table = jnp.concatenate(cols_list + [line], axis=0)
        table = jnp.concatenate([table, jnp.zeros((AUX - table.shape[0], width), F32)], axis=0)
        first = table.astype(BF16).astype(F32)
        second = (table - first).astype(BF16).astype(F32)
        third = table - first - second
        return jnp.concatenate([first, second, third, jnp.zeros_like(table)], axis=0).astype(BF16)

    aux = (aux_rows(half_rows, half_cols), aux_rows(full_rows, full_cols))
    for shift in range(shards):
        out_ref = outs[shift]
        high_target = lax.rem(shard + shift, shards) >= shards // 2
        for which, chosen in ((1, high_target), (0, jnp.logical_not(high_target))):

            @pl.when(chosen)
            def _():
                for k in range(per_shard):
                    out_ref[k * rows : (k + 1) * rows, :] = coefs[k][which]
                out_ref[base : base + COEF_AUX, :] = aux[which]


def unpack_aux(ref, base):
    packed = ref[base : base + COEF_AUX, :].astype(F32)
    return packed[:AUX] + packed[AUX : 2 * AUX] + packed[2 * AUX : 3 * AUX]


def passage_kernel(
    bounds, shards, per_shard, rows, slot_ref, shard_ref, query_ref, pool_ref, mask_ref, low_row_hbm, low_col_hbm,
    low_coef_hbm, *refs
):
    ins = refs[:shards]
    out_hbm, half_hbm, row_hbm, coef_ref, row_ref, col_ref, spread_ref, sum_ref, scale_ref, out_ref, half_ref = refs[shards:-8]
    low_row_ref, low_col_ref, low_coef_ref, out_sem, half_sem, row_sem, low_sem, pair_sem = refs[-8:]
    shard = shard_ref[0]
    base = per_shard * rows
    blocks = shards * per_shard
    slots, _, width = pool_ref.shape
    cands = coef_ref.shape[1]
    count = cands // PBLK

    loads = [
        pltpu.make_async_copy(low_row_hbm, low_row_ref, low_sem.at[0]),
        pltpu.make_async_copy(low_col_hbm, low_col_ref, low_sem.at[1]),
    ]
    pairs = blocks // 2

    def pair_rows(pair):
        return pl.ds(pair * 2 * rows, 2 * rows)

    def pair_load(pair):
        here = pair_rows(pair)
        return pltpu.make_async_copy(low_coef_hbm.at[:, here], low_coef_ref.at[:, here], pair_sem.at[pair])

    row_copy = pltpu.make_async_copy(row_ref, row_hbm, row_sem)

    @pl.when(shard == 0)
    def _():
        for load in loads:
            load.start()
        for pair in range(pairs):
            pair_load(pair).start()
        sum_ref[...] = jnp.zeros_like(sum_ref)

    scale_ref[...] = jnp.zeros_like(scale_ref)
    for shift in range(shards):
        source = lax.rem(shard - shift + shards, shards)
        coef_ref[pl.ds(source * base, base), :] = ins[shift][:base, :]
        aux = unpack_aux(ins[shift], base)
        for k in range(per_shard):
            col_ref[source * per_shard + k] = aux[k : k + 1, :]
            line = aux[per_shard : per_shard + 1, k * rows : (k + 1) * rows]
            row_ref[source * per_shard + k] = jnp.broadcast_to(line, (8, rows))

    def add_scales(block, low):
        cols = jnp.broadcast_to(col_ref[block], (8, cands))
        if low:
            cols = cols + low_col_ref[block]
        col_cols = columns(cols)
        for n in range(count):
            slot = slot_ref[block * count + n]
            scale_ref[slot] = scale_ref[slot] + col_cols[n * PBLK : (n + 1) * PBLK, :]

    def send(start, end):
        done = pl.ds(start, end - start)
        pltpu.make_async_copy(out_ref.at[:, :, done], out_hbm.at[:, :, done], out_sem).start()

    @pl.when(shard == 0)
    def _():
        levels = len(bounds)
        for load in loads:
            load.wait()
        row_ref[...] = row_ref[...] + low_row_ref[...]
        row_copy.start()

        def one(block):
            here = pl.ds(block * rows, rows)
            add_scales(block, True)
            base_coef = coef_ref[here, :].astype(F32)
            coefs = [(base_coef + low_coef_ref[level, here, :]).astype(BF16) for level in range(levels)]
            for level in range(levels):
                half_ref[level, here, :] = coefs[level]
            grads = [contract(coefs[0], mask_ref[0, here, :], 0, 0) + contract(coefs[1], mask_ref[1, here, :], 0, 0)]
            starts = [0]
            for level in range(2, levels):
                lo, hi = bounds[level]
                grads.append(contract(coefs[level], query_ref[here, lo:hi], 0, 0))
                starts.append(lo)
            for n in range(count):
                slot = slot_ref[block * count + n]
                for start, grad in zip(starts, grads):
                    lanes = slice(start, start + grad.shape[1])
                    sum_ref[slot, :, lanes] = sum_ref[slot, :, lanes] + grad[n * PBLK : (n + 1) * PBLK, :]

        for pair in range(pairs):
            pair_load(pair).wait()
            for j in range(2):
                one(pair * 2 + j)
            here = pair_rows(pair)
            pltpu.make_async_copy(half_ref.at[:, here], half_hbm.at[:, here], half_sem).start()
        copy = pltpu.make_async_copy(half_ref, half_hbm, half_sem)
        level_of = lax.broadcasted_iota(jnp.int32, (LANES, width), 0)
        column = lax.broadcasted_iota(jnp.int32, (LANES, width), 1)
        member = jnp.zeros((LANES, width), F32)
        for level, (lo, hi) in enumerate(bounds):
            member = jnp.where((level_of == level) & (column >= lo) & (column < hi), 1.0, member)
        member = member.astype(BF16)
        step_slots = slots // CHUNKS
        for chunk in range(CHUNKS):
            part = slice(chunk * step_slots, (chunk + 1) * step_slots)
            scale = scale_ref[part].reshape(step_slots * PBLK, LANES)
            high = scale.astype(BF16)
            rest = scale - high.astype(F32)
            middle = rest.astype(BF16)
            low = (rest - middle.astype(F32)).astype(BF16)
            wide = contract(high, member, 1, 0) + contract(middle, member, 1, 0) + contract(low, member, 1, 0)
            pool = pool_ref[part].reshape(step_slots * PBLK, width).astype(F32)
            total = sum_ref[part].reshape(step_slots * PBLK, width)
            out_ref[part] = (total - wide * pool).astype(BF16).reshape(step_slots, PBLK, width)
            pltpu.make_async_copy(out_ref.at[part], out_hbm.at[part], out_sem).start()
        copy.wait()
        row_copy.wait()
        pltpu.make_async_copy(out_ref, out_hbm, out_sem).wait()

    @pl.when(shard != 0)
    def _():
        row_copy.start()
        copy = pltpu.make_async_copy(coef_ref, half_hbm.at[0], half_sem)
        copy.start()
        spread_ref[...] = jnp.zeros_like(spread_ref)
        for block in range(blocks):
            add_scales(block, False)
            turned = coef_ref[pl.ds(block * rows, rows), :].astype(F32).T.astype(BF16)
            for n in range(count):
                spread_ref[slot_ref[block * count + n], :, block * rows : (block + 1) * rows] = turned[
                    n * PBLK : (n + 1) * PBLK, :
                ]
        spread = spread_ref[0:slots].reshape(slots * PBLK, blocks * rows)
        scale = scale_ref[0:slots].reshape(slots * PBLK, LANES)[:, 0:1]
        for start in range(0, width, PIECE):
            end = start + PIECE
            grad = contract(spread, query_ref[:, start:end], 1, 0)
            pool = pool_ref[:, :, start:end].reshape(slots * PBLK, end - start).astype(F32)
            out_ref[:, :, start:end] = (grad - scale * pool).astype(BF16).reshape(slots, PBLK, end - start)
            send(start, end)
        copy.wait()
        row_copy.wait()
        pltpu.make_async_copy(out_ref, out_hbm, out_sem).wait()


def query_kernel(
    bounds, rows, loss_scale, slot_ref, shard_ref, query_ref, pool_ref, row_ref, low_loss_ref, high_loss_ref, half_hbm,
    query_grad_ref, loss_ref, cand_ref, half_ref, sem,
):
    shard = shard_ref[0]
    blocks, cands = low_loss_ref.shape[0], half_ref.shape[2]
    count = cand_ref.shape[0]
    width = query_ref.shape[1]
    per_line = LANES // rows
    first = pltpu.make_async_copy(half_hbm.at[0], half_ref.at[0], sem.at[0])
    rest = pl.ds(1, half_ref.shape[0] - 1)
    others = pltpu.make_async_copy(half_hbm.at[rest], half_ref.at[rest], sem.at[1])
    first.start()

    @pl.when(shard == 0)
    def _():
        others.start()

    for block in range(blocks):
        j = block % per_line
        loss_ref[block // per_line : block // per_line + 1, j * rows : (j + 1) * rows] = low_loss_ref[block : block + 1, :]
    loss_ref[pl.ds(shard, 1), :] = loss_ref[pl.ds(shard, 1), :] + high_loss_ref[...]
    loss_ref[...] = loss_ref[...] * loss_scale

    def run(spans):
        def step(block, carry):
            take_blocks(pool_ref, slot_ref, block, count, cand_ref)
            row_cols = columns(row_ref[block])
            here = pl.ds(block * rows, rows)
            for level, (lo, hi) in enumerate(spans):
                query = query_ref[here, lo:hi].astype(F32)
                cand = cand_ref[:, :, lo:hi].reshape(cands, hi - lo)
                grad = contract(half_ref[level, here, :], cand, 1, 0) - row_cols[:rows, level : level + 1] * query
                query_grad_ref[here, lo:hi] = grad.astype(BF16)
            return carry

        lax.fori_loop(0, blocks, step, 0)

    first.wait()

    @pl.when(shard == 0)
    def _():
        others.wait()
        run(bounds)

    @pl.when(shard != 0)
    def _():
        run([(0, width)])


def collect_kernel(target_ref, back_hbm, out_ref, back_ref, sem):
    rows = out_ref.shape[0]
    size = back_ref.shape[0] // 2
    copies = []
    for half in range(2):
        part = pl.ds(half * size, size)
        copies.append(pltpu.make_async_copy(back_hbm.at[part], back_ref.at[part], sem.at[half]))
        copies[-1].start()
    here = lax.broadcasted_iota(jnp.int32, (rows, size), 0)
    total = None
    for half in range(2):
        part = slice(half * size, (half + 1) * size)
        choose = jnp.where(here == target_ref[:, part], 1.0, 0.0).astype(BF16)
        copies[half].wait()
        grad = contract(choose, back_ref[part, :], 1, 0)
        total = grad if total is None else total + grad
    out_ref[...] = total.astype(BF16)


def per_device(queries, passages, neg_lists, positives):
    peers = lax.axis_size("dp")
    shards = lax.axis_size("tensor")
    total_rows, width = queries.shape
    blocks = neg_lists.shape[0] // peers
    count = neg_lists.shape[1]
    rows = total_rows // blocks
    local_blocks = passages.shape[0] // PBLK
    cands = count * PBLK
    per_shard = blocks // shards
    base = per_shard * rows
    slots = peers
    my_index = lax.axis_index("dp")
    shard = lax.axis_index("tensor")
    sizes = [MINP * 2**level for level in range(NPRE)]
    low_sizes = [size for size in sizes if size <= width]
    high_sizes = [size for size in sizes if size > width]
    assert high_sizes == [width * shards // 2, width * shards] and low_sizes[-1] == width
    assert shards == 4 and base == LANES
    bounds = list(zip([0] + low_sizes[:-1], low_sizes))
    levels = len(bounds)
    weight_total = sum(size / MINP for size in sizes)

    flat = neg_lists.reshape(peers, blocks * count)
    mine = (flat >= 0) & (flat // local_blocks == my_index)
    wanted = jnp.max(jnp.where(mine, flat % local_blocks, -1), axis=1)
    own = lax.dynamic_slice_in_dim(neg_lists, my_index * blocks, blocks, 0)
    valid = own >= 0
    slot = jnp.where(valid, own // local_blocks, 0).reshape(blocks * count)
    spare_slot = jnp.where(valid, own // local_blocks, slots).reshape(blocks * count)
    within = jnp.arange(PBLK, dtype=jnp.int32)
    ids = jnp.where(valid[:, :, None], own[:, :, None] * PBLK + within[None, None, :], -1)
    ids = ids.reshape(blocks, cands).astype(F32)
    target = jnp.where(wanted[:, None] >= 0, wanted[:, None] * PBLK + within[None, :], -1).reshape(1, slots * PBLK)
    pos = positives.reshape(blocks, rows).astype(F32)
    shard_arr = shard.reshape(1).astype(jnp.int32)
    pool_shape = (slots, PBLK, width)

    pinned = partial(pltpu.with_memory_space_constraint, memory_space=pltpu.HBM)
    panels = pl.pallas_call(
        pack_kernel,
        out_shape=pltpu.HBM(pool_shape, BF16),
        in_specs=[smem(), hbm(), hbm()],
        out_specs=hbm(),
        scratch_shapes=[
            pltpu.VMEM((count, neg_lists.shape[0]), jnp.int32),
            pltpu.VMEM((local_blocks, PBLK, width), BF16),
            pltpu.VMEM((8, neg_lists.shape[0]), jnp.int32),
            pltpu.SMEM((8, neg_lists.shape[0]), jnp.int32),
            pltpu.SemaphoreType.DMA(()),
            pltpu.SemaphoreType.DMA(()),
            pltpu.SemaphoreType.DMA(()),
            pltpu.SemaphoreType.DMA(()),
        ],
        compiler_params=params(),
        name="pack",
    )(
        (my_index * local_blocks).reshape(1).astype(jnp.int32), pinned(neg_lists.T),
        pinned(passages.reshape(local_blocks, PBLK, width)),
    )
    pool = lax.all_to_all(panels, "dp", split_axis=0, concat_axis=0, tiled=True)
    full_norms, masked = pl.pallas_call(
        partial(prep_kernel, bounds[0][1], rows),
        out_shape=[
            jax.ShapeDtypeStruct((blocks, 1, rows), F32),
            jax.ShapeDtypeStruct((2, total_rows, LANES), BF16),
        ],
        in_specs=[vmem()],
        out_specs=[vmem()] * 2,
        compiler_params=params(),
        name="prep",
    )(queries)

    def shift_by(part, s):
        return lax.ppermute(part, "tensor", [(i, (i + s) % shards) for i in range(shards)])

    cand_scratch = pltpu.VMEM((count, PBLK, width), BF16)
    message = jax.ShapeDtypeStruct((base + AUX, cands), F32)
    norm_rows_of, far, right, left, here = pl.pallas_call(
        partial(dots_kernel, bounds, shards, per_shard, rows, (2, 1, 3, 0)),
        out_shape=[jax.ShapeDtypeStruct((blocks, 8, cands), F32)] + [message] * shards,
        in_specs=[smem(), smem(), vmem(), vmem(), vmem()],
        out_specs=[vmem()] * (shards + 1),
        scratch_shapes=[pltpu.VMEM((slots, PBLK, LANES), F32), cand_scratch],
        compiler_params=params(),
        name="dots",
    )(slot, shard_arr, queries, pool, full_norms)
    arrived = [here, shift_by(right, 1), shift_by(far, 2), shift_by(left, 3)]

    low_coef, low_row, low_col, low_loss = pl.pallas_call(
        partial(low_kernel, bounds, rows),
        out_shape=[
            pltpu.HBM((levels, total_rows, cands), F32),
            pltpu.HBM((blocks, 8, rows), F32),
            pltpu.HBM((blocks, 8, cands), F32),
            jax.ShapeDtypeStruct((blocks, rows), F32),
        ],
        in_specs=[smem(), smem()] + [vmem()] * 5,
        out_specs=[hbm()] * 3 + [vmem()],
        scratch_shapes=[
            pltpu.VMEM((2, count, PBLK, width), BF16),
            pltpu.VMEM((2, levels, rows, cands), F32),
            pltpu.VMEM((levels, total_rows, cands), F32),
            pltpu.VMEM((blocks, 8, rows), F32),
            pltpu.VMEM((blocks, 8, cands), F32),
            pltpu.SemaphoreType.DMA(()),
            pltpu.SemaphoreType.DMA(()),
            pltpu.SemaphoreType.DMA(()),
        ],
        compiler_params=params(),
        name="low",
    )(slot, shard_arr, queries, pool, norm_rows_of, ids, pos)
    *coefs, high_loss = pl.pallas_call(
        partial(high_kernel, shards, per_shard, rows, [size / MINP for size in high_sizes]),
        out_shape=[jax.ShapeDtypeStruct((base + COEF_AUX, cands), BF16)] * shards
        + [jax.ShapeDtypeStruct((1, base), F32)],
        in_specs=[smem()] + [vmem()] * 2 + [hbm()] + [vmem()] * shards,
        out_specs=[vmem()] * (shards + 1),
        compiler_params=params(),
        name="high",
    )(shard_arr, ids, pos, pinned(low_row), *arrived)
    coefs = [coefs[0]] + [shift_by(coefs[s], s) for s in range(1, shards)]

    half_shape = (levels, total_rows, cands)
    slot_grad, half, row_table = pl.pallas_call(
        partial(passage_kernel, bounds, shards, per_shard, rows),
        out_shape=[pltpu.HBM(pool_shape, BF16), pltpu.HBM(half_shape, BF16), pltpu.HBM((blocks, 8, rows), F32)],
        in_specs=[smem(), smem()] + [vmem()] * 3 + [hbm()] * 3 + [vmem()] * shards,
        out_specs=[hbm()] * 3,
        scratch_shapes=[
            pltpu.VMEM((total_rows, cands), BF16),
            pltpu.VMEM((blocks, 8, rows), F32),
            pltpu.VMEM((blocks, 1, cands), F32),
            pltpu.VMEM((slots + 1, PBLK, total_rows), BF16),
            pltpu.VMEM((slots + 1, PBLK, width), F32),
            pltpu.VMEM((slots + 1, PBLK, LANES), F32),
            pltpu.VMEM(pool_shape, BF16),
            pltpu.VMEM(half_shape, BF16),
            pltpu.VMEM((blocks, 8, rows), F32),
            pltpu.VMEM((blocks, 8, cands), F32),
            pltpu.VMEM((levels, total_rows, cands), F32),
            pltpu.SemaphoreType.DMA(()),
            pltpu.SemaphoreType.DMA(()),
            pltpu.SemaphoreType.DMA(()),
            pltpu.SemaphoreType.DMA((2,)),
            pltpu.SemaphoreType.DMA((blocks // 2,)),
        ],
        compiler_params=params(),
        name="passage",
    )(
        spare_slot, shard_arr, queries, pool, masked,
        pinned(low_row), pinned(low_col), pinned(low_coef), *coefs,
    )
    back = lax.all_to_all(slot_grad, "dp", split_axis=0, concat_axis=0, tiled=True)

    query_grad, loss = pl.pallas_call(
        partial(query_kernel, bounds, rows, 1.0 / weight_total),
        out_shape=[
            jax.ShapeDtypeStruct((total_rows, width), BF16),
            jax.ShapeDtypeStruct((shards, base), F32),
        ],
        in_specs=[smem(), smem()] + [vmem()] * 5 + [hbm()],
        out_specs=[vmem()] * 2,
        scratch_shapes=[cand_scratch, pltpu.VMEM(half_shape, BF16), pltpu.SemaphoreType.DMA((2,))],
        compiler_params=params(),
        name="query",
    )(slot, shard_arr, queries, pool, row_table, low_loss, high_loss, pinned(half))
    loss = lax.psum(loss, "tensor")

    passage_grad = pl.pallas_call(
        collect_kernel,
        out_shape=jax.ShapeDtypeStruct((local_blocks * PBLK, width), BF16),
        in_specs=[vmem(), hbm()],
        out_specs=vmem(),
        scratch_shapes=[pltpu.VMEM((slots * PBLK, width), BF16), pltpu.SemaphoreType.DMA((2,))],
        compiler_params=params(),
        name="collect",
    )(target, pinned(back.reshape(slots * PBLK, width)))
    return (
        query_grad,
        passage_grad,
        loss.reshape(total_rows),
    )


def solution(mesh):
    return jax.shard_map(
        per_device,
        mesh=mesh,
        in_specs=(P("dp", "tensor"), P("dp", "tensor"), P(), P("dp")),
        out_specs=(P("dp", "tensor"), P("dp", "tensor"), P("dp")),
        check_vma=False,
    )
```

```python
from functools import partial

import jax
import jax.numpy as jnp
from jax import lax
from jax.experimental import pallas as pl
from jax.experimental.pallas import tpu as pltpu
from jax.sharding import PartitionSpec as P

MINP = 64
NPRE = 7
PBLK = 16

EPS = 1e-06
INV_TEMP = 20.0

F32 = jnp.float32
BF16 = jnp.bfloat16

AUX = 8
COEF_AUX = 32
LANES = 128
PIECE = 256
CHUNKS = 4


def vmem():
    return pl.BlockSpec(memory_space=pltpu.VMEM)


def smem():
    return pl.BlockSpec(memory_space=pltpu.SMEM)


def hbm():
    return pl.BlockSpec(memory_space=pltpu.HBM)


def params():
    return pltpu.CompilerParams(vmem_limit_bytes=20 * 2**20)


def contract(a, b, da, db):
    return lax.dot_general(a, b, (((da,), (db,)), ((), ())), preferred_element_type=F32)


def eye(n):
    return lax.broadcasted_iota(jnp.int32, (n, n), 0) == lax.broadcasted_iota(jnp.int32, (n, n), 1)


def to_col(row):
    return jnp.sum(jnp.where(eye(row.shape[1]), row, 0.0), axis=1, keepdims=True)


def to_row(col):
    return jnp.sum(jnp.where(eye(col.shape[0]), col, 0.0), axis=0, keepdims=True)


def square_sums(half):
    wide = half.astype(F32)
    return jnp.sum(wide * wide, axis=1, keepdims=True)


def columns(table):
    table = jnp.concatenate([table, jnp.zeros((8, LANES - table.shape[1]), F32)], axis=1) if table.shape[1] < LANES else table
    return jnp.concatenate([table, jnp.zeros((LANES - 8, table.shape[1]), F32)], axis=0).T


def terms(dots, a, pp_row, live, labels, weight):
    b = jnp.where(live, lax.rsqrt(pp_row + EPS), 0.0)
    scale = (a * INV_TEMP) * b
    logits = dots * scale
    exponent = jnp.where(live, jnp.exp(logits), 0.0)
    total = jnp.sum(exponent, axis=1, keepdims=True)
    gradient = weight * (exponent * (1.0 / total) - labels)
    inner = gradient * logits
    row = jnp.square(a[:, :1]) * jnp.sum(inner, axis=1, keepdims=True)
    col = (b * b) * jnp.sum(inner, axis=0, keepdims=True)
    return gradient * scale, row, col, weight * jnp.log(total), weight * logits


def take_blocks(pool_ref, slot_ref, block, count, out_ref):
    for n in range(count):
        out_ref[n] = pool_ref[slot_ref[block * count + n]]


def pool_norms(pool_ref, norm_ref, bounds):
    step_slots = 4
    rows = step_slots * PBLK
    lane = lax.broadcasted_iota(jnp.int32, (rows, LANES), 1)

    def lane_sum(part):
        return jnp.sum(part, axis=1, keepdims=True)

    def step(i, carry):
        here = pl.ds(i * step_slots, step_slots)
        wide = pool_ref[here].reshape(rows, pool_ref.shape[2]).astype(F32)
        square = wide * wide
        result, before, inside = None, None, None
        for level, (low, high) in enumerate(bounds):
            if high < LANES:
                total = lane_sum(jnp.where(lane < high, square[:, :LANES], 0.0))
            else:
                start = low // LANES * LANES
                parts = [square[:, j : j + LANES] for j in range(start, high, LANES)]
                while len(parts) > 1:
                    parts = [x + y for x, y in zip(parts[::2], parts[1::2])]
                total = lane_sum(parts[0])
                if start:
                    total = total + before
            before = total
            result = jnp.broadcast_to(total, (rows, LANES)) if result is None else jnp.where(lane == level, total, result)
        norm_ref[here] = result.reshape(step_slots, PBLK, LANES)
        return carry

    lax.fori_loop(0, pool_ref.shape[0] // step_slots, step, 0, unroll=4)


def norm_rows(norm_ref, slot_ref, block, count):
    table = jnp.concatenate([norm_ref[slot_ref[block * count + n]] for n in range(count)], axis=0)
    return table.T[:8, :]


def pack_kernel(
    first_ref, lists_hbm, block_hbm, out_hbm, lists_ref, block_ref, row_ref, wanted_ref, lists_sem, in_sem, row_sem, out_sem
):
    load = pltpu.make_async_copy(block_hbm, block_ref, in_sem)
    lists = pltpu.make_async_copy(lists_hbm, lists_ref, lists_sem)
    lists.start()
    load.start()
    lists.wait()
    local = lists_ref[...] - first_ref[0]
    local = jnp.where((local >= 0) & (local < block_ref.shape[0]), local, 0).astype(F32)
    row = jnp.broadcast_to(jnp.max(local, axis=0, keepdims=True), row_ref.shape)
    size = row.shape[1]
    step = 1
    while step < size // out_hbm.shape[0]:
        row = jnp.maximum(row, pltpu.roll(row, size - step, 1))
        step *= 2
    row_ref[...] = row.astype(jnp.int32)
    save = pltpu.make_async_copy(row_ref, wanted_ref, row_sem)
    save.start()
    save.wait()
    load.wait()
    share = size // out_hbm.shape[0]

    def one(d, carry):
        pltpu.make_async_copy(block_ref.at[wanted_ref[0, d * share]], out_hbm.at[d], out_sem).start()
        return carry

    lax.fori_loop(0, out_hbm.shape[0], one, 0, unroll=8)
    pltpu.make_async_copy(out_hbm, out_hbm, out_sem).wait()


def prep_kernel(split, rows, query_ref, full_ref, mask_ref):
    lane = lax.broadcasted_iota(jnp.int32, (rows, LANES), 1)

    def step(block, carry):
        here = pl.ds(block * rows, rows)
        full_ref[block] = to_row(square_sums(query_ref[here, :]))
        first = query_ref[here, :LANES].astype(F32)
        mask_ref[0, here, :] = jnp.where(lane < split, first, 0.0).astype(BF16)
        mask_ref[1, here, :] = jnp.where(lane < split, 0.0, first).astype(BF16)
        return carry

    lax.fori_loop(0, full_ref.shape[0], step, 0)


def dots_kernel(
    bounds, shards, per_shard, rows, shifts, slot_ref, shard_ref, query_ref, pool_ref, full_ref, pp_ref, *refs
):
    outs, (norm_ref, cand_ref) = refs[:-2], refs[-2:]
    pool_norms(pool_ref, norm_ref, bounds)
    count, _, width = cand_ref.shape
    shard = shard_ref[0]
    base = per_shard * rows
    last = len(bounds) - 1
    for shift, out_ref in zip(shifts, outs):
        target = lax.rem(shard + shift, shards)
        for k in range(per_shard):
            block = target * per_shard + k
            take_blocks(pool_ref, slot_ref, block, count, cand_ref)
            query = query_ref[pl.ds(block * rows, rows), :]
            cand = cand_ref[...].reshape(count * PBLK, width)
            out_ref[k * rows : (k + 1) * rows, :] = contract(query, cand, 1, 1)
            pp = norm_rows(norm_ref, slot_ref, block, count)
            pp_ref[block] = pp
            out_ref[base + k : base + k + 1, :] = pp[last : last + 1, :]
            out_ref[base + per_shard : base + per_shard + 1, k * rows : (k + 1) * rows] = full_ref[block]


def prefix_dots(bounds, rows, block, query_ref, cand_ref):
    here = pl.ds(block * rows, rows)
    cands = cand_ref.shape[0] * PBLK
    lane = lax.broadcasted_iota(jnp.int32, (rows, LANES), 1)
    first = query_ref[here, :LANES]
    short = jnp.where(lane < bounds[0][1], first.astype(F32), 0.0).astype(BF16)
    both = contract(
        jnp.concatenate([short, first], axis=0), cand_ref[:, :, :LANES].reshape(cands, LANES), 1, 1
    )
    yield both[:rows]
    dots = both[rows:]
    yield dots
    for low, high in bounds[2:]:
        dots = dots + contract(query_ref[here, low:high], cand_ref[:, :, low:high].reshape(cands, high - low), 1, 1)
        yield dots


def low_kernel(
    bounds, rows, slot_ref, shard_ref, query_ref, pool_ref, pp_ref, ids_ref, pos_ref,
    coef_hbm, row_hbm, col_hbm, loss_ref, cand_ref, term_ref, coef_ref, row_ref, col_ref, sem, row_sem, col_sem,
):
    count = cand_ref.shape[1]
    levels, _, cands = coef_ref.shape
    blocks = loss_ref.shape[0]

    @pl.when(shard_ref[0] == 0)
    def _():
        row_ref[...] = jnp.zeros_like(row_ref)
        col_ref[...] = jnp.zeros_like(col_ref)

        def one(block, cand_ref, term_ref):
            here = pl.ds(block * rows, rows)
            take_blocks(pool_ref, slot_ref, block, count, cand_ref)
            pp = pp_ref[block]
            ids = ids_ref[pl.ds(block, 1), :]
            live = ids >= 0.0
            labels = jnp.where(ids == to_col(pos_ref[pl.ds(block, 1), :]), 1.0, 0.0)
            qq = jnp.zeros((rows, 1), F32)
            entropy = jnp.zeros((rows, 1), F32)
            logit_sum = jnp.zeros((rows, cands), F32)
            row_terms, col_terms = [], []
            sums = prefix_dots(bounds, rows, block, query_ref, cand_ref)
            for level, ((low, high), dots) in enumerate(zip(bounds, sums)):
                qq = qq + square_sums(query_ref[here, low:high])
                coef, row, col, part, logits = terms(
                    dots, lax.rsqrt(qq + EPS), pp[level : level + 1, :], live, labels, float(high // MINP)
                )
                term_ref[level] = coef
                row_terms.append(row)
                col_terms.append(col)
                entropy = entropy + part
                logit_sum = logit_sum + logits
            loss = entropy - jnp.sum(labels * logit_sum, axis=1, keepdims=True)
            coef = jnp.zeros((rows, cands), F32)
            row = jnp.zeros((rows, 1), F32)
            col = jnp.zeros((1, cands), F32)
            for level in reversed(range(levels)):
                coef = coef + term_ref[level]
                row = row + row_terms[level]
                col = col + col_terms[level]
                coef_ref[level, here, :] = coef
                row_ref[block, level : level + 1, :] = to_row(row)
                col_ref[block, level : level + 1, :] = col
            loss_ref[pl.ds(block, 1), :] = to_row(loss)

        def step(pair, carry):
            for j in range(2):
                one(pair * 2 + j, cand_ref.at[j], term_ref.at[j])
            here = pl.ds(pair * 2 * rows, 2 * rows)
            pltpu.make_async_copy(coef_ref.at[:, here], coef_hbm.at[:, here], sem).start()
            return carry

        lax.fori_loop(0, blocks // 2, step, 0)
        copies = [
            pltpu.make_async_copy(row_ref, row_hbm, row_sem),
            pltpu.make_async_copy(col_ref, col_hbm, col_sem),
        ]
        for copy in copies:
            copy.start()
        for copy in copies:
            copy.wait()
        pltpu.make_async_copy(coef_ref, coef_hbm, sem).wait()

    @pl.when(shard_ref[0] != 0)
    def _():
        loss_ref[...] = jnp.zeros_like(loss_ref)


def high_kernel(shards, per_shard, rows, weights, shard_ref, ids_ref, pos_ref, after_ref, *refs):
    del after_ref
    ins, outs, loss_ref = refs[:shards], refs[shards:-1], refs[-1]
    shard = shard_ref[0]
    base = per_shard * rows
    width = ids_ref.shape[1]
    in_half = [
        jnp.where(lax.rem(shard - shift + shards, shards) < shards // 2, 1.0, 0.0)
        for shift in range(shards)
    ]

    def total(span, keep):
        pieces = [ref[span, :] * scale if keep else ref[span, :] for ref, scale in zip(ins, in_half)]
        return (pieces[0] + pieces[1]) + (pieces[2] + pieces[3])

    below = slice(base, base + AUX)
    half_rows, half_cols, full_rows, full_cols, losses, coefs = [], [], [], [], [], []
    aux_half, aux_full = total(below, True), total(below, False)
    for k in range(per_shard):
        block = shard * per_shard + k
        ids = ids_ref[pl.ds(block, 1), :]
        live = ids >= 0.0
        labels = jnp.where(ids == to_col(pos_ref[pl.ds(block, 1), :]), 1.0, 0.0)
        span = slice(k * rows, (k + 1) * rows)
        results = []
        for keep, aux, weight in ((True, aux_half, weights[0]), (False, aux_full, weights[1])):
            scale = to_col(lax.rsqrt(aux[per_shard : per_shard + 1, span] + EPS))
            results.append(terms(total(span, keep), scale, aux[k : k + 1, :], live, labels, weight))
        (coef_h, row_h, col_h, part_h, logit_h), (coef_f, row_f, col_f, part_f, logit_f) = results
        loss = part_h + part_f - jnp.sum(labels * (logit_h + logit_f), axis=1, keepdims=True)
        coefs.append(((coef_h + coef_f).astype(BF16), coef_f.astype(BF16)))
        half_rows.append(to_row(row_h + row_f))
        full_rows.append(to_row(row_f))
        half_cols.append(col_h + col_f)
        full_cols.append(col_f)
        losses.append(to_row(loss))
    loss_ref[...] = jnp.concatenate(losses, axis=1)

    def aux_rows(rows_list, cols_list):
        line = jnp.concatenate(rows_list + [jnp.zeros((1, width - base), F32)], axis=1)
        table = jnp.concatenate(cols_list + [line], axis=0)
        table = jnp.concatenate([table, jnp.zeros((AUX - table.shape[0], width), F32)], axis=0)
        first = table.astype(BF16).astype(F32)
        second = (table - first).astype(BF16).astype(F32)
        third = table - first - second
        return jnp.concatenate([first, second, third, jnp.zeros_like(table)], axis=0).astype(BF16)

    aux = (aux_rows(half_rows, half_cols), aux_rows(full_rows, full_cols))
    for shift in range(shards):
        out_ref = outs[shift]
        high_target = lax.rem(shard + shift, shards) >= shards // 2
        for which, chosen in ((1, high_target), (0, jnp.logical_not(high_target))):

            @pl.when(chosen)
            def _():
                for k in range(per_shard):
                    out_ref[k * rows : (k + 1) * rows, :] = coefs[k][which]
                out_ref[base : base + COEF_AUX, :] = aux[which]


def unpack_aux(ref, base):
    packed = ref[base : base + COEF_AUX, :].astype(F32)
    return packed[:AUX] + packed[AUX : 2 * AUX] + packed[2 * AUX : 3 * AUX]


def stage_kernel(shard_ref, row_hbm, col_hbm, coef_hbm, after_ref, row_ref, col_ref, coef_ref, sem):
    del after_ref

    @pl.when(shard_ref[0] == 0)
    def _():
        copies = [
            pltpu.make_async_copy(source, target, sem.at[i])
            for i, (source, target) in enumerate(((row_hbm, row_ref), (col_hbm, col_ref), (coef_hbm, coef_ref)))
        ]
        for copy in copies:
            copy.start()
        for copy in copies:
            copy.wait()


def passage_kernel(
    bounds, shards, per_shard, rows, slot_ref, shard_ref, query_ref, pool_ref, mask_ref, low_row_ref, low_col_ref,
    low_coef_ref, *refs
):
    ins = refs[:shards]
    out_hbm, half_hbm, row_hbm, coef_ref, row_ref, col_ref, spread_ref, sum_ref, scale_ref, out_ref, half_ref = refs[shards:-3]
    out_sem, half_sem, row_sem = refs[-3:]
    shard = shard_ref[0]
    base = per_shard * rows
    blocks = shards * per_shard
    slots, _, width = pool_ref.shape
    cands = coef_ref.shape[1]
    count = cands // PBLK

    pairs = blocks // 2

    def pair_rows(pair):
        return pl.ds(pair * 2 * rows, 2 * rows)

    row_copy = pltpu.make_async_copy(row_ref, row_hbm, row_sem)

    @pl.when(shard == 0)
    def _():
        sum_ref[...] = jnp.zeros_like(sum_ref)

    scale_ref[...] = jnp.zeros_like(scale_ref)
    for shift in range(shards):
        source = lax.rem(shard - shift + shards, shards)
        coef_ref[pl.ds(source * base, base), :] = ins[shift][:base, :]
        aux = unpack_aux(ins[shift], base)
        for k in range(per_shard):
            col_ref[source * per_shard + k] = aux[k : k + 1, :]
            line = aux[per_shard : per_shard + 1, k * rows : (k + 1) * rows]
            row_ref[source * per_shard + k] = jnp.broadcast_to(line, (8, rows))

    def add_scales(block, low):
        cols = jnp.broadcast_to(col_ref[block], (8, cands))
        if low:
            cols = cols + low_col_ref[block]
        col_cols = columns(cols)
        for n in range(count):
            slot = slot_ref[block * count + n]
            scale_ref[slot] = scale_ref[slot] + col_cols[n * PBLK : (n + 1) * PBLK, :]

    def send(start, end):
        done = pl.ds(start, end - start)
        pltpu.make_async_copy(out_ref.at[:, :, done], out_hbm.at[:, :, done], out_sem).start()

    @pl.when(shard == 0)
    def _():
        levels = len(bounds)
        row_ref[...] = row_ref[...] + low_row_ref[...]
        row_copy.start()

        def one(block):
            here = pl.ds(block * rows, rows)
            add_scales(block, True)
            base_coef = coef_ref[here, :].astype(F32)
            coefs = [(base_coef + low_coef_ref[level, here, :]).astype(BF16) for level in range(levels)]
            for level in range(levels):
                half_ref[level, here, :] = coefs[level]
            grads = [contract(coefs[0], mask_ref[0, here, :], 0, 0) + contract(coefs[1], mask_ref[1, here, :], 0, 0)]
            starts = [0]
            for level in range(2, levels):
                lo, hi = bounds[level]
                grads.append(contract(coefs[level], query_ref[here, lo:hi], 0, 0))
                starts.append(lo)
            for n in range(count):
                slot = slot_ref[block * count + n]
                for start, grad in zip(starts, grads):
                    lanes = slice(start, start + grad.shape[1])
                    sum_ref[slot, :, lanes] = sum_ref[slot, :, lanes] + grad[n * PBLK : (n + 1) * PBLK, :]

        for pair in range(pairs):
            for j in range(2):
                one(pair * 2 + j)
            here = pair_rows(pair)
            pltpu.make_async_copy(half_ref.at[:, here], half_hbm.at[:, here], half_sem).start()
        copy = pltpu.make_async_copy(half_ref, half_hbm, half_sem)
        level_of = lax.broadcasted_iota(jnp.int32, (LANES, width), 0)
        column = lax.broadcasted_iota(jnp.int32, (LANES, width), 1)
        member = jnp.zeros((LANES, width), F32)
        for level, (lo, hi) in enumerate(bounds):
            member = jnp.where((level_of == level) & (column >= lo) & (column < hi), 1.0, member)
        member = member.astype(BF16)
        step_slots = slots // CHUNKS
        for chunk in range(CHUNKS):
            part = slice(chunk * step_slots, (chunk + 1) * step_slots)
            scale = scale_ref[part].reshape(step_slots * PBLK, LANES)
            high = scale.astype(BF16)
            rest = scale - high.astype(F32)
            middle = rest.astype(BF16)
            low = (rest - middle.astype(F32)).astype(BF16)
            wide = contract(high, member, 1, 0) + contract(middle, member, 1, 0) + contract(low, member, 1, 0)
            pool = pool_ref[part].reshape(step_slots * PBLK, width).astype(F32)
            total = sum_ref[part].reshape(step_slots * PBLK, width)
            out_ref[part] = (total - wide * pool).astype(BF16).reshape(step_slots, PBLK, width)
            pltpu.make_async_copy(out_ref.at[part], out_hbm.at[part], out_sem).start()
        copy.wait()
        row_copy.wait()
        pltpu.make_async_copy(out_ref, out_hbm, out_sem).wait()

    @pl.when(shard != 0)
    def _():
        row_copy.start()
        copy = pltpu.make_async_copy(coef_ref, half_hbm.at[0], half_sem)
        copy.start()
        spread_ref[...] = jnp.zeros_like(spread_ref)
        for block in range(blocks):
            add_scales(block, False)
            turned = coef_ref[pl.ds(block * rows, rows), :].astype(F32).T.astype(BF16)
            for n in range(count):
                spread_ref[slot_ref[block * count + n], :, block * rows : (block + 1) * rows] = turned[
                    n * PBLK : (n + 1) * PBLK, :
                ]
        spread = spread_ref[0:slots].reshape(slots * PBLK, blocks * rows)
        scale = scale_ref[0:slots].reshape(slots * PBLK, LANES)[:, 0:1]
        for start in range(0, width, PIECE):
            end = start + PIECE
            grad = contract(spread, query_ref[:, start:end], 1, 0)
            pool = pool_ref[:, :, start:end].reshape(slots * PBLK, end - start).astype(F32)
            out_ref[:, :, start:end] = (grad - scale * pool).astype(BF16).reshape(slots, PBLK, end - start)
            send(start, end)
        copy.wait()
        row_copy.wait()
        pltpu.make_async_copy(out_ref, out_hbm, out_sem).wait()


def query_kernel(
    bounds, rows, loss_scale, slot_ref, shard_ref, query_ref, pool_ref, row_ref, low_loss_ref, high_loss_ref, half_hbm,
    query_grad_ref, loss_ref, cand_ref, half_ref, sem,
):
    shard = shard_ref[0]
    blocks, cands = low_loss_ref.shape[0], half_ref.shape[2]
    count = cand_ref.shape[0]
    width = query_ref.shape[1]
    per_line = LANES // rows
    first = pltpu.make_async_copy(half_hbm.at[0], half_ref.at[0], sem.at[0])
    rest = pl.ds(1, half_ref.shape[0] - 1)
    others = pltpu.make_async_copy(half_hbm.at[rest], half_ref.at[rest], sem.at[1])
    first.start()

    @pl.when(shard == 0)
    def _():
        others.start()

    for block in range(blocks):
        j = block % per_line
        loss_ref[block // per_line : block // per_line + 1, j * rows : (j + 1) * rows] = low_loss_ref[block : block + 1, :]
    loss_ref[pl.ds(shard, 1), :] = loss_ref[pl.ds(shard, 1), :] + high_loss_ref[...]
    loss_ref[...] = loss_ref[...] * loss_scale

    def run(spans):
        def step(block, carry):
            take_blocks(pool_ref, slot_ref, block, count, cand_ref)
            row_cols = columns(row_ref[block])
            here = pl.ds(block * rows, rows)
            for level, (lo, hi) in enumerate(spans):
                query = query_ref[here, lo:hi].astype(F32)
                cand = cand_ref[:, :, lo:hi].reshape(cands, hi - lo)
                grad = contract(half_ref[level, here, :], cand, 1, 0) - row_cols[:rows, level : level + 1] * query
                query_grad_ref[here, lo:hi] = grad.astype(BF16)
            return carry

        lax.fori_loop(0, blocks, step, 0)

    first.wait()

    @pl.when(shard == 0)
    def _():
        others.wait()
        run(bounds)

    @pl.when(shard != 0)
    def _():
        run([(0, width)])


def collect_kernel(target_ref, back_hbm, out_ref, back_ref, sem):
    rows = out_ref.shape[0]
    size = back_ref.shape[0] // 2
    copies = []
    for half in range(2):
        part = pl.ds(half * size, size)
        copies.append(pltpu.make_async_copy(back_hbm.at[part], back_ref.at[part], sem.at[half]))
        copies[-1].start()
    here = lax.broadcasted_iota(jnp.int32, (rows, size), 0)
    total = None
    for half in range(2):
        part = slice(half * size, (half + 1) * size)
        choose = jnp.where(here == target_ref[:, part], 1.0, 0.0).astype(BF16)
        copies[half].wait()
        grad = contract(choose, back_ref[part, :], 1, 0)
        total = grad if total is None else total + grad
    out_ref[...] = total.astype(BF16)


def per_device(queries, passages, neg_lists, positives):
    peers = lax.axis_size("dp")
    shards = lax.axis_size("tensor")
    total_rows, width = queries.shape
    blocks = neg_lists.shape[0] // peers
    count = neg_lists.shape[1]
    rows = total_rows // blocks
    local_blocks = passages.shape[0] // PBLK
    cands = count * PBLK
    per_shard = blocks // shards
    base = per_shard * rows
    slots = peers
    my_index = lax.axis_index("dp")
    shard = lax.axis_index("tensor")
    sizes = [MINP * 2**level for level in range(NPRE)]
    low_sizes = [size for size in sizes if size <= width]
    high_sizes = [size for size in sizes if size > width]
    assert high_sizes == [width * shards // 2, width * shards] and low_sizes[-1] == width
    assert shards == 4 and base == LANES
    bounds = list(zip([0] + low_sizes[:-1], low_sizes))
    levels = len(bounds)
    weight_total = sum(size / MINP for size in sizes)

    flat = neg_lists.reshape(peers, blocks * count)
    mine = (flat >= 0) & (flat // local_blocks == my_index)
    wanted = jnp.max(jnp.where(mine, flat % local_blocks, -1), axis=1)
    own = lax.dynamic_slice_in_dim(neg_lists, my_index * blocks, blocks, 0)
    valid = own >= 0
    slot = jnp.where(valid, own // local_blocks, 0).reshape(blocks * count)
    spare_slot = jnp.where(valid, own // local_blocks, slots).reshape(blocks * count)
    within = jnp.arange(PBLK, dtype=jnp.int32)
    ids = jnp.where(valid[:, :, None], own[:, :, None] * PBLK + within[None, None, :], -1)
    ids = ids.reshape(blocks, cands).astype(F32)
    target = jnp.where(wanted[:, None] >= 0, wanted[:, None] * PBLK + within[None, :], -1).reshape(1, slots * PBLK)
    pos = positives.reshape(blocks, rows).astype(F32)
    shard_arr = shard.reshape(1).astype(jnp.int32)
    pool_shape = (slots, PBLK, width)

    pinned = partial(pltpu.with_memory_space_constraint, memory_space=pltpu.HBM)
    panels = pl.pallas_call(
        pack_kernel,
        out_shape=pltpu.HBM(pool_shape, BF16),
        in_specs=[smem(), hbm(), hbm()],
        out_specs=hbm(),
        scratch_shapes=[
            pltpu.VMEM((count, neg_lists.shape[0]), jnp.int32),
            pltpu.VMEM((local_blocks, PBLK, width), BF16),
            pltpu.VMEM((8, neg_lists.shape[0]), jnp.int32),
            pltpu.SMEM((8, neg_lists.shape[0]), jnp.int32),
            pltpu.SemaphoreType.DMA(()),
            pltpu.SemaphoreType.DMA(()),
            pltpu.SemaphoreType.DMA(()),
            pltpu.SemaphoreType.DMA(()),
        ],
        compiler_params=params(),
        name="pack",
    )(
        (my_index * local_blocks).reshape(1).astype(jnp.int32), pinned(neg_lists.T),
        pinned(passages.reshape(local_blocks, PBLK, width)),
    )
    pool = lax.all_to_all(panels, "dp", split_axis=0, concat_axis=0, tiled=True)
    full_norms, masked = pl.pallas_call(
        partial(prep_kernel, bounds[0][1], rows),
        out_shape=[
            jax.ShapeDtypeStruct((blocks, 1, rows), F32),
            jax.ShapeDtypeStruct((2, total_rows, LANES), BF16),
        ],
        in_specs=[vmem()],
        out_specs=[vmem()] * 2,
        compiler_params=params(),
        name="prep",
    )(queries)

    def shift_by(part, s):
        return lax.ppermute(part, "tensor", [(i, (i + s) % shards) for i in range(shards)])

    cand_scratch = pltpu.VMEM((count, PBLK, width), BF16)
    message = jax.ShapeDtypeStruct((base + AUX, cands), F32)
    norm_rows_of, far, right, left, here = pl.pallas_call(
        partial(dots_kernel, bounds, shards, per_shard, rows, (2, 1, 3, 0)),
        out_shape=[jax.ShapeDtypeStruct((blocks, 8, cands), F32)] + [message] * shards,
        in_specs=[smem(), smem(), vmem(), vmem(), vmem()],
        out_specs=[vmem()] * (shards + 1),
        scratch_shapes=[pltpu.VMEM((slots, PBLK, LANES), F32), cand_scratch],
        compiler_params=params(),
        name="dots",
    )(slot, shard_arr, queries, pool, full_norms)
    arrived = [here, shift_by(right, 1), shift_by(far, 2), shift_by(left, 3)]

    low_coef, low_row, low_col, low_loss = pl.pallas_call(
        partial(low_kernel, bounds, rows),
        out_shape=[
            pltpu.HBM((levels, total_rows, cands), F32),
            pltpu.HBM((blocks, 8, rows), F32),
            pltpu.HBM((blocks, 8, cands), F32),
            jax.ShapeDtypeStruct((blocks, rows), F32),
        ],
        in_specs=[smem(), smem()] + [vmem()] * 5,
        out_specs=[hbm()] * 3 + [vmem()],
        scratch_shapes=[
            pltpu.VMEM((2, count, PBLK, width), BF16),
            pltpu.VMEM((2, levels, rows, cands), F32),
            pltpu.VMEM((levels, total_rows, cands), F32),
            pltpu.VMEM((blocks, 8, rows), F32),
            pltpu.VMEM((blocks, 8, cands), F32),
            pltpu.SemaphoreType.DMA(()),
            pltpu.SemaphoreType.DMA(()),
            pltpu.SemaphoreType.DMA(()),
        ],
        compiler_params=params(),
        name="low",
    )(slot, shard_arr, queries, pool, norm_rows_of, ids, pos)
    *coefs, high_loss = pl.pallas_call(
        partial(high_kernel, shards, per_shard, rows, [size / MINP for size in high_sizes]),
        out_shape=[jax.ShapeDtypeStruct((base + COEF_AUX, cands), BF16)] * shards
        + [jax.ShapeDtypeStruct((1, base), F32)],
        in_specs=[smem()] + [vmem()] * 2 + [hbm()] + [vmem()] * shards,
        out_specs=[vmem()] * (shards + 1),
        compiler_params=params(),
        name="high",
    )(shard_arr, ids, pos, pinned(low_row), *arrived)
    staged_row, staged_col, staged_coef = pl.pallas_call(
        stage_kernel,
        out_shape=[
            jax.ShapeDtypeStruct((blocks, 8, rows), F32),
            jax.ShapeDtypeStruct((blocks, 8, cands), F32),
            jax.ShapeDtypeStruct((levels, total_rows, cands), F32),
        ],
        in_specs=[smem()] + [hbm()] * 3 + [pl.BlockSpec(memory_space=pl.ANY)],
        out_specs=[vmem()] * 3,
        scratch_shapes=[pltpu.SemaphoreType.DMA((3,))],
        compiler_params=params(),
        name="stage",
    )(shard_arr, pinned(low_row), pinned(low_col), pinned(low_coef), high_loss)
    coefs = [coefs[0]] + [shift_by(coefs[s], s) for s in range(1, shards)]

    half_shape = (levels, total_rows, cands)
    slot_grad, half, row_table = pl.pallas_call(
        partial(passage_kernel, bounds, shards, per_shard, rows),
        out_shape=[pltpu.HBM(pool_shape, BF16), pltpu.HBM(half_shape, BF16), pltpu.HBM((blocks, 8, rows), F32)],
        in_specs=[smem(), smem()] + [vmem()] * (6 + shards),
        out_specs=[hbm()] * 3,
        scratch_shapes=[
            pltpu.VMEM((total_rows, cands), BF16),
            pltpu.VMEM((blocks, 8, rows), F32),
            pltpu.VMEM((blocks, 1, cands), F32),
            pltpu.VMEM((slots + 1, PBLK, total_rows), BF16),
            pltpu.VMEM((slots + 1, PBLK, width), F32),
            pltpu.VMEM((slots + 1, PBLK, LANES), F32),
            pltpu.VMEM(pool_shape, BF16),
            pltpu.VMEM(half_shape, BF16),
            pltpu.SemaphoreType.DMA(()),
            pltpu.SemaphoreType.DMA(()),
            pltpu.SemaphoreType.DMA(()),
        ],
        compiler_params=params(),
        name="passage",
    )(
        spare_slot, shard_arr, queries, pool, masked,
        staged_row, staged_col, staged_coef, *coefs,
    )
    back = lax.all_to_all(slot_grad, "dp", split_axis=0, concat_axis=0, tiled=True)

    query_grad, loss = pl.pallas_call(
        partial(query_kernel, bounds, rows, 1.0 / weight_total),
        out_shape=[
            jax.ShapeDtypeStruct((total_rows, width), BF16),
            jax.ShapeDtypeStruct((shards, base), F32),
        ],
        in_specs=[smem(), smem()] + [vmem()] * 5 + [hbm()],
        out_specs=[vmem()] * 2,
        scratch_shapes=[cand_scratch, pltpu.VMEM(half_shape, BF16), pltpu.SemaphoreType.DMA((2,))],
        compiler_params=params(),
        name="query",
    )(slot, shard_arr, queries, pool, row_table, low_loss, high_loss, pinned(half))
    loss = lax.psum(loss, "tensor")

    passage_grad = pl.pallas_call(
        collect_kernel,
        out_shape=jax.ShapeDtypeStruct((local_blocks * PBLK, width), BF16),
        in_specs=[vmem(), hbm()],
        out_specs=vmem(),
        scratch_shapes=[pltpu.VMEM((slots * PBLK, width), BF16), pltpu.SemaphoreType.DMA((2,))],
        compiler_params=params(),
        name="collect",
    )(target, pinned(back.reshape(slots * PBLK, width)))
    return (
        query_grad,
        passage_grad,
        loss.reshape(total_rows),
    )


def solution(mesh):
    return jax.shard_map(
        per_device,
        mesh=mesh,
        in_specs=(P("dp", "tensor"), P("dp", "tensor"), P(), P("dp")),
        out_specs=(P("dp", "tensor"), P("dp", "tensor"), P("dp")),
        check_vma=False,
    )
```

```python
from functools import partial

import jax
import jax.numpy as jnp
from jax import lax
from jax.experimental import pallas as pl
from jax.experimental.pallas import tpu as pltpu
from jax.sharding import PartitionSpec as P

MINP = 64
NPRE = 7
PBLK = 16

EPS = 1e-06
INV_TEMP = 20.0

F32 = jnp.float32
BF16 = jnp.bfloat16

AUX = 8
COEF_AUX = 32
LANES = 128
PIECE = 256
CHUNKS = 4


def vmem():
    return pl.BlockSpec(memory_space=pltpu.VMEM)


def smem():
    return pl.BlockSpec(memory_space=pltpu.SMEM)


def hbm():
    return pl.BlockSpec(memory_space=pltpu.HBM)


def params():
    return pltpu.CompilerParams(vmem_limit_bytes=20 * 2**20)


def contract(a, b, da, db):
    return lax.dot_general(a, b, (((da,), (db,)), ((), ())), preferred_element_type=F32)


def eye(n):
    return lax.broadcasted_iota(jnp.int32, (n, n), 0) == lax.broadcasted_iota(jnp.int32, (n, n), 1)


def to_col(row):
    return jnp.sum(jnp.where(eye(row.shape[1]), row, 0.0), axis=1, keepdims=True)


def to_row(col):
    return jnp.sum(jnp.where(eye(col.shape[0]), col, 0.0), axis=0, keepdims=True)


def square_sums(half):
    wide = half.astype(F32)
    return jnp.sum(wide * wide, axis=1, keepdims=True)


def columns(table):
    table = jnp.concatenate([table, jnp.zeros((8, LANES - table.shape[1]), F32)], axis=1) if table.shape[1] < LANES else table
    return jnp.concatenate([table, jnp.zeros((LANES - 8, table.shape[1]), F32)], axis=0).T


def terms(dots, a, pp_row, live, labels, weight):
    b = jnp.where(live, lax.rsqrt(pp_row + EPS), 0.0)
    scale = (a * INV_TEMP) * b
    logits = dots * scale
    exponent = jnp.where(live, jnp.exp(logits), 0.0)
    total = jnp.sum(exponent, axis=1, keepdims=True)
    gradient = weight * (exponent * (1.0 / total) - labels)
    inner = gradient * logits
    row = jnp.square(a[:, :1]) * jnp.sum(inner, axis=1, keepdims=True)
    col = (b * b) * jnp.sum(inner, axis=0, keepdims=True)
    return gradient * scale, row, col, weight * jnp.log(total), weight * logits


def take_blocks(pool_ref, slot_ref, block, count, out_ref):
    for n in range(count):
        out_ref[n] = pool_ref[slot_ref[block * count + n]]


def pool_norms(pool_ref, norm_ref, bounds):
    step_slots = 4
    rows = step_slots * PBLK
    lane = lax.broadcasted_iota(jnp.int32, (rows, LANES), 1)

    def lane_sum(part):
        return jnp.sum(part, axis=1, keepdims=True)

    def step(i):
        here = slice(i * step_slots, (i + 1) * step_slots)
        wide = pool_ref[here].reshape(rows, pool_ref.shape[2]).astype(F32)
        square = wide * wide
        result, before, inside = None, None, None
        for level, (low, high) in enumerate(bounds):
            if high < LANES:
                total = lane_sum(jnp.where(lane < high, square[:, :LANES], 0.0))
            else:
                start = low // LANES * LANES
                parts = [square[:, j : j + LANES] for j in range(start, high, LANES)]
                while len(parts) > 1:
                    parts = [x + y for x, y in zip(parts[::2], parts[1::2])]
                total = lane_sum(parts[0])
                if start:
                    total = total + before
            before = total
            result = jnp.broadcast_to(total, (rows, LANES)) if result is None else jnp.where(lane == level, total, result)
        norm_ref[here] = result.reshape(step_slots, PBLK, LANES)

    for i in range(pool_ref.shape[0] // step_slots):
        step(i)


def norm_rows(norm_ref, slot_ref, block, count):
    table = jnp.concatenate([norm_ref[slot_ref[block * count + n]] for n in range(count)], axis=0)
    return table.T[:8, :]


def pack_kernel(
    first_ref, lists_hbm, block_hbm, out_hbm, lists_ref, block_ref, row_ref, wanted_ref, lists_sem, in_sem, row_sem, out_sem
):
    load = pltpu.make_async_copy(block_hbm, block_ref, in_sem)
    lists = pltpu.make_async_copy(lists_hbm, lists_ref, lists_sem)
    lists.start()
    load.start()
    lists.wait()
    local = lists_ref[...] - first_ref[0]
    local = jnp.where((local >= 0) & (local < block_ref.shape[0]), local, 0).astype(F32)
    row = jnp.broadcast_to(jnp.max(local, axis=0, keepdims=True), row_ref.shape)
    size = row.shape[1]
    step = 1
    while step < size // out_hbm.shape[0]:
        row = jnp.maximum(row, pltpu.roll(row, size - step, 1))
        step *= 2
    row_ref[...] = row.astype(jnp.int32)
    save = pltpu.make_async_copy(row_ref, wanted_ref, row_sem)
    save.start()
    save.wait()
    load.wait()
    share = size // out_hbm.shape[0]

    def one(d, carry):
        pltpu.make_async_copy(block_ref.at[wanted_ref[0, d * share]], out_hbm.at[d], out_sem).start()
        return carry

    lax.fori_loop(0, out_hbm.shape[0], one, 0, unroll=8)
    pltpu.make_async_copy(out_hbm, out_hbm, out_sem).wait()


def prep_kernel(split, rows, query_ref, full_ref, mask_ref):
    lane = lax.broadcasted_iota(jnp.int32, (rows, LANES), 1)

    def step(block, carry):
        here = pl.ds(block * rows, rows)
        full_ref[block] = to_row(square_sums(query_ref[here, :]))
        first = query_ref[here, :LANES].astype(F32)
        mask_ref[0, here, :] = jnp.where(lane < split, first, 0.0).astype(BF16)
        mask_ref[1, here, :] = jnp.where(lane < split, 0.0, first).astype(BF16)
        return carry

    lax.fori_loop(0, full_ref.shape[0], step, 0)


def dots_kernel(
    bounds, shards, per_shard, rows, shifts, slot_ref, shard_ref, query_ref, pool_ref, full_ref, pp_ref, *refs
):
    outs, (norm_ref, cand_ref) = refs[:-2], refs[-2:]
    pool_norms(pool_ref, norm_ref, bounds)
    count, _, width = cand_ref.shape
    shard = shard_ref[0]
    base = per_shard * rows
    last = len(bounds) - 1
    for shift, out_ref in zip(shifts, outs):
        target = lax.rem(shard + shift, shards)
        for k in range(per_shard):
            block = target * per_shard + k
            take_blocks(pool_ref, slot_ref, block, count, cand_ref)
            query = query_ref[pl.ds(block * rows, rows), :]
            cand = cand_ref[...].reshape(count * PBLK, width)
            out_ref[k * rows : (k + 1) * rows, :] = contract(query, cand, 1, 1)
            pp = norm_rows(norm_ref, slot_ref, block, count)
            pp_ref[block] = pp
            out_ref[base + k : base + k + 1, :] = pp[last : last + 1, :]
            out_ref[base + per_shard : base + per_shard + 1, k * rows : (k + 1) * rows] = full_ref[block]


def prefix_dots(bounds, rows, block, query_ref, cand_ref):
    here = pl.ds(block * rows, rows)
    cands = cand_ref.shape[0] * PBLK
    lane = lax.broadcasted_iota(jnp.int32, (rows, LANES), 1)
    first = query_ref[here, :LANES]
    short = jnp.where(lane < bounds[0][1], first.astype(F32), 0.0).astype(BF16)
    both = contract(
        jnp.concatenate([short, first], axis=0), cand_ref[:, :, :LANES].reshape(cands, LANES), 1, 1
    )
    yield both[:rows]
    dots = both[rows:]
    yield dots
    for low, high in bounds[2:]:
        dots = dots + contract(query_ref[here, low:high], cand_ref[:, :, low:high].reshape(cands, high - low), 1, 1)
        yield dots


def low_kernel(
    bounds, rows, slot_ref, shard_ref, query_ref, pool_ref, pp_ref, ids_ref, pos_ref,
    coef_hbm, row_hbm, col_hbm, loss_ref, cand_ref, term_ref, coef_ref, row_ref, col_ref, sem, row_sem, col_sem,
):
    count = cand_ref.shape[1]
    levels, _, cands = coef_ref.shape
    blocks = loss_ref.shape[0]

    @pl.when(shard_ref[0] == 0)
    def _():
        row_ref[...] = jnp.zeros_like(row_ref)
        col_ref[...] = jnp.zeros_like(col_ref)

        def one(block, cand_ref, term_ref):
            here = pl.ds(block * rows, rows)
            take_blocks(pool_ref, slot_ref, block, count, cand_ref)
            pp = pp_ref[block]
            ids = ids_ref[pl.ds(block, 1), :]
            live = ids >= 0.0
            labels = jnp.where(ids == to_col(pos_ref[pl.ds(block, 1), :]), 1.0, 0.0)
            qq = jnp.zeros((rows, 1), F32)
            entropy = jnp.zeros((rows, 1), F32)
            logit_sum = jnp.zeros((rows, cands), F32)
            row_terms, col_terms = [], []
            sums = prefix_dots(bounds, rows, block, query_ref, cand_ref)
            for level, ((low, high), dots) in enumerate(zip(bounds, sums)):
                qq = qq + square_sums(query_ref[here, low:high])
                coef, row, col, part, logits = terms(
                    dots, lax.rsqrt(qq + EPS), pp[level : level + 1, :], live, labels, float(high // MINP)
                )
                term_ref[level] = coef
                row_terms.append(row)
                col_terms.append(col)
                entropy = entropy + part
                logit_sum = logit_sum + logits
            loss = entropy - jnp.sum(labels * logit_sum, axis=1, keepdims=True)
            coef = jnp.zeros((rows, cands), F32)
            row = jnp.zeros((rows, 1), F32)
            col = jnp.zeros((1, cands), F32)
            for level in reversed(range(levels)):
                coef = coef + term_ref[level]
                row = row + row_terms[level]
                col = col + col_terms[level]
                coef_ref[level, here, :] = coef
                row_ref[block, level : level + 1, :] = to_row(row)
                col_ref[block, level : level + 1, :] = col
            loss_ref[pl.ds(block, 1), :] = to_row(loss)

        def step(pair, carry):
            for j in range(2):
                one(pair * 2 + j, cand_ref.at[j], term_ref.at[j])
            here = pl.ds(pair * 2 * rows, 2 * rows)
            pltpu.make_async_copy(coef_ref.at[:, here], coef_hbm.at[:, here], sem).start()
            return carry

        lax.fori_loop(0, blocks // 2, step, 0)
        copies = [
            pltpu.make_async_copy(row_ref, row_hbm, row_sem),
            pltpu.make_async_copy(col_ref, col_hbm, col_sem),
        ]
        for copy in copies:
            copy.start()
        for copy in copies:
            copy.wait()
        pltpu.make_async_copy(coef_ref, coef_hbm, sem).wait()

    @pl.when(shard_ref[0] != 0)
    def _():
        loss_ref[...] = jnp.zeros_like(loss_ref)


def high_kernel(shards, per_shard, rows, weights, shard_ref, ids_ref, pos_ref, after_ref, *refs):
    del after_ref
    ins, outs, loss_ref = refs[:shards], refs[shards:-1], refs[-1]
    shard = shard_ref[0]
    base = per_shard * rows
    width = ids_ref.shape[1]
    in_half = [
        jnp.where(lax.rem(shard - shift + shards, shards) < shards // 2, 1.0, 0.0)
        for shift in range(shards)
    ]

    def total(span, keep):
        pieces = [ref[span, :] * scale if keep else ref[span, :] for ref, scale in zip(ins, in_half)]
        return (pieces[0] + pieces[1]) + (pieces[2] + pieces[3])

    below = slice(base, base + AUX)
    half_rows, half_cols, full_rows, full_cols, losses, coefs = [], [], [], [], [], []
    aux_half, aux_full = total(below, True), total(below, False)
    for k in range(per_shard):
        block = shard * per_shard + k
        ids = ids_ref[pl.ds(block, 1), :]
        live = ids >= 0.0
        labels = jnp.where(ids == to_col(pos_ref[pl.ds(block, 1), :]), 1.0, 0.0)
        span = slice(k * rows, (k + 1) * rows)
        results = []
        for keep, aux, weight in ((True, aux_half, weights[0]), (False, aux_full, weights[1])):
            scale = to_col(lax.rsqrt(aux[per_shard : per_shard + 1, span] + EPS))
            results.append(terms(total(span, keep), scale, aux[k : k + 1, :], live, labels, weight))
        (coef_h, row_h, col_h, part_h, logit_h), (coef_f, row_f, col_f, part_f, logit_f) = results
        loss = part_h + part_f - jnp.sum(labels * (logit_h + logit_f), axis=1, keepdims=True)
        coefs.append(((coef_h + coef_f).astype(BF16), coef_f.astype(BF16)))
        half_rows.append(to_row(row_h + row_f))
        full_rows.append(to_row(row_f))
        half_cols.append(col_h + col_f)
        full_cols.append(col_f)
        losses.append(to_row(loss))
    loss_ref[...] = jnp.concatenate(losses, axis=1)

    def aux_rows(rows_list, cols_list):
        line = jnp.concatenate(rows_list + [jnp.zeros((1, width - base), F32)], axis=1)
        table = jnp.concatenate(cols_list + [line], axis=0)
        table = jnp.concatenate([table, jnp.zeros((AUX - table.shape[0], width), F32)], axis=0)
        first = table.astype(BF16).astype(F32)
        second = (table - first).astype(BF16).astype(F32)
        third = table - first - second
        return jnp.concatenate([first, second, third, jnp.zeros_like(table)], axis=0).astype(BF16)

    aux = (aux_rows(half_rows, half_cols), aux_rows(full_rows, full_cols))
    for shift in range(shards):
        out_ref = outs[shift]
        high_target = lax.rem(shard + shift, shards) >= shards // 2
        for which, chosen in ((1, high_target), (0, jnp.logical_not(high_target))):

            @pl.when(chosen)
            def _():
                for k in range(per_shard):
                    out_ref[k * rows : (k + 1) * rows, :] = coefs[k][which]
                out_ref[base : base + COEF_AUX, :] = aux[which]


def unpack_aux(ref, base):
    packed = ref[base : base + COEF_AUX, :].astype(F32)
    return packed[:AUX] + packed[AUX : 2 * AUX] + packed[2 * AUX : 3 * AUX]


def stage_kernel(shard_ref, row_hbm, col_hbm, coef_hbm, after_ref, row_ref, col_ref, coef_ref, sem):
    del after_ref

    @pl.when(shard_ref[0] == 0)
    def _():
        copies = [
            pltpu.make_async_copy(source, target, sem.at[i])
            for i, (source, target) in enumerate(((row_hbm, row_ref), (col_hbm, col_ref), (coef_hbm, coef_ref)))
        ]
        for copy in copies:
            copy.start()
        for copy in copies:
            copy.wait()


def passage_kernel(
    bounds, shards, per_shard, rows, slot_ref, shard_ref, query_ref, pool_ref, mask_ref, low_row_ref, low_col_ref,
    low_coef_ref, *refs
):
    ins = refs[:shards]
    out_hbm, half_hbm, row_hbm, coef_ref, row_ref, col_ref, spread_ref, sum_ref, scale_ref, out_ref, half_ref = refs[shards:-3]
    out_sem, half_sem, row_sem = refs[-3:]
    shard = shard_ref[0]
    base = per_shard * rows
    blocks = shards * per_shard
    slots, _, width = pool_ref.shape
    cands = coef_ref.shape[1]
    count = cands // PBLK

    pairs = blocks // 2

    def pair_rows(pair):
        return pl.ds(pair * 2 * rows, 2 * rows)

    row_copy = pltpu.make_async_copy(row_ref, row_hbm, row_sem)

    @pl.when(shard == 0)
    def _():
        sum_ref[...] = jnp.zeros_like(sum_ref)

    scale_ref[...] = jnp.zeros_like(scale_ref)
    for shift in range(shards):
        source = lax.rem(shard - shift + shards, shards)
        coef_ref[pl.ds(source * base, base), :] = ins[shift][:base, :]
        aux = unpack_aux(ins[shift], base)
        for k in range(per_shard):
            col_ref[source * per_shard + k] = aux[k : k + 1, :]
            line = aux[per_shard : per_shard + 1, k * rows : (k + 1) * rows]
            row_ref[source * per_shard + k] = jnp.broadcast_to(line, (8, rows))

    def add_scales(block, low):
        cols = jnp.broadcast_to(col_ref[block], (8, cands))
        if low:
            cols = cols + low_col_ref[block]
        col_cols = columns(cols)
        for n in range(count):
            slot = slot_ref[block * count + n]
            scale_ref[slot] = scale_ref[slot] + col_cols[n * PBLK : (n + 1) * PBLK, :]

    def send(start, end):
        done = pl.ds(start, end - start)
        pltpu.make_async_copy(out_ref.at[:, :, done], out_hbm.at[:, :, done], out_sem).start()

    @pl.when(shard == 0)
    def _():
        levels = len(bounds)
        row_ref[...] = row_ref[...] + low_row_ref[...]
        row_copy.start()

        def one(block):
            here = pl.ds(block * rows, rows)
            add_scales(block, True)
            base_coef = coef_ref[here, :].astype(F32)
            coefs = [(base_coef + low_coef_ref[level, here, :]).astype(BF16) for level in range(levels)]
            for level in range(levels):
                half_ref[level, here, :] = coefs[level]
            grads = [contract(coefs[0], mask_ref[0, here, :], 0, 0) + contract(coefs[1], mask_ref[1, here, :], 0, 0)]
            starts = [0]
            for level in range(2, levels):
                lo, hi = bounds[level]
                grads.append(contract(coefs[level], query_ref[here, lo:hi], 0, 0))
                starts.append(lo)
            for n in range(count):
                slot = slot_ref[block * count + n]
                for start, grad in zip(starts, grads):
                    lanes = slice(start, start + grad.shape[1])
                    sum_ref[slot, :, lanes] = sum_ref[slot, :, lanes] + grad[n * PBLK : (n + 1) * PBLK, :]

        for pair in range(pairs):
            for j in range(2):
                one(pair * 2 + j)
            here = pair_rows(pair)
            pltpu.make_async_copy(half_ref.at[:, here], half_hbm.at[:, here], half_sem).start()
        copy = pltpu.make_async_copy(half_ref, half_hbm, half_sem)
        level_of = lax.broadcasted_iota(jnp.int32, (LANES, width), 0)
        column = lax.broadcasted_iota(jnp.int32, (LANES, width), 1)
        member = jnp.zeros((LANES, width), F32)
        for level, (lo, hi) in enumerate(bounds):
            member = jnp.where((level_of == level) & (column >= lo) & (column < hi), 1.0, member)
        member = member.astype(BF16)
        step_slots = slots // CHUNKS
        for chunk in range(CHUNKS):
            part = slice(chunk * step_slots, (chunk + 1) * step_slots)
            scale = scale_ref[part].reshape(step_slots * PBLK, LANES)
            high = scale.astype(BF16)
            rest = scale - high.astype(F32)
            middle = rest.astype(BF16)
            low = (rest - middle.astype(F32)).astype(BF16)
            wide = contract(high, member, 1, 0) + contract(middle, member, 1, 0) + contract(low, member, 1, 0)
            pool = pool_ref[part].reshape(step_slots * PBLK, width).astype(F32)
            total = sum_ref[part].reshape(step_slots * PBLK, width)
            out_ref[part] = (total - wide * pool).astype(BF16).reshape(step_slots, PBLK, width)
            pltpu.make_async_copy(out_ref.at[part], out_hbm.at[part], out_sem).start()
        copy.wait()
        row_copy.wait()
        pltpu.make_async_copy(out_ref, out_hbm, out_sem).wait()

    @pl.when(shard != 0)
    def _():
        row_copy.start()
        copy = pltpu.make_async_copy(coef_ref, half_hbm.at[0], half_sem)
        copy.start()
        spread_ref[...] = jnp.zeros_like(spread_ref)
        for block in range(blocks):
            add_scales(block, False)
            turned = coef_ref[pl.ds(block * rows, rows), :].astype(F32).T.astype(BF16)
            for n in range(count):
                spread_ref[slot_ref[block * count + n], :, block * rows : (block + 1) * rows] = turned[
                    n * PBLK : (n + 1) * PBLK, :
                ]
        spread = spread_ref[0:slots].reshape(slots * PBLK, blocks * rows)
        scale = scale_ref[0:slots].reshape(slots * PBLK, LANES)[:, 0:1]
        for start in range(0, width, PIECE):
            end = start + PIECE
            grad = contract(spread, query_ref[:, start:end], 1, 0)
            pool = pool_ref[:, :, start:end].reshape(slots * PBLK, end - start).astype(F32)
            out_ref[:, :, start:end] = (grad - scale * pool).astype(BF16).reshape(slots, PBLK, end - start)
            send(start, end)
        copy.wait()
        row_copy.wait()
        pltpu.make_async_copy(out_ref, out_hbm, out_sem).wait()


def query_kernel(
    bounds, rows, loss_scale, slot_ref, shard_ref, query_ref, pool_ref, row_ref, low_loss_ref, high_loss_ref, half_hbm,
    query_grad_ref, loss_ref, cand_ref, half_ref, sem,
):
    shard = shard_ref[0]
    blocks, cands = low_loss_ref.shape[0], half_ref.shape[2]
    count = cand_ref.shape[0]
    width = query_ref.shape[1]
    per_line = LANES // rows
    first = pltpu.make_async_copy(half_hbm.at[0], half_ref.at[0], sem.at[0])
    rest = pl.ds(1, half_ref.shape[0] - 1)
    others = pltpu.make_async_copy(half_hbm.at[rest], half_ref.at[rest], sem.at[1])
    first.start()

    @pl.when(shard == 0)
    def _():
        others.start()

    for block in range(blocks):
        j = block % per_line
        loss_ref[block // per_line : block // per_line + 1, j * rows : (j + 1) * rows] = low_loss_ref[block : block + 1, :]
    loss_ref[pl.ds(shard, 1), :] = loss_ref[pl.ds(shard, 1), :] + high_loss_ref[...]
    loss_ref[...] = loss_ref[...] * loss_scale

    def run(spans):
        def step(block, carry):
            take_blocks(pool_ref, slot_ref, block, count, cand_ref)
            row_cols = columns(row_ref[block])
            here = pl.ds(block * rows, rows)
            for level, (lo, hi) in enumerate(spans):
                query = query_ref[here, lo:hi].astype(F32)
                cand = cand_ref[:, :, lo:hi].reshape(cands, hi - lo)
                grad = contract(half_ref[level, here, :], cand, 1, 0) - row_cols[:rows, level : level + 1] * query
                query_grad_ref[here, lo:hi] = grad.astype(BF16)
            return carry

        lax.fori_loop(0, blocks, step, 0)

    first.wait()

    @pl.when(shard == 0)
    def _():
        others.wait()
        run(bounds)

    @pl.when(shard != 0)
    def _():
        run([(0, width)])


def collect_kernel(target_ref, back_hbm, out_ref, back_ref, sem):
    rows = out_ref.shape[0]
    size = back_ref.shape[0] // 2
    copies = []
    for half in range(2):
        part = pl.ds(half * size, size)
        copies.append(pltpu.make_async_copy(back_hbm.at[part], back_ref.at[part], sem.at[half]))
        copies[-1].start()
    here = lax.broadcasted_iota(jnp.int32, (rows, size), 0)
    total = None
    for half in range(2):
        part = slice(half * size, (half + 1) * size)
        choose = jnp.where(here == target_ref[:, part], 1.0, 0.0).astype(BF16)
        copies[half].wait()
        grad = contract(choose, back_ref[part, :], 1, 0)
        total = grad if total is None else total + grad
    out_ref[...] = total.astype(BF16)


def per_device(queries, passages, neg_lists, positives):
    peers = lax.axis_size("dp")
    shards = lax.axis_size("tensor")
    total_rows, width = queries.shape
    blocks = neg_lists.shape[0] // peers
    count = neg_lists.shape[1]
    rows = total_rows // blocks
    local_blocks = passages.shape[0] // PBLK
    cands = count * PBLK
    per_shard = blocks // shards
    base = per_shard * rows
    slots = peers
    my_index = lax.axis_index("dp")
    shard = lax.axis_index("tensor")
    sizes = [MINP * 2**level for level in range(NPRE)]
    low_sizes = [size for size in sizes if size <= width]
    high_sizes = [size for size in sizes if size > width]
    assert high_sizes == [width * shards // 2, width * shards] and low_sizes[-1] == width
    assert shards == 4 and base == LANES
    bounds = list(zip([0] + low_sizes[:-1], low_sizes))
    levels = len(bounds)
    weight_total = sum(size / MINP for size in sizes)

    flat = neg_lists.reshape(peers, blocks * count)
    mine = (flat >= 0) & (flat // local_blocks == my_index)
    wanted = jnp.max(jnp.where(mine, flat % local_blocks, -1), axis=1)
    own = lax.dynamic_slice_in_dim(neg_lists, my_index * blocks, blocks, 0)
    valid = own >= 0
    slot = jnp.where(valid, own // local_blocks, 0).reshape(blocks * count)
    spare_slot = jnp.where(valid, own // local_blocks, slots).reshape(blocks * count)
    within = jnp.arange(PBLK, dtype=jnp.int32)
    ids = jnp.where(valid[:, :, None], own[:, :, None] * PBLK + within[None, None, :], -1)
    ids = ids.reshape(blocks, cands).astype(F32)
    target = jnp.where(wanted[:, None] >= 0, wanted[:, None] * PBLK + within[None, :], -1).reshape(1, slots * PBLK)
    pos = positives.reshape(blocks, rows).astype(F32)
    shard_arr = shard.reshape(1).astype(jnp.int32)
    pool_shape = (slots, PBLK, width)

    pinned = partial(pltpu.with_memory_space_constraint, memory_space=pltpu.HBM)
    panels = pl.pallas_call(
        pack_kernel,
        out_shape=pltpu.HBM(pool_shape, BF16),
        in_specs=[smem(), hbm(), hbm()],
        out_specs=hbm(),
        scratch_shapes=[
            pltpu.VMEM((count, neg_lists.shape[0]), jnp.int32),
            pltpu.VMEM((local_blocks, PBLK, width), BF16),
            pltpu.VMEM((8, neg_lists.shape[0]), jnp.int32),
            pltpu.SMEM((8, neg_lists.shape[0]), jnp.int32),
            pltpu.SemaphoreType.DMA(()),
            pltpu.SemaphoreType.DMA(()),
            pltpu.SemaphoreType.DMA(()),
            pltpu.SemaphoreType.DMA(()),
        ],
        compiler_params=params(),
        name="pack",
    )(
        (my_index * local_blocks).reshape(1).astype(jnp.int32), pinned(neg_lists.T),
        pinned(passages.reshape(local_blocks, PBLK, width)),
    )
    pool = lax.all_to_all(panels, "dp", split_axis=0, concat_axis=0, tiled=True)
    full_norms, masked = pl.pallas_call(
        partial(prep_kernel, bounds[0][1], rows),
        out_shape=[
            jax.ShapeDtypeStruct((blocks, 1, rows), F32),
            jax.ShapeDtypeStruct((2, total_rows, LANES), BF16),
        ],
        in_specs=[vmem()],
        out_specs=[vmem()] * 2,
        compiler_params=params(),
        name="prep",
    )(queries)

    def shift_by(part, s):
        return lax.ppermute(part, "tensor", [(i, (i + s) % shards) for i in range(shards)])

    cand_scratch = pltpu.VMEM((count, PBLK, width), BF16)
    message = jax.ShapeDtypeStruct((base + AUX, cands), F32)
    norm_rows_of, far, right, left, here = pl.pallas_call(
        partial(dots_kernel, bounds, shards, per_shard, rows, (2, 1, 3, 0)),
        out_shape=[jax.ShapeDtypeStruct((blocks, 8, cands), F32)] + [message] * shards,
        in_specs=[smem(), smem(), vmem(), vmem(), vmem()],
        out_specs=[vmem()] * (shards + 1),
        scratch_shapes=[pltpu.VMEM((slots, PBLK, LANES), F32), cand_scratch],
        compiler_params=params(),
        name="dots",
    )(slot, shard_arr, queries, pool, full_norms)
    arrived = [here, shift_by(right, 1), shift_by(far, 2), shift_by(left, 3)]

    low_coef, low_row, low_col, low_loss = pl.pallas_call(
        partial(low_kernel, bounds, rows),
        out_shape=[
            pltpu.HBM((levels, total_rows, cands), F32),
            pltpu.HBM((blocks, 8, rows), F32),
            pltpu.HBM((blocks, 8, cands), F32),
            jax.ShapeDtypeStruct((blocks, rows), F32),
        ],
        in_specs=[smem(), smem()] + [vmem()] * 5,
        out_specs=[hbm()] * 3 + [vmem()],
        scratch_shapes=[
            pltpu.VMEM((2, count, PBLK, width), BF16),
            pltpu.VMEM((2, levels, rows, cands), F32),
            pltpu.VMEM((levels, total_rows, cands), F32),
            pltpu.VMEM((blocks, 8, rows), F32),
            pltpu.VMEM((blocks, 8, cands), F32),
            pltpu.SemaphoreType.DMA(()),
            pltpu.SemaphoreType.DMA(()),
            pltpu.SemaphoreType.DMA(()),
        ],
        compiler_params=params(),
        name="low",
    )(slot, shard_arr, queries, pool, norm_rows_of, ids, pos)
    *coefs, high_loss = pl.pallas_call(
        partial(high_kernel, shards, per_shard, rows, [size / MINP for size in high_sizes]),
        out_shape=[jax.ShapeDtypeStruct((base + COEF_AUX, cands), BF16)] * shards
        + [jax.ShapeDtypeStruct((1, base), F32)],
        in_specs=[smem()] + [vmem()] * 2 + [hbm()] + [vmem()] * shards,
        out_specs=[vmem()] * (shards + 1),
        compiler_params=params(),
        name="high",
    )(shard_arr, ids, pos, pinned(low_row), *arrived)
    staged_row, staged_col, staged_coef = pl.pallas_call(
        stage_kernel,
        out_shape=[
            jax.ShapeDtypeStruct((blocks, 8, rows), F32),
            jax.ShapeDtypeStruct((blocks, 8, cands), F32),
            jax.ShapeDtypeStruct((levels, total_rows, cands), F32),
        ],
        in_specs=[smem()] + [hbm()] * 3 + [pl.BlockSpec(memory_space=pl.ANY)],
        out_specs=[vmem()] * 3,
        scratch_shapes=[pltpu.SemaphoreType.DMA((3,))],
        compiler_params=params(),
        name="stage",
    )(shard_arr, pinned(low_row), pinned(low_col), pinned(low_coef), high_loss)
    coefs = [coefs[0]] + [shift_by(coefs[s], s) for s in range(1, shards)]

    half_shape = (levels, total_rows, cands)
    slot_grad, half, row_table = pl.pallas_call(
        partial(passage_kernel, bounds, shards, per_shard, rows),
        out_shape=[pltpu.HBM(pool_shape, BF16), pltpu.HBM(half_shape, BF16), pltpu.HBM((blocks, 8, rows), F32)],
        in_specs=[smem(), smem()] + [vmem()] * (6 + shards),
        out_specs=[hbm()] * 3,
        scratch_shapes=[
            pltpu.VMEM((total_rows, cands), BF16),
            pltpu.VMEM((blocks, 8, rows), F32),
            pltpu.VMEM((blocks, 1, cands), F32),
            pltpu.VMEM((slots + 1, PBLK, total_rows), BF16),
            pltpu.VMEM((slots + 1, PBLK, width), F32),
            pltpu.VMEM((slots + 1, PBLK, LANES), F32),
            pltpu.VMEM(pool_shape, BF16),
            pltpu.VMEM(half_shape, BF16),
            pltpu.SemaphoreType.DMA(()),
            pltpu.SemaphoreType.DMA(()),
            pltpu.SemaphoreType.DMA(()),
        ],
        compiler_params=params(),
        name="passage",
    )(
        spare_slot, shard_arr, queries, pool, masked,
        staged_row, staged_col, staged_coef, *coefs,
    )
    back = lax.all_to_all(slot_grad, "dp", split_axis=0, concat_axis=0, tiled=True)

    query_grad, loss = pl.pallas_call(
        partial(query_kernel, bounds, rows, 1.0 / weight_total),
        out_shape=[
            jax.ShapeDtypeStruct((total_rows, width), BF16),
            jax.ShapeDtypeStruct((shards, base), F32),
        ],
        in_specs=[smem(), smem()] + [vmem()] * 5 + [hbm()],
        out_specs=[vmem()] * 2,
        scratch_shapes=[cand_scratch, pltpu.VMEM(half_shape, BF16), pltpu.SemaphoreType.DMA((2,))],
        compiler_params=params(),
        name="query",
    )(slot, shard_arr, queries, pool, row_table, low_loss, high_loss, pinned(half))
    loss = lax.psum(loss, "tensor")

    passage_grad = pl.pallas_call(
        collect_kernel,
        out_shape=jax.ShapeDtypeStruct((local_blocks * PBLK, width), BF16),
        in_specs=[vmem(), hbm()],
        out_specs=vmem(),
        scratch_shapes=[pltpu.VMEM((slots * PBLK, width), BF16), pltpu.SemaphoreType.DMA((2,))],
        compiler_params=params(),
        name="collect",
    )(target, pinned(back.reshape(slots * PBLK, width)))
    return (
        query_grad,
        passage_grad,
        loss.reshape(total_rows),
    )


def solution(mesh):
    return jax.shard_map(
        per_device,
        mesh=mesh,
        in_specs=(P("dp", "tensor"), P("dp", "tensor"), P(), P("dp")),
        out_specs=(P("dp", "tensor"), P("dp", "tensor"), P("dp")),
        check_vma=False,
    )
```

```python
from functools import partial

import jax
import jax.numpy as jnp
from jax import lax
from jax.experimental import pallas as pl
from jax.experimental.pallas import tpu as pltpu
from jax.sharding import PartitionSpec as P

MINP = 64
NPRE = 7
PBLK = 16

EPS = 1e-06
INV_TEMP = 20.0

F32 = jnp.float32
BF16 = jnp.bfloat16

AUX = 8
COEF_AUX = 32
LANES = 128
PIECE = 256
CHUNKS = 4


def vmem():
    return pl.BlockSpec(memory_space=pltpu.VMEM)


def smem():
    return pl.BlockSpec(memory_space=pltpu.SMEM)


def hbm():
    return pl.BlockSpec(memory_space=pltpu.HBM)


def params():
    return pltpu.CompilerParams(vmem_limit_bytes=20 * 2**20)


def contract(a, b, da, db):
    return lax.dot_general(a, b, (((da,), (db,)), ((), ())), preferred_element_type=F32)


def eye(n):
    return lax.broadcasted_iota(jnp.int32, (n, n), 0) == lax.broadcasted_iota(jnp.int32, (n, n), 1)


def to_col(row):
    return jnp.sum(jnp.where(eye(row.shape[1]), row, 0.0), axis=1, keepdims=True)


def to_row(col):
    return jnp.sum(jnp.where(eye(col.shape[0]), col, 0.0), axis=0, keepdims=True)


def square_sums(half):
    wide = half.astype(F32)
    return jnp.sum(wide * wide, axis=1, keepdims=True)


def columns(table):
    table = jnp.concatenate([table, jnp.zeros((8, LANES - table.shape[1]), F32)], axis=1) if table.shape[1] < LANES else table
    return jnp.concatenate([table, jnp.zeros((LANES - 8, table.shape[1]), F32)], axis=0).T


def terms(dots, a, pp_row, live, labels, weight):
    b = jnp.where(live, lax.rsqrt(pp_row + EPS), 0.0)
    scale = (a * INV_TEMP) * b
    logits = dots * scale
    exponent = jnp.where(live, jnp.exp(logits), 0.0)
    total = jnp.sum(exponent, axis=1, keepdims=True)
    gradient = weight * (exponent * (1.0 / total) - labels)
    inner = gradient * logits
    row = jnp.square(a[:, :1]) * jnp.sum(inner, axis=1, keepdims=True)
    col = (b * b) * jnp.sum(inner, axis=0, keepdims=True)
    return gradient * scale, row, col, weight * jnp.log(total), weight * logits


def take_blocks(pool_ref, slot_ref, block, count, out_ref):
    for n in range(count):
        out_ref[n] = pool_ref[slot_ref[block * count + n]]


def pool_norms(pool_ref, norm_ref, bounds):
    step_slots = 4
    rows = step_slots * PBLK
    lane = lax.broadcasted_iota(jnp.int32, (rows, LANES), 1)

    def lane_sum(part):
        return jnp.sum(part, axis=1, keepdims=True)

    def step(i):
        here = slice(i * step_slots, (i + 1) * step_slots)
        wide = pool_ref[here].reshape(rows, pool_ref.shape[2]).astype(F32)
        square = wide * wide
        result, before, inside = None, None, None
        for level, (low, high) in enumerate(bounds):
            if high < LANES:
                total = lane_sum(jnp.where(lane < high, square[:, :LANES], 0.0))
            else:
                start = low // LANES * LANES
                parts = [square[:, j : j + LANES] for j in range(start, high, LANES)]
                while len(parts) > 1:
                    parts = [x + y for x, y in zip(parts[::2], parts[1::2])]
                total = lane_sum(parts[0])
                if start:
                    total = total + before
            before = total
            result = jnp.broadcast_to(total, (rows, LANES)) if result is None else jnp.where(lane == level, total, result)
        norm_ref[here] = result.reshape(step_slots, PBLK, LANES)

    for i in range(pool_ref.shape[0] // step_slots):
        step(i)


def norm_rows(norm_ref, slot_ref, block, count):
    table = jnp.concatenate([norm_ref[slot_ref[block * count + n]] for n in range(count)], axis=0)
    return table.T[:8, :]


def pack_kernel(
    first_ref, lists_hbm, block_hbm, out_hbm, lists_ref, block_ref, row_ref, wanted_ref, lists_sem, in_sem, row_sem, out_sem
):
    load = pltpu.make_async_copy(block_hbm, block_ref, in_sem)
    lists = pltpu.make_async_copy(lists_hbm, lists_ref, lists_sem)
    lists.start()
    load.start()
    lists.wait()
    local = lists_ref[...] - first_ref[0]
    local = jnp.where((local >= 0) & (local < block_ref.shape[0]), local, 0).astype(F32)
    row = jnp.broadcast_to(jnp.max(local, axis=0, keepdims=True), row_ref.shape)
    size = row.shape[1]
    step = 1
    while step < size // out_hbm.shape[0]:
        row = jnp.maximum(row, pltpu.roll(row, size - step, 1))
        step *= 2
    row_ref[...] = row.astype(jnp.int32)
    save = pltpu.make_async_copy(row_ref, wanted_ref, row_sem)
    save.start()
    save.wait()
    load.wait()
    share = size // out_hbm.shape[0]

    def one(d, carry):
        pltpu.make_async_copy(block_ref.at[wanted_ref[0, d * share]], out_hbm.at[d], out_sem).start()
        return carry

    lax.fori_loop(0, out_hbm.shape[0], one, 0, unroll=8)
    pltpu.make_async_copy(out_hbm, out_hbm, out_sem).wait()


def prep_kernel(split, rows, query_ref, full_ref, mask_ref):
    lane = lax.broadcasted_iota(jnp.int32, (rows, LANES), 1)

    def step(block, carry):
        here = pl.ds(block * rows, rows)
        full_ref[block] = to_row(square_sums(query_ref[here, :]))
        first = query_ref[here, :LANES].astype(F32)
        mask_ref[0, here, :] = jnp.where(lane < split, first, 0.0).astype(BF16)
        mask_ref[1, here, :] = jnp.where(lane < split, 0.0, first).astype(BF16)
        return carry

    lax.fori_loop(0, full_ref.shape[0], step, 0)


def dots_kernel(
    bounds, shards, per_shard, rows, shifts, slot_ref, shard_ref, query_ref, pool_ref, full_ref, pp_ref, *refs
):
    outs, (norm_ref, cand_ref) = refs[:-2], refs[-2:]
    pool_norms(pool_ref, norm_ref, bounds)
    count, _, width = cand_ref.shape
    shard = shard_ref[0]
    base = per_shard * rows
    last = len(bounds) - 1
    for shift, out_ref in zip(shifts, outs):
        target = lax.rem(shard + shift, shards)
        for k in range(per_shard):
            block = target * per_shard + k
            take_blocks(pool_ref, slot_ref, block, count, cand_ref)
            query = query_ref[pl.ds(block * rows, rows), :]
            cand = cand_ref[...].reshape(count * PBLK, width)
            out_ref[k * rows : (k + 1) * rows, :] = contract(query, cand, 1, 1)
            pp = norm_rows(norm_ref, slot_ref, block, count)
            pp_ref[block] = pp
            out_ref[base + k : base + k + 1, :] = pp[last : last + 1, :]
            out_ref[base + per_shard : base + per_shard + 1, k * rows : (k + 1) * rows] = full_ref[block]


def prefix_dots(bounds, rows, block, query_ref, cand_ref):
    here = pl.ds(block * rows, rows)
    cands = cand_ref.shape[0] * PBLK
    lane = lax.broadcasted_iota(jnp.int32, (rows, LANES), 1)
    first = query_ref[here, :LANES]
    short = jnp.where(lane < bounds[0][1], first.astype(F32), 0.0).astype(BF16)
    both = contract(
        jnp.concatenate([short, first], axis=0), cand_ref[:, :, :LANES].reshape(cands, LANES), 1, 1
    )
    yield both[:rows]
    dots = both[rows:]
    yield dots
    for low, high in bounds[2:]:
        dots = dots + contract(query_ref[here, low:high], cand_ref[:, :, low:high].reshape(cands, high - low), 1, 1)
        yield dots


def low_kernel(
    bounds, rows, slot_ref, shard_ref, query_ref, pool_ref, pp_ref, ids_ref, pos_ref,
    coef_hbm, row_hbm, col_hbm, loss_ref, cand_ref, term_ref, coef_ref, row_ref, col_ref, sem, row_sem, col_sem,
):
    count = cand_ref.shape[1]
    levels, _, cands = coef_ref.shape
    blocks = loss_ref.shape[0]

    @pl.when(shard_ref[0] == 0)
    def _():
        row_ref[...] = jnp.zeros_like(row_ref)
        col_ref[...] = jnp.zeros_like(col_ref)

        def one(block, cand_ref, term_ref):
            here = pl.ds(block * rows, rows)
            take_blocks(pool_ref, slot_ref, block, count, cand_ref)
            pp = pp_ref[block]
            ids = ids_ref[pl.ds(block, 1), :]
            live = ids >= 0.0
            labels = jnp.where(ids == to_col(pos_ref[pl.ds(block, 1), :]), 1.0, 0.0)
            qq = jnp.zeros((rows, 1), F32)
            entropy = jnp.zeros((rows, 1), F32)
            logit_sum = jnp.zeros((rows, cands), F32)
            row_terms, col_terms = [], []
            sums = prefix_dots(bounds, rows, block, query_ref, cand_ref)
            for level, ((low, high), dots) in enumerate(zip(bounds, sums)):
                qq = qq + square_sums(query_ref[here, low:high])
                coef, row, col, part, logits = terms(
                    dots, lax.rsqrt(qq + EPS), pp[level : level + 1, :], live, labels, float(high // MINP)
                )
                term_ref[level] = coef
                row_terms.append(row)
                col_terms.append(col)
                entropy = entropy + part
                logit_sum = logit_sum + logits
            loss = entropy - jnp.sum(labels * logit_sum, axis=1, keepdims=True)
            coef = jnp.zeros((rows, cands), F32)
            row = jnp.zeros((rows, 1), F32)
            col = jnp.zeros((1, cands), F32)
            for level in reversed(range(levels)):
                coef = coef + term_ref[level]
                row = row + row_terms[level]
                col = col + col_terms[level]
                coef_ref[level, here, :] = coef
                row_ref[block, level : level + 1, :] = to_row(row)
                col_ref[block, level : level + 1, :] = col
            loss_ref[pl.ds(block, 1), :] = to_row(loss)

        def step(pair, carry):
            for j in range(2):
                one(pair * 2 + j, cand_ref.at[j], term_ref.at[j])
            here = pl.ds(pair * 2 * rows, 2 * rows)
            pltpu.make_async_copy(coef_ref.at[:, here], coef_hbm.at[:, here], sem).start()
            return carry

        lax.fori_loop(0, blocks // 2, step, 0)
        copies = [
            pltpu.make_async_copy(row_ref, row_hbm, row_sem),
            pltpu.make_async_copy(col_ref, col_hbm, col_sem),
        ]
        for copy in copies:
            copy.start()
        for copy in copies:
            copy.wait()
        pltpu.make_async_copy(coef_ref, coef_hbm, sem).wait()

    @pl.when(shard_ref[0] != 0)
    def _():
        loss_ref[...] = jnp.zeros_like(loss_ref)


def high_kernel(shards, per_shard, rows, weights, shard_ref, ids_ref, pos_ref, after_ref, *refs):
    del after_ref
    ins, outs, loss_ref = refs[:shards], refs[shards:-1], refs[-1]
    shard = shard_ref[0]
    base = per_shard * rows
    width = ids_ref.shape[1]
    in_half = [
        jnp.where(lax.rem(shard - shift + shards, shards) < shards // 2, 1.0, 0.0)
        for shift in range(shards)
    ]

    def total(span, keep):
        pieces = [ref[span, :] * scale if keep else ref[span, :] for ref, scale in zip(ins, in_half)]
        return (pieces[0] + pieces[1]) + (pieces[2] + pieces[3])

    below = slice(base, base + AUX)
    half_rows, half_cols, full_rows, full_cols, losses, coefs = [], [], [], [], [], []
    aux_half, aux_full = total(below, True), total(below, False)
    for k in range(per_shard):
        block = shard * per_shard + k
        ids = ids_ref[pl.ds(block, 1), :]
        live = ids >= 0.0
        labels = jnp.where(ids == to_col(pos_ref[pl.ds(block, 1), :]), 1.0, 0.0)
        span = slice(k * rows, (k + 1) * rows)
        results = []
        for keep, aux, weight in ((True, aux_half, weights[0]), (False, aux_full, weights[1])):
            scale = to_col(lax.rsqrt(aux[per_shard : per_shard + 1, span] + EPS))
            results.append(terms(total(span, keep), scale, aux[k : k + 1, :], live, labels, weight))
        (coef_h, row_h, col_h, part_h, logit_h), (coef_f, row_f, col_f, part_f, logit_f) = results
        loss = part_h + part_f - jnp.sum(labels * (logit_h + logit_f), axis=1, keepdims=True)
        coefs.append(((coef_h + coef_f).astype(BF16), coef_f.astype(BF16)))
        half_rows.append(to_row(row_h + row_f))
        full_rows.append(to_row(row_f))
        half_cols.append(col_h + col_f)
        full_cols.append(col_f)
        losses.append(to_row(loss))
    loss_ref[...] = jnp.concatenate(losses, axis=1)

    def aux_rows(rows_list, cols_list):
        line = jnp.concatenate(rows_list + [jnp.zeros((1, width - base), F32)], axis=1)
        table = jnp.concatenate(cols_list + [line], axis=0)
        table = jnp.concatenate([table, jnp.zeros((AUX - table.shape[0], width), F32)], axis=0)
        first = table.astype(BF16).astype(F32)
        second = (table - first).astype(BF16).astype(F32)
        third = table - first - second
        return jnp.concatenate([first, second, third, jnp.zeros_like(table)], axis=0).astype(BF16)

    aux = (aux_rows(half_rows, half_cols), aux_rows(full_rows, full_cols))
    for shift in range(shards):
        out_ref = outs[shift]
        high_target = lax.rem(shard + shift, shards) >= shards // 2
        for which, chosen in ((1, high_target), (0, jnp.logical_not(high_target))):

            @pl.when(chosen)
            def _():
                for k in range(per_shard):
                    out_ref[k * rows : (k + 1) * rows, :] = coefs[k][which]
                out_ref[base : base + COEF_AUX, :] = aux[which]


def unpack_aux(ref, base):
    packed = ref[base : base + COEF_AUX, :].astype(F32)
    return packed[:AUX] + packed[AUX : 2 * AUX] + packed[2 * AUX : 3 * AUX]


def stage_kernel(shard_ref, row_hbm, col_hbm, coef_hbm, after_ref, row_ref, col_ref, coef_ref, sem):
    del after_ref

    @pl.when(shard_ref[0] == 0)
    def _():
        copies = [
            pltpu.make_async_copy(source, target, sem.at[i])
            for i, (source, target) in enumerate(((row_hbm, row_ref), (col_hbm, col_ref), (coef_hbm, coef_ref)))
        ]
        for copy in copies:
            copy.start()
        for copy in copies:
            copy.wait()


def passage_kernel(
    bounds, shards, per_shard, rows, slot_ref, shard_ref, query_ref, pool_ref, mask_ref, low_row_ref, low_col_ref,
    low_coef_ref, *refs
):
    ins = refs[:shards]
    out_hbm, half_hbm, row_hbm, coef_ref, row_ref, col_ref, spread_ref, sum_ref, scale_ref, out_ref, half_ref = refs[shards:-3]
    out_sem, half_sem, row_sem = refs[-3:]
    shard = shard_ref[0]
    base = per_shard * rows
    blocks = shards * per_shard
    slots, _, width = pool_ref.shape
    cands = coef_ref.shape[1]
    count = cands // PBLK

    row_copy = pltpu.make_async_copy(row_ref, row_hbm, row_sem)

    @pl.when(shard == 0)
    def _():
        sum_ref[...] = jnp.zeros_like(sum_ref)

    scale_ref[...] = jnp.zeros_like(scale_ref)
    for shift in range(shards):
        source = lax.rem(shard - shift + shards, shards)
        coef_ref[pl.ds(source * base, base), :] = ins[shift][:base, :]
        aux = unpack_aux(ins[shift], base)
        for k in range(per_shard):
            col_ref[source * per_shard + k] = aux[k : k + 1, :]
            line = aux[per_shard : per_shard + 1, k * rows : (k + 1) * rows]
            row_ref[source * per_shard + k] = jnp.broadcast_to(line, (8, rows))

    def add_scales(block, low):
        cols = jnp.broadcast_to(col_ref[block], (8, cands))
        if low:
            cols = cols + low_col_ref[block]
        col_cols = columns(cols)
        for n in range(count):
            slot = slot_ref[block * count + n]
            scale_ref[slot] = scale_ref[slot] + col_cols[n * PBLK : (n + 1) * PBLK, :]

    def send(start, end):
        done = pl.ds(start, end - start)
        pltpu.make_async_copy(out_ref.at[:, :, done], out_hbm.at[:, :, done], out_sem).start()

    @pl.when(shard == 0)
    def _():
        levels = len(bounds)
        row_ref[...] = row_ref[...] + low_row_ref[...]
        row_copy.start()

        level_of = lax.broadcasted_iota(jnp.int32, (LANES, width), 0)
        column = lax.broadcasted_iota(jnp.int32, (LANES, width), 1)
        member = jnp.zeros((LANES, width), F32)
        for level, (lo, hi) in enumerate(bounds):
            member = jnp.where((level_of == level) & (column >= lo) & (column < hi), 1.0, member)
        member = member.astype(BF16)
        for block in range(blocks):
            add_scales(block, True)
        step_slots = slots // CHUNKS
        for group in (range(levels - 1, levels), range(levels - 1)):
            left, right = bounds[group[0]][0], bounds[group[-1]][1]
            for block in range(blocks):
                here = pl.ds(block * rows, rows)
                base_coef = coef_ref[here, :].astype(F32)
                coefs = {level: (base_coef + low_coef_ref[level, here, :]).astype(BF16) for level in group}
                for level in group:
                    half_ref[level, here, :] = coefs[level]
                grads = []
                if left == 0:
                    first = contract(coefs[0], mask_ref[0, here, :], 0, 0) + contract(coefs[1], mask_ref[1, here, :], 0, 0)
                    grads.append((0, first))
                for level in group:
                    if level >= 2:
                        lo, hi = bounds[level]
                        grads.append((lo, contract(coefs[level], query_ref[here, lo:hi], 0, 0)))
                for n in range(count):
                    slot = slot_ref[block * count + n]
                    for start, grad in grads:
                        lanes = slice(start, start + grad.shape[1])
                        sum_ref[slot, :, lanes] = sum_ref[slot, :, lanes] + grad[n * PBLK : (n + 1) * PBLK, :]
            done = pl.ds(group[0], len(group))
            pltpu.make_async_copy(half_ref.at[done], half_hbm.at[done], half_sem).start()
            for chunk in range(CHUNKS):
                part = slice(chunk * step_slots, (chunk + 1) * step_slots)
                scale = scale_ref[part].reshape(step_slots * PBLK, LANES)
                high = scale.astype(BF16)
                rest = scale - high.astype(F32)
                middle = rest.astype(BF16)
                low = (rest - middle.astype(F32)).astype(BF16)
                side = member[:, left:right]
                wide = contract(high, side, 1, 0) + contract(middle, side, 1, 0) + contract(low, side, 1, 0)
                pool = pool_ref[part, :, left:right].reshape(step_slots * PBLK, right - left).astype(F32)
                total = sum_ref[part, :, left:right].reshape(step_slots * PBLK, right - left)
                out_ref[part, :, left:right] = (total - wide * pool).astype(BF16).reshape(step_slots, PBLK, right - left)
                lanes = pl.ds(left, right - left)
                pltpu.make_async_copy(out_ref.at[part, :, lanes], out_hbm.at[part, :, lanes], out_sem).start()
        pltpu.make_async_copy(half_ref, half_hbm, half_sem).wait()
        row_copy.wait()
        pltpu.make_async_copy(out_ref, out_hbm, out_sem).wait()

    @pl.when(shard != 0)
    def _():
        row_copy.start()
        copy = pltpu.make_async_copy(coef_ref, half_hbm.at[0], half_sem)
        copy.start()
        spread_ref[...] = jnp.zeros_like(spread_ref)
        for block in range(blocks):
            add_scales(block, False)
            turned = coef_ref[pl.ds(block * rows, rows), :].astype(F32).T.astype(BF16)
            for n in range(count):
                spread_ref[slot_ref[block * count + n], :, block * rows : (block + 1) * rows] = turned[
                    n * PBLK : (n + 1) * PBLK, :
                ]
        spread = spread_ref[0:slots].reshape(slots * PBLK, blocks * rows)
        scale = scale_ref[0:slots].reshape(slots * PBLK, LANES)[:, 0:1]
        for start in range(0, width, PIECE):
            end = start + PIECE
            grad = contract(spread, query_ref[:, start:end], 1, 0)
            pool = pool_ref[:, :, start:end].reshape(slots * PBLK, end - start).astype(F32)
            out_ref[:, :, start:end] = (grad - scale * pool).astype(BF16).reshape(slots, PBLK, end - start)
            send(start, end)
        copy.wait()
        row_copy.wait()
        pltpu.make_async_copy(out_ref, out_hbm, out_sem).wait()


def query_kernel(
    bounds, rows, loss_scale, slot_ref, shard_ref, query_ref, pool_ref, row_ref, low_loss_ref, high_loss_ref, half_hbm,
    query_grad_ref, loss_ref, cand_ref, half_ref, sem,
):
    shard = shard_ref[0]
    blocks, cands = low_loss_ref.shape[0], half_ref.shape[2]
    count = cand_ref.shape[0]
    width = query_ref.shape[1]
    per_line = LANES // rows
    first = pltpu.make_async_copy(half_hbm.at[0], half_ref.at[0], sem.at[0])
    rest = pl.ds(1, half_ref.shape[0] - 1)
    others = pltpu.make_async_copy(half_hbm.at[rest], half_ref.at[rest], sem.at[1])
    first.start()

    @pl.when(shard == 0)
    def _():
        others.start()

    for block in range(blocks):
        j = block % per_line
        loss_ref[block // per_line : block // per_line + 1, j * rows : (j + 1) * rows] = low_loss_ref[block : block + 1, :]
    loss_ref[pl.ds(shard, 1), :] = loss_ref[pl.ds(shard, 1), :] + high_loss_ref[...]
    loss_ref[...] = loss_ref[...] * loss_scale

    def run(spans):
        def step(block, carry):
            take_blocks(pool_ref, slot_ref, block, count, cand_ref)
            row_cols = columns(row_ref[block])
            here = pl.ds(block * rows, rows)
            for level, (lo, hi) in enumerate(spans):
                query = query_ref[here, lo:hi].astype(F32)
                cand = cand_ref[:, :, lo:hi].reshape(cands, hi - lo)
                grad = contract(half_ref[level, here, :], cand, 1, 0) - row_cols[:rows, level : level + 1] * query
                query_grad_ref[here, lo:hi] = grad.astype(BF16)
            return carry

        lax.fori_loop(0, blocks, step, 0)

    first.wait()

    @pl.when(shard == 0)
    def _():
        others.wait()
        run(bounds)

    @pl.when(shard != 0)
    def _():
        run([(0, width)])


def collect_kernel(target_ref, back_hbm, out_ref, back_ref, sem):
    rows = out_ref.shape[0]
    size = back_ref.shape[0] // CHUNKS
    copies = []
    for half in range(CHUNKS):
        part = pl.ds(half * size, size)
        copies.append(pltpu.make_async_copy(back_hbm.at[part], back_ref.at[part], sem.at[half]))
        copies[-1].start()
    here = lax.broadcasted_iota(jnp.int32, (rows, size), 0)
    total = None
    for half in range(CHUNKS):
        part = slice(half * size, (half + 1) * size)
        choose = jnp.where(here == target_ref[:, part], 1.0, 0.0).astype(BF16)
        copies[half].wait()
        grad = contract(choose, back_ref[part, :], 1, 0)
        total = grad if total is None else total + grad
    out_ref[...] = total.astype(BF16)


def per_device(queries, passages, neg_lists, positives):
    peers = lax.axis_size("dp")
    shards = lax.axis_size("tensor")
    total_rows, width = queries.shape
    blocks = neg_lists.shape[0] // peers
    count = neg_lists.shape[1]
    rows = total_rows // blocks
    local_blocks = passages.shape[0] // PBLK
    cands = count * PBLK
    per_shard = blocks // shards
    base = per_shard * rows
    slots = peers
    my_index = lax.axis_index("dp")
    shard = lax.axis_index("tensor")
    sizes = [MINP * 2**level for level in range(NPRE)]
    low_sizes = [size for size in sizes if size <= width]
    high_sizes = [size for size in sizes if size > width]
    assert high_sizes == [width * shards // 2, width * shards] and low_sizes[-1] == width
    assert shards == 4 and base == LANES
    bounds = list(zip([0] + low_sizes[:-1], low_sizes))
    levels = len(bounds)
    weight_total = sum(size / MINP for size in sizes)

    flat = neg_lists.reshape(peers, blocks * count)
    mine = (flat >= 0) & (flat // local_blocks == my_index)
    wanted = jnp.max(jnp.where(mine, flat % local_blocks, -1), axis=1)
    own = lax.dynamic_slice_in_dim(neg_lists, my_index * blocks, blocks, 0)
    valid = own >= 0
    slot = jnp.where(valid, own // local_blocks, 0).reshape(blocks * count)
    spare_slot = jnp.where(valid, own // local_blocks, slots).reshape(blocks * count)
    within = jnp.arange(PBLK, dtype=jnp.int32)
    ids = jnp.where(valid[:, :, None], own[:, :, None] * PBLK + within[None, None, :], -1)
    ids = ids.reshape(blocks, cands).astype(F32)
    target = jnp.where(wanted[:, None] >= 0, wanted[:, None] * PBLK + within[None, :], -1).reshape(1, slots * PBLK)
    pos = positives.reshape(blocks, rows).astype(F32)
    shard_arr = shard.reshape(1).astype(jnp.int32)
    pool_shape = (slots, PBLK, width)

    pinned = partial(pltpu.with_memory_space_constraint, memory_space=pltpu.HBM)
    panels = pl.pallas_call(
        pack_kernel,
        out_shape=pltpu.HBM(pool_shape, BF16),
        in_specs=[smem(), hbm(), hbm()],
        out_specs=hbm(),
        scratch_shapes=[
            pltpu.VMEM((count, neg_lists.shape[0]), jnp.int32),
            pltpu.VMEM((local_blocks, PBLK, width), BF16),
            pltpu.VMEM((8, neg_lists.shape[0]), jnp.int32),
            pltpu.SMEM((8, neg_lists.shape[0]), jnp.int32),
            pltpu.SemaphoreType.DMA(()),
            pltpu.SemaphoreType.DMA(()),
            pltpu.SemaphoreType.DMA(()),
            pltpu.SemaphoreType.DMA(()),
        ],
        compiler_params=params(),
        name="pack",
    )(
        (my_index * local_blocks).reshape(1).astype(jnp.int32), pinned(neg_lists.T),
        pinned(passages.reshape(local_blocks, PBLK, width)),
    )
    pool = lax.all_to_all(panels, "dp", split_axis=0, concat_axis=0, tiled=True)
    full_norms, masked = pl.pallas_call(
        partial(prep_kernel, bounds[0][1], rows),
        out_shape=[
            jax.ShapeDtypeStruct((blocks, 1, rows), F32),
            jax.ShapeDtypeStruct((2, total_rows, LANES), BF16),
        ],
        in_specs=[vmem()],
        out_specs=[vmem()] * 2,
        compiler_params=params(),
        name="prep",
    )(queries)

    def shift_by(part, s):
        return lax.ppermute(part, "tensor", [(i, (i + s) % shards) for i in range(shards)])

    cand_scratch = pltpu.VMEM((count, PBLK, width), BF16)
    message = jax.ShapeDtypeStruct((base + AUX, cands), F32)
    norm_rows_of, far, right, left, here = pl.pallas_call(
        partial(dots_kernel, bounds, shards, per_shard, rows, (2, 1, 3, 0)),
        out_shape=[jax.ShapeDtypeStruct((blocks, 8, cands), F32)] + [message] * shards,
        in_specs=[smem(), smem(), vmem(), vmem(), vmem()],
        out_specs=[vmem()] * (shards + 1),
        scratch_shapes=[pltpu.VMEM((slots, PBLK, LANES), F32), cand_scratch],
        compiler_params=params(),
        name="dots",
    )(slot, shard_arr, queries, pool, full_norms)
    arrived = [here, shift_by(right, 1), shift_by(far, 2), shift_by(left, 3)]

    low_coef, low_row, low_col, low_loss = pl.pallas_call(
        partial(low_kernel, bounds, rows),
        out_shape=[
            pltpu.HBM((levels, total_rows, cands), F32),
            pltpu.HBM((blocks, 8, rows), F32),
            pltpu.HBM((blocks, 8, cands), F32),
            jax.ShapeDtypeStruct((blocks, rows), F32),
        ],
        in_specs=[smem(), smem()] + [vmem()] * 5,
        out_specs=[hbm()] * 3 + [vmem()],
        scratch_shapes=[
            pltpu.VMEM((2, count, PBLK, width), BF16),
            pltpu.VMEM((2, levels, rows, cands), F32),
            pltpu.VMEM((levels, total_rows, cands), F32),
            pltpu.VMEM((blocks, 8, rows), F32),
            pltpu.VMEM((blocks, 8, cands), F32),
            pltpu.SemaphoreType.DMA(()),
            pltpu.SemaphoreType.DMA(()),
            pltpu.SemaphoreType.DMA(()),
        ],
        compiler_params=params(),
        name="low",
    )(slot, shard_arr, queries, pool, norm_rows_of, ids, pos)
    *coefs, high_loss = pl.pallas_call(
        partial(high_kernel, shards, per_shard, rows, [size / MINP for size in high_sizes]),
        out_shape=[jax.ShapeDtypeStruct((base + COEF_AUX, cands), BF16)] * shards
        + [jax.ShapeDtypeStruct((1, base), F32)],
        in_specs=[smem()] + [vmem()] * 2 + [hbm()] + [vmem()] * shards,
        out_specs=[vmem()] * (shards + 1),
        compiler_params=params(),
        name="high",
    )(shard_arr, ids, pos, pinned(low_row), *arrived)
    staged_row, staged_col, staged_coef = pl.pallas_call(
        stage_kernel,
        out_shape=[
            jax.ShapeDtypeStruct((blocks, 8, rows), F32),
            jax.ShapeDtypeStruct((blocks, 8, cands), F32),
            jax.ShapeDtypeStruct((levels, total_rows, cands), F32),
        ],
        in_specs=[smem()] + [hbm()] * 3 + [pl.BlockSpec(memory_space=pl.ANY)],
        out_specs=[vmem()] * 3,
        scratch_shapes=[pltpu.SemaphoreType.DMA((3,))],
        compiler_params=params(),
        name="stage",
    )(shard_arr, pinned(low_row), pinned(low_col), pinned(low_coef), high_loss)
    coefs = [coefs[0]] + [shift_by(coefs[s], s) for s in range(1, shards)]

    half_shape = (levels, total_rows, cands)
    slot_grad, half, row_table = pl.pallas_call(
        partial(passage_kernel, bounds, shards, per_shard, rows),
        out_shape=[pltpu.HBM(pool_shape, BF16), pltpu.HBM(half_shape, BF16), pltpu.HBM((blocks, 8, rows), F32)],
        in_specs=[smem(), smem()] + [vmem()] * (6 + shards),
        out_specs=[hbm()] * 3,
        scratch_shapes=[
            pltpu.VMEM((total_rows, cands), BF16),
            pltpu.VMEM((blocks, 8, rows), F32),
            pltpu.VMEM((blocks, 1, cands), F32),
            pltpu.VMEM((slots + 1, PBLK, total_rows), BF16),
            pltpu.VMEM((slots + 1, PBLK, width), F32),
            pltpu.VMEM((slots + 1, PBLK, LANES), F32),
            pltpu.VMEM(pool_shape, BF16),
            pltpu.VMEM(half_shape, BF16),
            pltpu.SemaphoreType.DMA(()),
            pltpu.SemaphoreType.DMA(()),
            pltpu.SemaphoreType.DMA(()),
        ],
        compiler_params=params(),
        name="passage",
    )(
        spare_slot, shard_arr, queries, pool, masked,
        staged_row, staged_col, staged_coef, *coefs,
    )
    back = lax.all_to_all(slot_grad, "dp", split_axis=0, concat_axis=0, tiled=True)

    query_grad, loss = pl.pallas_call(
        partial(query_kernel, bounds, rows, 1.0 / weight_total),
        out_shape=[
            jax.ShapeDtypeStruct((total_rows, width), BF16),
            jax.ShapeDtypeStruct((shards, base), F32),
        ],
        in_specs=[smem(), smem()] + [vmem()] * 5 + [hbm()],
        out_specs=[vmem()] * 2,
        scratch_shapes=[cand_scratch, pltpu.VMEM(half_shape, BF16), pltpu.SemaphoreType.DMA((2,))],
        compiler_params=params(),
        name="query",
    )(slot, shard_arr, queries, pool, row_table, low_loss, high_loss, pinned(half))
    loss = lax.psum(loss, "tensor")

    passage_grad = pl.pallas_call(
        collect_kernel,
        out_shape=jax.ShapeDtypeStruct((local_blocks * PBLK, width), BF16),
        in_specs=[vmem(), hbm()],
        out_specs=vmem(),
        scratch_shapes=[pltpu.VMEM((slots * PBLK, width), BF16), pltpu.SemaphoreType.DMA((CHUNKS,))],
        compiler_params=params(),
        name="collect",
    )(target, pinned(back.reshape(slots * PBLK, width)))
    return (
        query_grad,
        passage_grad,
        loss.reshape(total_rows),
    )


def solution(mesh):
    return jax.shard_map(
        per_device,
        mesh=mesh,
        in_specs=(P("dp", "tensor"), P("dp", "tensor"), P(), P("dp")),
        out_specs=(P("dp", "tensor"), P("dp", "tensor"), P("dp")),
        check_vma=False,
    )
```

```python
from functools import partial

import jax
import jax.numpy as jnp
from jax import lax
from jax.experimental import pallas as pl
from jax.experimental.pallas import tpu as pltpu
from jax.sharding import PartitionSpec as P

MINP = 64
NPRE = 7
PBLK = 16

EPS = 1e-06
INV_TEMP = 20.0

F32 = jnp.float32
BF16 = jnp.bfloat16

AUX = 8
COEF_AUX = 32
LANES = 128
PIECE = 256
CHUNKS = 4


def vmem():
    return pl.BlockSpec(memory_space=pltpu.VMEM)


def smem():
    return pl.BlockSpec(memory_space=pltpu.SMEM)


def hbm():
    return pl.BlockSpec(memory_space=pltpu.HBM)


def params():
    return pltpu.CompilerParams(vmem_limit_bytes=20 * 2**20)


def contract(a, b, da, db):
    return lax.dot_general(a, b, (((da,), (db,)), ((), ())), preferred_element_type=F32)


def eye(n):
    return lax.broadcasted_iota(jnp.int32, (n, n), 0) == lax.broadcasted_iota(jnp.int32, (n, n), 1)


def to_col(row):
    return jnp.sum(jnp.where(eye(row.shape[1]), row, 0.0), axis=1, keepdims=True)


def to_row(col):
    return jnp.sum(jnp.where(eye(col.shape[0]), col, 0.0), axis=0, keepdims=True)


def square_sums(half):
    wide = half.astype(F32)
    return jnp.sum(wide * wide, axis=1, keepdims=True)


def columns(table):
    table = jnp.concatenate([table, jnp.zeros((8, LANES - table.shape[1]), F32)], axis=1) if table.shape[1] < LANES else table
    return jnp.concatenate([table, jnp.zeros((LANES - 8, table.shape[1]), F32)], axis=0).T


def terms(dots, a, pp_row, live, labels, weight):
    b = jnp.where(live, lax.rsqrt(pp_row + EPS), 0.0)
    scale = (a * INV_TEMP) * b
    logits = dots * scale
    exponent = jnp.where(live, jnp.exp(logits), 0.0)
    total = jnp.sum(exponent, axis=1, keepdims=True)
    gradient = weight * (exponent * (1.0 / total) - labels)
    inner = gradient * logits
    row = jnp.square(a[:, :1]) * jnp.sum(inner, axis=1, keepdims=True)
    col = (b * b) * jnp.sum(inner, axis=0, keepdims=True)
    return gradient * scale, row, col, weight * jnp.log(total), weight * logits


def take_blocks(pool_ref, slot_ref, block, count, out_ref):
    for n in range(count):
        out_ref[n] = pool_ref[slot_ref[block * count + n]]


def pool_norms(pool_ref, norm_ref, bounds):
    step_slots = 4
    rows = step_slots * PBLK
    lane = lax.broadcasted_iota(jnp.int32, (rows, LANES), 1)

    def lane_sum(part):
        return jnp.sum(part, axis=1, keepdims=True)

    def step(i):
        here = slice(i * step_slots, (i + 1) * step_slots)
        wide = pool_ref[here].reshape(rows, pool_ref.shape[2]).astype(F32)
        square = wide * wide
        result, before, inside = None, None, None
        for level, (low, high) in enumerate(bounds):
            if high < LANES:
                total = lane_sum(jnp.where(lane < high, square[:, :LANES], 0.0))
            else:
                start = low // LANES * LANES
                parts = [square[:, j : j + LANES] for j in range(start, high, LANES)]
                while len(parts) > 1:
                    parts = [x + y for x, y in zip(parts[::2], parts[1::2])]
                total = lane_sum(parts[0])
                if start:
                    total = total + before
            before = total
            result = jnp.broadcast_to(total, (rows, LANES)) if result is None else jnp.where(lane == level, total, result)
        norm_ref[here] = result.reshape(step_slots, PBLK, LANES)

    for i in range(pool_ref.shape[0] // step_slots):
        step(i)


def norm_rows(norm_ref, slot_ref, block, count):
    table = jnp.concatenate([norm_ref[slot_ref[block * count + n]] for n in range(count)], axis=0)
    return table.T[:8, :]


def pack_kernel(
    first_ref, lists_hbm, block_hbm, out_hbm, lists_ref, block_ref, row_ref, wanted_ref, lists_sem, in_sem, row_sem, out_sem
):
    load = pltpu.make_async_copy(block_hbm, block_ref, in_sem)
    lists = pltpu.make_async_copy(lists_hbm, lists_ref, lists_sem)
    lists.start()
    load.start()
    lists.wait()
    local = lists_ref[...] - first_ref[0]
    local = jnp.where((local >= 0) & (local < block_ref.shape[0]), local, 0).astype(F32)
    row = jnp.broadcast_to(jnp.max(local, axis=0, keepdims=True), row_ref.shape)
    size = row.shape[1]
    step = 1
    while step < size // out_hbm.shape[0]:
        row = jnp.maximum(row, pltpu.roll(row, size - step, 1))
        step *= 2
    row_ref[...] = row.astype(jnp.int32)
    save = pltpu.make_async_copy(row_ref, wanted_ref, row_sem)
    save.start()
    save.wait()
    load.wait()
    share = size // out_hbm.shape[0]

    def one(d, carry):
        pltpu.make_async_copy(block_ref.at[wanted_ref[0, d * share]], out_hbm.at[d], out_sem).start()
        return carry

    for d in range(out_hbm.shape[0]):
        one(d, 0)
    pltpu.make_async_copy(out_hbm, out_hbm, out_sem).wait()


def prep_kernel(split, rows, query_ref, full_ref, mask_ref):
    lane = lax.broadcasted_iota(jnp.int32, (rows, LANES), 1)

    def step(block, carry):
        here = pl.ds(block * rows, rows)
        full_ref[block] = to_row(square_sums(query_ref[here, :]))
        first = query_ref[here, :LANES].astype(F32)
        mask_ref[0, here, :] = jnp.where(lane < split, first, 0.0).astype(BF16)
        mask_ref[1, here, :] = jnp.where(lane < split, 0.0, first).astype(BF16)
        return carry

    lax.fori_loop(0, full_ref.shape[0], step, 0)


def dots_kernel(
    bounds, shards, per_shard, rows, shifts, slot_ref, shard_ref, query_ref, pool_ref, full_ref, pp_ref, *refs
):
    outs, (norm_ref, cand_ref) = refs[:-2], refs[-2:]
    pool_norms(pool_ref, norm_ref, bounds)
    count, _, width = cand_ref.shape
    shard = shard_ref[0]
    base = per_shard * rows
    last = len(bounds) - 1
    for shift, out_ref in zip(shifts, outs):
        target = lax.rem(shard + shift, shards)
        for k in range(per_shard):
            block = target * per_shard + k
            take_blocks(pool_ref, slot_ref, block, count, cand_ref)
            query = query_ref[pl.ds(block * rows, rows), :]
            cand = cand_ref[...].reshape(count * PBLK, width)
            out_ref[k * rows : (k + 1) * rows, :] = contract(query, cand, 1, 1)
            pp = norm_rows(norm_ref, slot_ref, block, count)
            pp_ref[block] = pp
            out_ref[base + k : base + k + 1, :] = pp[last : last + 1, :]
            out_ref[base + per_shard : base + per_shard + 1, k * rows : (k + 1) * rows] = full_ref[block]


def prefix_dots(bounds, rows, block, query_ref, cand_ref):
    here = pl.ds(block * rows, rows)
    cands = cand_ref.shape[0] * PBLK
    lane = lax.broadcasted_iota(jnp.int32, (rows, LANES), 1)
    first = query_ref[here, :LANES]
    short = jnp.where(lane < bounds[0][1], first.astype(F32), 0.0).astype(BF16)
    both = contract(
        jnp.concatenate([short, first], axis=0), cand_ref[:, :, :LANES].reshape(cands, LANES), 1, 1
    )
    yield both[:rows]
    dots = both[rows:]
    yield dots
    for low, high in bounds[2:]:
        dots = dots + contract(query_ref[here, low:high], cand_ref[:, :, low:high].reshape(cands, high - low), 1, 1)
        yield dots


def low_kernel(
    bounds, rows, slot_ref, shard_ref, query_ref, pool_ref, pp_ref, ids_ref, pos_ref,
    coef_hbm, row_hbm, col_hbm, loss_ref, cand_ref, term_ref, coef_ref, row_ref, col_ref, sem, row_sem, col_sem,
):
    count = cand_ref.shape[1]
    levels, _, cands = coef_ref.shape
    blocks = loss_ref.shape[0]

    @pl.when(shard_ref[0] == 0)
    def _():
        row_ref[...] = jnp.zeros_like(row_ref)
        col_ref[...] = jnp.zeros_like(col_ref)

        def one(block, cand_ref, term_ref):
            here = pl.ds(block * rows, rows)
            take_blocks(pool_ref, slot_ref, block, count, cand_ref)
            pp = pp_ref[block]
            ids = ids_ref[pl.ds(block, 1), :]
            live = ids >= 0.0
            labels = jnp.where(ids == to_col(pos_ref[pl.ds(block, 1), :]), 1.0, 0.0)
            qq = jnp.zeros((rows, 1), F32)
            entropy = jnp.zeros((rows, 1), F32)
            logit_sum = jnp.zeros((rows, cands), F32)
            row_terms, col_terms = [], []
            sums = prefix_dots(bounds, rows, block, query_ref, cand_ref)
            for level, ((low, high), dots) in enumerate(zip(bounds, sums)):
                qq = qq + square_sums(query_ref[here, low:high])
                coef, row, col, part, logits = terms(
                    dots, lax.rsqrt(qq + EPS), pp[level : level + 1, :], live, labels, float(high // MINP)
                )
                term_ref[level] = coef
                row_terms.append(row)
                col_terms.append(col)
                entropy = entropy + part
                logit_sum = logit_sum + logits
            loss = entropy - jnp.sum(labels * logit_sum, axis=1, keepdims=True)
            coef = jnp.zeros((rows, cands), F32)
            row = jnp.zeros((rows, 1), F32)
            col = jnp.zeros((1, cands), F32)
            for level in reversed(range(levels)):
                coef = coef + term_ref[level]
                row = row + row_terms[level]
                col = col + col_terms[level]
                coef_ref[level, here, :] = coef
                row_ref[block, level : level + 1, :] = to_row(row)
                col_ref[block, level : level + 1, :] = col
            loss_ref[pl.ds(block, 1), :] = to_row(loss)

        def step(pair, carry):
            for j in range(2):
                one(pair * 2 + j, cand_ref.at[j], term_ref.at[j])
            here = pl.ds(pair * 2 * rows, 2 * rows)
            pltpu.make_async_copy(coef_ref.at[:, here], coef_hbm.at[:, here], sem).start()
            return carry

        lax.fori_loop(0, blocks // 2, step, 0)
        copies = [
            pltpu.make_async_copy(row_ref, row_hbm, row_sem),
            pltpu.make_async_copy(col_ref, col_hbm, col_sem),
        ]
        for copy in copies:
            copy.start()
        for copy in copies:
            copy.wait()
        pltpu.make_async_copy(coef_ref, coef_hbm, sem).wait()

    @pl.when(shard_ref[0] != 0)
    def _():
        loss_ref[...] = jnp.zeros_like(loss_ref)


def high_kernel(shards, per_shard, rows, weights, shard_ref, ids_ref, pos_ref, after_ref, *refs):
    del after_ref
    ins, outs, loss_ref = refs[:shards], refs[shards:-1], refs[-1]
    shard = shard_ref[0]
    base = per_shard * rows
    width = ids_ref.shape[1]
    in_half = [
        jnp.where(lax.rem(shard - shift + shards, shards) < shards // 2, 1.0, 0.0)
        for shift in range(shards)
    ]

    def total(span, keep):
        pieces = [ref[span, :] * scale if keep else ref[span, :] for ref, scale in zip(ins, in_half)]
        return (pieces[0] + pieces[1]) + (pieces[2] + pieces[3])

    below = slice(base, base + AUX)
    half_rows, half_cols, full_rows, full_cols, losses, coefs = [], [], [], [], [], []
    aux_half, aux_full = total(below, True), total(below, False)
    for k in range(per_shard):
        block = shard * per_shard + k
        ids = ids_ref[pl.ds(block, 1), :]
        live = ids >= 0.0
        labels = jnp.where(ids == to_col(pos_ref[pl.ds(block, 1), :]), 1.0, 0.0)
        span = slice(k * rows, (k + 1) * rows)
        results = []
        for keep, aux, weight in ((True, aux_half, weights[0]), (False, aux_full, weights[1])):
            scale = to_col(lax.rsqrt(aux[per_shard : per_shard + 1, span] + EPS))
            results.append(terms(total(span, keep), scale, aux[k : k + 1, :], live, labels, weight))
        (coef_h, row_h, col_h, part_h, logit_h), (coef_f, row_f, col_f, part_f, logit_f) = results
        loss = part_h + part_f - jnp.sum(labels * (logit_h + logit_f), axis=1, keepdims=True)
        coefs.append(((coef_h + coef_f).astype(BF16), coef_f.astype(BF16)))
        half_rows.append(to_row(row_h + row_f))
        full_rows.append(to_row(row_f))
        half_cols.append(col_h + col_f)
        full_cols.append(col_f)
        losses.append(to_row(loss))
    loss_ref[...] = jnp.concatenate(losses, axis=1)

    def aux_rows(rows_list, cols_list):
        line = jnp.concatenate(rows_list + [jnp.zeros((1, width - base), F32)], axis=1)
        table = jnp.concatenate(cols_list + [line], axis=0)
        table = jnp.concatenate([table, jnp.zeros((AUX - table.shape[0], width), F32)], axis=0)
        first = table.astype(BF16).astype(F32)
        second = (table - first).astype(BF16).astype(F32)
        third = table - first - second
        return jnp.concatenate([first, second, third, jnp.zeros_like(table)], axis=0).astype(BF16)

    aux = (aux_rows(half_rows, half_cols), aux_rows(full_rows, full_cols))
    for shift in range(shards):
        out_ref = outs[shift]
        high_target = lax.rem(shard + shift, shards) >= shards // 2
        for which, chosen in ((1, high_target), (0, jnp.logical_not(high_target))):

            @pl.when(chosen)
            def _():
                for k in range(per_shard):
                    out_ref[k * rows : (k + 1) * rows, :] = coefs[k][which]
                out_ref[base : base + COEF_AUX, :] = aux[which]


def unpack_aux(ref, base):
    packed = ref[base : base + COEF_AUX, :].astype(F32)
    return packed[:AUX] + packed[AUX : 2 * AUX] + packed[2 * AUX : 3 * AUX]


def stage_kernel(shard_ref, row_hbm, col_hbm, coef_hbm, after_ref, row_ref, col_ref, coef_ref, sem):
    del after_ref

    @pl.when(shard_ref[0] == 0)
    def _():
        copies = [
            pltpu.make_async_copy(source, target, sem.at[i])
            for i, (source, target) in enumerate(((row_hbm, row_ref), (col_hbm, col_ref), (coef_hbm, coef_ref)))
        ]
        for copy in copies:
            copy.start()
        for copy in copies:
            copy.wait()


def passage_kernel(
    bounds, shards, per_shard, rows, slot_ref, shard_ref, query_ref, pool_ref, mask_ref, low_row_ref, low_col_ref,
    low_coef_ref, *refs
):
    ins = refs[:shards]
    out_hbm, half_hbm, row_hbm, coef_ref, row_ref, col_ref, spread_ref, sum_ref, scale_ref, out_ref, half_ref = refs[shards:-3]
    out_sem, half_sem, row_sem = refs[-3:]
    shard = shard_ref[0]
    base = per_shard * rows
    blocks = shards * per_shard
    slots, _, width = pool_ref.shape
    cands = coef_ref.shape[1]
    count = cands // PBLK

    row_copy = pltpu.make_async_copy(row_ref, row_hbm, row_sem)

    @pl.when(shard == 0)
    def _():
        sum_ref[...] = jnp.zeros_like(sum_ref)

    scale_ref[...] = jnp.zeros_like(scale_ref)
    for shift in range(shards):
        source = lax.rem(shard - shift + shards, shards)
        coef_ref[pl.ds(source * base, base), :] = ins[shift][:base, :]
        aux = unpack_aux(ins[shift], base)
        for k in range(per_shard):
            col_ref[source * per_shard + k] = aux[k : k + 1, :]
            line = aux[per_shard : per_shard + 1, k * rows : (k + 1) * rows]
            row_ref[source * per_shard + k] = jnp.broadcast_to(line, (8, rows))

    def add_scales(block, low):
        cols = jnp.broadcast_to(col_ref[block], (8, cands))
        if low:
            cols = cols + low_col_ref[block]
        col_cols = columns(cols)
        for n in range(count):
            slot = slot_ref[block * count + n]
            scale_ref[slot] = scale_ref[slot] + col_cols[n * PBLK : (n + 1) * PBLK, :]

    def send(start, end):
        done = pl.ds(start, end - start)
        pltpu.make_async_copy(out_ref.at[:, :, done], out_hbm.at[:, :, done], out_sem).start()

    @pl.when(shard == 0)
    def _():
        levels = len(bounds)
        row_ref[...] = row_ref[...] + low_row_ref[...]
        row_copy.start()

        level_of = lax.broadcasted_iota(jnp.int32, (LANES, width), 0)
        column = lax.broadcasted_iota(jnp.int32, (LANES, width), 1)
        member = jnp.zeros((LANES, width), F32)
        for level, (lo, hi) in enumerate(bounds):
            member = jnp.where((level_of == level) & (column >= lo) & (column < hi), 1.0, member)
        member = member.astype(BF16)
        for block in range(blocks):
            add_scales(block, True)
        step_slots = slots // CHUNKS
        for group in (range(levels - 1, levels), range(levels - 1)):
            left, right = bounds[group[0]][0], bounds[group[-1]][1]
            for block in range(blocks):
                here = pl.ds(block * rows, rows)
                base_coef = coef_ref[here, :].astype(F32)
                coefs = {level: (base_coef + low_coef_ref[level, here, :]).astype(BF16) for level in group}
                for level in group:
                    half_ref[level, here, :] = coefs[level]
                grads = []
                if left == 0:
                    first = contract(coefs[0], mask_ref[0, here, :], 0, 0) + contract(coefs[1], mask_ref[1, here, :], 0, 0)
                    grads.append((0, first))
                for level in group:
                    if level >= 2:
                        lo, hi = bounds[level]
                        grads.append((lo, contract(coefs[level], query_ref[here, lo:hi], 0, 0)))
                for n in range(count):
                    slot = slot_ref[block * count + n]
                    for start, grad in grads:
                        lanes = slice(start, start + grad.shape[1])
                        sum_ref[slot, :, lanes] = sum_ref[slot, :, lanes] + grad[n * PBLK : (n + 1) * PBLK, :]
            done = pl.ds(group[0], len(group))
            pltpu.make_async_copy(half_ref.at[done], half_hbm.at[done], half_sem).start()
            for chunk in range(CHUNKS):
                part = slice(chunk * step_slots, (chunk + 1) * step_slots)
                scale = scale_ref[part].reshape(step_slots * PBLK, LANES)
                high = scale.astype(BF16)
                rest = scale - high.astype(F32)
                middle = rest.astype(BF16)
                low = (rest - middle.astype(F32)).astype(BF16)
                side = member[:, left:right]
                wide = contract(high, side, 1, 0) + contract(middle, side, 1, 0) + contract(low, side, 1, 0)
                pool = pool_ref[part, :, left:right].reshape(step_slots * PBLK, right - left).astype(F32)
                total = sum_ref[part, :, left:right].reshape(step_slots * PBLK, right - left)
                out_ref[part, :, left:right] = (total - wide * pool).astype(BF16).reshape(step_slots, PBLK, right - left)
                lanes = pl.ds(left, right - left)
                pltpu.make_async_copy(out_ref.at[part, :, lanes], out_hbm.at[part, :, lanes], out_sem).start()
        pltpu.make_async_copy(half_ref, half_hbm, half_sem).wait()
        row_copy.wait()
        pltpu.make_async_copy(out_ref, out_hbm, out_sem).wait()

    @pl.when(shard != 0)
    def _():
        row_copy.start()
        copy = pltpu.make_async_copy(coef_ref, half_hbm.at[0], half_sem)
        copy.start()
        spread_ref[...] = jnp.zeros_like(spread_ref)
        for block in range(blocks):
            add_scales(block, False)
            turned = coef_ref[pl.ds(block * rows, rows), :].astype(F32).T.astype(BF16)
            for n in range(count):
                spread_ref[slot_ref[block * count + n], :, block * rows : (block + 1) * rows] = turned[
                    n * PBLK : (n + 1) * PBLK, :
                ]
        spread = spread_ref[0:slots].reshape(slots * PBLK, blocks * rows)
        scale = scale_ref[0:slots].reshape(slots * PBLK, LANES)[:, 0:1]
        for start in range(0, width, PIECE):
            end = start + PIECE
            grad = contract(spread, query_ref[:, start:end], 1, 0)
            pool = pool_ref[:, :, start:end].reshape(slots * PBLK, end - start).astype(F32)
            out_ref[:, :, start:end] = (grad - scale * pool).astype(BF16).reshape(slots, PBLK, end - start)
            send(start, end)
        copy.wait()
        row_copy.wait()
        pltpu.make_async_copy(out_ref, out_hbm, out_sem).wait()


def query_kernel(
    bounds, rows, loss_scale, slot_ref, shard_ref, query_ref, pool_ref, row_ref, low_loss_ref, high_loss_ref, half_hbm,
    query_grad_ref, loss_ref, cand_ref, half_ref, sem,
):
    shard = shard_ref[0]
    blocks, cands = low_loss_ref.shape[0], half_ref.shape[2]
    count = cand_ref.shape[0]
    width = query_ref.shape[1]
    per_line = LANES // rows
    first = pltpu.make_async_copy(half_hbm.at[0], half_ref.at[0], sem.at[0])
    rest = pl.ds(1, half_ref.shape[0] - 1)
    others = pltpu.make_async_copy(half_hbm.at[rest], half_ref.at[rest], sem.at[1])
    first.start()

    @pl.when(shard == 0)
    def _():
        others.start()

    for block in range(blocks):
        j = block % per_line
        loss_ref[block // per_line : block // per_line + 1, j * rows : (j + 1) * rows] = low_loss_ref[block : block + 1, :]
    loss_ref[pl.ds(shard, 1), :] = loss_ref[pl.ds(shard, 1), :] + high_loss_ref[...]
    loss_ref[...] = loss_ref[...] * loss_scale

    def run(spans):
        def step(block, carry):
            take_blocks(pool_ref, slot_ref, block, count, cand_ref)
            row_cols = columns(row_ref[block])
            here = pl.ds(block * rows, rows)
            for level, (lo, hi) in enumerate(spans):
                query = query_ref[here, lo:hi].astype(F32)
                cand = cand_ref[:, :, lo:hi].reshape(cands, hi - lo)
                grad = contract(half_ref[level, here, :], cand, 1, 0) - row_cols[:rows, level : level + 1] * query
                query_grad_ref[here, lo:hi] = grad.astype(BF16)
            return carry

        lax.fori_loop(0, blocks, step, 0)

    first.wait()

    @pl.when(shard == 0)
    def _():
        others.wait()
        run(bounds)

    @pl.when(shard != 0)
    def _():
        run([(0, width)])


def collect_kernel(target_ref, back_hbm, out_ref, back_ref, sem):
    rows = out_ref.shape[0]
    size = back_ref.shape[0] // CHUNKS
    copies = []
    for half in range(CHUNKS):
        part = pl.ds(half * size, size)
        copies.append(pltpu.make_async_copy(back_hbm.at[part], back_ref.at[part], sem.at[half]))
        copies[-1].start()
    here = lax.broadcasted_iota(jnp.int32, (rows, size), 0)
    total = None
    for half in range(CHUNKS):
        part = slice(half * size, (half + 1) * size)
        choose = jnp.where(here == target_ref[:, part], 1.0, 0.0).astype(BF16)
        copies[half].wait()
        grad = contract(choose, back_ref[part, :], 1, 0)
        total = grad if total is None else total + grad
    out_ref[...] = total.astype(BF16)


def per_device(queries, passages, neg_lists, positives):
    peers = lax.axis_size("dp")
    shards = lax.axis_size("tensor")
    total_rows, width = queries.shape
    blocks = neg_lists.shape[0] // peers
    count = neg_lists.shape[1]
    rows = total_rows // blocks
    local_blocks = passages.shape[0] // PBLK
    cands = count * PBLK
    per_shard = blocks // shards
    base = per_shard * rows
    slots = peers
    my_index = lax.axis_index("dp")
    shard = lax.axis_index("tensor")
    sizes = [MINP * 2**level for level in range(NPRE)]
    low_sizes = [size for size in sizes if size <= width]
    high_sizes = [size for size in sizes if size > width]
    assert high_sizes == [width * shards // 2, width * shards] and low_sizes[-1] == width
    assert shards == 4 and base == LANES
    bounds = list(zip([0] + low_sizes[:-1], low_sizes))
    levels = len(bounds)
    weight_total = sum(size / MINP for size in sizes)

    flat = neg_lists.reshape(peers, blocks * count)
    mine = (flat >= 0) & (flat // local_blocks == my_index)
    wanted = jnp.max(jnp.where(mine, flat % local_blocks, -1), axis=1)
    own = lax.dynamic_slice_in_dim(neg_lists, my_index * blocks, blocks, 0)
    valid = own >= 0
    slot = jnp.where(valid, own // local_blocks, 0).reshape(blocks * count)
    spare_slot = jnp.where(valid, own // local_blocks, slots).reshape(blocks * count)
    within = jnp.arange(PBLK, dtype=jnp.int32)
    ids = jnp.where(valid[:, :, None], own[:, :, None] * PBLK + within[None, None, :], -1)
    ids = ids.reshape(blocks, cands).astype(F32)
    target = jnp.where(wanted[:, None] >= 0, wanted[:, None] * PBLK + within[None, :], -1).reshape(1, slots * PBLK)
    pos = positives.reshape(blocks, rows).astype(F32)
    shard_arr = shard.reshape(1).astype(jnp.int32)
    pool_shape = (slots, PBLK, width)

    pinned = partial(pltpu.with_memory_space_constraint, memory_space=pltpu.HBM)
    panels = pl.pallas_call(
        pack_kernel,
        out_shape=pltpu.HBM(pool_shape, BF16),
        in_specs=[smem(), hbm(), hbm()],
        out_specs=hbm(),
        scratch_shapes=[
            pltpu.VMEM((count, neg_lists.shape[0]), jnp.int32),
            pltpu.VMEM((local_blocks, PBLK, width), BF16),
            pltpu.VMEM((8, neg_lists.shape[0]), jnp.int32),
            pltpu.SMEM((8, neg_lists.shape[0]), jnp.int32),
            pltpu.SemaphoreType.DMA(()),
            pltpu.SemaphoreType.DMA(()),
            pltpu.SemaphoreType.DMA(()),
            pltpu.SemaphoreType.DMA(()),
        ],
        compiler_params=params(),
        name="pack",
    )(
        (my_index * local_blocks).reshape(1).astype(jnp.int32), pinned(neg_lists.T),
        pinned(passages.reshape(local_blocks, PBLK, width)),
    )
    pool = lax.all_to_all(panels, "dp", split_axis=0, concat_axis=0, tiled=True)
    full_norms, masked = pl.pallas_call(
        partial(prep_kernel, bounds[0][1], rows),
        out_shape=[
            jax.ShapeDtypeStruct((blocks, 1, rows), F32),
            jax.ShapeDtypeStruct((2, total_rows, LANES), BF16),
        ],
        in_specs=[vmem()],
        out_specs=[vmem()] * 2,
        compiler_params=params(),
        name="prep",
    )(queries)

    def shift_by(part, s):
        return lax.ppermute(part, "tensor", [(i, (i + s) % shards) for i in range(shards)])

    cand_scratch = pltpu.VMEM((count, PBLK, width), BF16)
    message = jax.ShapeDtypeStruct((base + AUX, cands), F32)
    norm_rows_of, far, right, left, here = pl.pallas_call(
        partial(dots_kernel, bounds, shards, per_shard, rows, (2, 1, 3, 0)),
        out_shape=[jax.ShapeDtypeStruct((blocks, 8, cands), F32)] + [message] * shards,
        in_specs=[smem(), smem(), vmem(), vmem(), vmem()],
        out_specs=[vmem()] * (shards + 1),
        scratch_shapes=[pltpu.VMEM((slots, PBLK, LANES), F32), cand_scratch],
        compiler_params=params(),
        name="dots",
    )(slot, shard_arr, queries, pool, full_norms)
    arrived = [here, shift_by(right, 1), shift_by(far, 2), shift_by(left, 3)]

    low_coef, low_row, low_col, low_loss = pl.pallas_call(
        partial(low_kernel, bounds, rows),
        out_shape=[
            pltpu.HBM((levels, total_rows, cands), F32),
            pltpu.HBM((blocks, 8, rows), F32),
            pltpu.HBM((blocks, 8, cands), F32),
            jax.ShapeDtypeStruct((blocks, rows), F32),
        ],
        in_specs=[smem(), smem()] + [vmem()] * 5,
        out_specs=[hbm()] * 3 + [vmem()],
        scratch_shapes=[
            pltpu.VMEM((2, count, PBLK, width), BF16),
            pltpu.VMEM((2, levels, rows, cands), F32),
            pltpu.VMEM((levels, total_rows, cands), F32),
            pltpu.VMEM((blocks, 8, rows), F32),
            pltpu.VMEM((blocks, 8, cands), F32),
            pltpu.SemaphoreType.DMA(()),
            pltpu.SemaphoreType.DMA(()),
            pltpu.SemaphoreType.DMA(()),
        ],
        compiler_params=params(),
        name="low",
    )(slot, shard_arr, queries, pool, norm_rows_of, ids, pos)
    *coefs, high_loss = pl.pallas_call(
        partial(high_kernel, shards, per_shard, rows, [size / MINP for size in high_sizes]),
        out_shape=[jax.ShapeDtypeStruct((base + COEF_AUX, cands), BF16)] * shards
        + [jax.ShapeDtypeStruct((1, base), F32)],
        in_specs=[smem()] + [vmem()] * 2 + [hbm()] + [vmem()] * shards,
        out_specs=[vmem()] * (shards + 1),
        compiler_params=params(),
        name="high",
    )(shard_arr, ids, pos, pinned(low_row), *arrived)
    staged_row, staged_col, staged_coef = pl.pallas_call(
        stage_kernel,
        out_shape=[
            jax.ShapeDtypeStruct((blocks, 8, rows), F32),
            jax.ShapeDtypeStruct((blocks, 8, cands), F32),
            jax.ShapeDtypeStruct((levels, total_rows, cands), F32),
        ],
        in_specs=[smem()] + [hbm()] * 3 + [pl.BlockSpec(memory_space=pl.ANY)],
        out_specs=[vmem()] * 3,
        scratch_shapes=[pltpu.SemaphoreType.DMA((3,))],
        compiler_params=params(),
        name="stage",
    )(shard_arr, pinned(low_row), pinned(low_col), pinned(low_coef), high_loss)
    coefs = [coefs[0]] + [shift_by(coefs[s], s) for s in range(1, shards)]

    half_shape = (levels, total_rows, cands)
    slot_grad, half, row_table = pl.pallas_call(
        partial(passage_kernel, bounds, shards, per_shard, rows),
        out_shape=[pltpu.HBM(pool_shape, BF16), pltpu.HBM(half_shape, BF16), pltpu.HBM((blocks, 8, rows), F32)],
        in_specs=[smem(), smem()] + [vmem()] * (6 + shards),
        out_specs=[hbm()] * 3,
        scratch_shapes=[
            pltpu.VMEM((total_rows, cands), BF16),
            pltpu.VMEM((blocks, 8, rows), F32),
            pltpu.VMEM((blocks, 1, cands), F32),
            pltpu.VMEM((slots + 1, PBLK, total_rows), BF16),
            pltpu.VMEM((slots + 1, PBLK, width), F32),
            pltpu.VMEM((slots + 1, PBLK, LANES), F32),
            pltpu.VMEM(pool_shape, BF16),
            pltpu.VMEM(half_shape, BF16),
            pltpu.SemaphoreType.DMA(()),
            pltpu.SemaphoreType.DMA(()),
            pltpu.SemaphoreType.DMA(()),
        ],
        compiler_params=params(),
        name="passage",
    )(
        spare_slot, shard_arr, queries, pool, masked,
        staged_row, staged_col, staged_coef, *coefs,
    )
    back = lax.all_to_all(slot_grad, "dp", split_axis=0, concat_axis=0, tiled=True)

    query_grad, loss = pl.pallas_call(
        partial(query_kernel, bounds, rows, 1.0 / weight_total),
        out_shape=[
            jax.ShapeDtypeStruct((total_rows, width), BF16),
            jax.ShapeDtypeStruct((shards, base), F32),
        ],
        in_specs=[smem(), smem()] + [vmem()] * 5 + [hbm()],
        out_specs=[vmem()] * 2,
        scratch_shapes=[cand_scratch, pltpu.VMEM(half_shape, BF16), pltpu.SemaphoreType.DMA((2,))],
        compiler_params=params(),
        name="query",
    )(slot, shard_arr, queries, pool, row_table, low_loss, high_loss, pinned(half))
    loss = lax.psum(loss, "tensor")

    passage_grad = pl.pallas_call(
        collect_kernel,
        out_shape=jax.ShapeDtypeStruct((local_blocks * PBLK, width), BF16),
        in_specs=[vmem(), hbm()],
        out_specs=vmem(),
        scratch_shapes=[pltpu.VMEM((slots * PBLK, width), BF16), pltpu.SemaphoreType.DMA((CHUNKS,))],
        compiler_params=params(),
        name="collect",
    )(target, pinned(back.reshape(slots * PBLK, width)))
    return (
        query_grad,
        passage_grad,
        loss.reshape(total_rows),
    )


def solution(mesh):
    return jax.shard_map(
        per_device,
        mesh=mesh,
        in_specs=(P("dp", "tensor"), P("dp", "tensor"), P(), P("dp")),
        out_specs=(P("dp", "tensor"), P("dp", "tensor"), P("dp")),
        check_vma=False,
    )
```
